32 devices in a mesh: groups: 2 (over y), seq: 4 (over z), head: 4 (over x, core).
Axes of the slice: x: 2, y: 2, z: 4, core: 2. Of those that a mesh axis runs over, the one named last changes fastest.
Arguments:
- hit_features: bfloat16 [256, 12288], P('head', ('groups', 'seq')), parts along dimension 1, may hold values from -6 to 6
- depth_kernel: bfloat16 [7, 256], P(None, 'head'), may hold values from -2 to 2
- point_weight: bfloat16 [800, 256], P('head'), may hold values from -0.375 to 0.375
- pair_weight: float32 [8, 3], P('head'), may hold values from -45 to 45
- hit_order: int32 [12288], P(('groups', 'seq')), parts along dimension 0, may hold values from 0 to 1535, as said below
- valid_counts: int32 [8], P(('groups', 'seq')), parts along dimension 0, may hold values from 768 to 1536, as said below
Outputs:
- attended: bfloat16 [256, 12288], P('head', ('groups', 'seq')), parts along dimension 1
The draws below stay inside these ranges and needn't reach their ends.
There are 2 independent parts, one for each index of `groups`. The reference program is written for one: setup_inputs(seed, part) draws one part's arguments, and reference() takes and returns one part's arrays. A program takes and returns all parts, laid end to end along the dimension named above; an argument that names none is the same for every part. Nothing has to cross between parts.
Inputs may be any that keep to these rules, and one draw needn't show every extreme that they name: `hit_order`: each aligned block of 1536 entries is a permutation of 0 .. 1535. `valid_counts`: in every draw one block is full and one holds exactly 768 real hits.
All inputs are finite; a program needn't handle non-finite values.
Results may differ from the reference program's by a relative error of at most 0.0045.
The reference program's roundings to bfloat16 on the way count: a program that leaves them out, or rounds other values in their place, can miss the bound.
Values may be sent and summed in bfloat16 or wider, within the bound.
A program may use at most 64 MiB of HBM per device.

```python
import jax
import jax.numpy as jnp
from jax import lax

C = 256
HEADS = 8
HD = 32
KSIZE = 7
PROJ = 100
HIT_DEV = 1536
HITS = 6144
NBLOCKS = 4


def draw_pair_weight(key, part):
    base_draw = jax.random.uniform(jax.random.fold_in(key, 11), (HEADS, 3), jnp.float32, -1.5, 1.5)
    return base_draw


def draw_hit_order(key, part):
    block_keys = jax.random.split(jax.random.fold_in(key, 21), NBLOCKS)
    orders = jax.vmap(lambda single: jax.random.permutation(single, HIT_DEV))(block_keys)
    return orders.reshape(-1).astype(jnp.int32)


def draw_valid_counts(key, part):
    counts_drawn = jax.random.randint(jax.random.fold_in(key, 31), (NBLOCKS,), HIT_DEV // 2, HIT_DEV + 1)
    shuffled = jax.random.permutation(jax.random.fold_in(key, 32), NBLOCKS)
    counts_drawn = counts_drawn.at[shuffled[0]].set(HIT_DEV).at[shuffled[1]].set(HIT_DEV // 2)
    return counts_drawn.astype(jnp.int32)


def shard_levels(own_key, dims, cuts, low, largest):
    factor_of, own = 1.0, jax.random.fold_in(own_key, 6)
    for dim, shards_of in cuts:
        draws = jnp.exp(jax.random.uniform(jax.random.fold_in(own, dim), (shards_of,), jnp.float32, low / len(cuts), largest / len(cuts)))
        factor_of = factor_of * jnp.repeat(draws, dims[dim] // shards_of).reshape([-1 if axis == dim else 1 for axis in range(len(dims))])
    return factor_of


def centred(key, dims, width, reach, cuts=(), held_as=jnp.bfloat16):
    gain = shard_levels(key, dims, cuts, -0.22, 0.18) if cuts else 1.0
    entries = jax.random.normal(key, dims, jnp.float32) * width * gain
    return jnp.minimum(jnp.maximum(entries, -reach), reach).astype(held_as)


def setup_inputs(seed: int = 0, part: int = 0) -> dict:
    streams_of = jax.random.split(jax.random.key(seed), 7)
    own_keys = jax.random.split(jax.random.fold_in(streams_of[6], part), 7)
    return {
        "hit_features": centred(own_keys[0], (C, HITS), 1.0, 6.0, ((0, 4), (1, 4))),
        "depth_kernel": centred(streams_of[1], (KSIZE, C), KSIZE ** -0.5, 2.0, ((1, 4),)),
        "point_weight": centred(streams_of[2], (HEADS * PROJ, C), C ** -0.5, 0.375, ((0, 4),)),
        "pair_weight": draw_pair_weight(jax.random.fold_in(streams_of[6], 71), part),
        "hit_order": draw_hit_order(jax.random.fold_in(jax.random.fold_in(streams_of[6], part), 71), part),
        "valid_counts": draw_valid_counts(jax.random.fold_in(jax.random.fold_in(streams_of[6], part), 71), part),
    }


floor_pt = 0.1
mass_offset = 0.1
masked_score = -1e+30

def kinematics(raw_vector):
    hit_mass = mass_offset + jax.nn.softplus(raw_vector[0])
    along_x = raw_vector[1]
    along_y = raw_vector[2]
    along_z = raw_vector[3]
    mass_sq = hit_mass * hit_mass
    trans_sq = along_x * along_x + along_y * along_y
    energy = jnp.sqrt(mass_sq + trans_sq + along_z * along_z)
    trans_mass = jnp.sqrt(mass_sq + trans_sq)
    magnitude = jnp.log((jnp.abs(along_z) + energy) / trans_mass)
    rapidity = jnp.where(along_z < 0.0, -magnitude, magnitude)
    inverse_pt = 1.0 / jnp.maximum(jnp.sqrt(trans_sq), floor_pt)
    return jnp.stack([energy, along_x, along_y, along_z, mass_sq, rapidity, along_x * inverse_pt, along_y * inverse_pt, trans_sq])

def pair_bias(query_side, key_side, weights_row):
    left = query_side[:, :, None]
    right = key_side[:, None, :]
    minkowski = left[0] * right[0] - left[1] * right[1] - left[2] * right[2] - left[3] * right[3]
    invariant = left[4] + right[4] + 2.0 * minkowski
    separation = (left[5] - right[5]) ** 2 + 2.0 * (1.0 - left[6] * right[6] - left[7] * right[7])
    kt_sq = jnp.minimum(left[8], right[8]) * separation
    return weights_row[0] * jnp.log(invariant) + weights_row[1] * jnp.log1p(kt_sq) + weights_row[2] * jnp.log1p(separation)

def one_head(args):
    queries, query_kin, keys, values, key_kin, weights_row, key_valid = args
    scores = jnp.dot(queries.T, keys, preferred_element_type=jnp.float32) * HD ** (-0.5)
    scores = scores + pair_bias(query_kin, key_kin, weights_row)
    scores = jnp.where(key_valid[None, :], scores, masked_score)
    row_max = lax.optimization_barrier(jnp.max(scores, axis=1, keepdims=True))
    weights_full = jnp.exp(scores - row_max)
    total = lax.optimization_barrier(jnp.sum(weights_full, axis=1))
    weights_low = weights_full.astype(jnp.bfloat16)
    summed = jnp.dot(values, weights_low.T, preferred_element_type=jnp.float32)
    return (summed / total[None, :]).astype(jnp.bfloat16)

def wrap_ends(array):
    return jnp.concatenate([array[..., -HIT_DEV:], array, array[..., :2 * HIT_DEV]], axis=-1)

def reference(hit_features, depth_kernel, point_weight, pair_weight, hit_order, valid_counts):
    hits = hit_features.shape[1]
    blocks = hits // HIT_DEV
    position = jnp.arange(hits, dtype=jnp.int32)
    block_of = position // HIT_DEV
    ordered = jnp.take(hit_features, (block_of * HIT_DEV + hit_order).astype(jnp.int32), axis=1)
    half = KSIZE // 2
    padded = jnp.pad(ordered, ((0, 0), (half, half))).astype(jnp.float32)
    taps = depth_kernel.astype(jnp.float32)
    summed = jnp.zeros((ordered.shape[0], hits), jnp.float32)
    for offset in range(KSIZE):
        summed = summed + taps[offset][:, None] * padded[:, offset:offset + hits]
    smoothed = summed.astype(jnp.bfloat16)
    projected = jnp.dot(point_weight, smoothed, preferred_element_type=jnp.float32)
    stored = projected.reshape(HEADS, PROJ, hits).astype(jnp.bfloat16)
    queries = stored[:, :HD]
    keys = stored[:, HD:2 * HD]
    values = stored[:, 2 * HD:3 * HD]
    kinetic = jax.vmap(kinematics)(stored[:, 3 * HD:].astype(jnp.float32))
    valid = position % HIT_DEV < valid_counts[block_of]
    keys_padded = wrap_ends(keys)
    values_padded = wrap_ends(values)
    kin_padded = wrap_ends(kinetic)
    valid_padded = wrap_ends(valid)

    def one_block(block_index):
        start = (block_index * HIT_DEV).astype(jnp.int32)
        query_rows = lax.dynamic_slice_in_dim(queries, start, HIT_DEV, 2)
        query_kin = lax.dynamic_slice_in_dim(kinetic, start, HIT_DEV, 2)
        key_rows = lax.dynamic_slice_in_dim(keys_padded, start, 4 * HIT_DEV, 2)
        value_rows = lax.dynamic_slice_in_dim(values_padded, start, 4 * HIT_DEV, 2)
        key_kin = lax.dynamic_slice_in_dim(kin_padded, start, 4 * HIT_DEV, 2)
        key_valid = lax.dynamic_slice_in_dim(valid_padded, start, 4 * HIT_DEV, 0)
        key_valid_all = jnp.broadcast_to(key_valid, (HEADS, 4 * HIT_DEV))
        return lax.map(one_head, (query_rows, query_kin, key_rows, value_rows, key_kin, pair_weight, key_valid_all))
    outputs = lax.map(one_block, jnp.arange(blocks, dtype=jnp.int32))
    return outputs.transpose(1, 2, 0, 3).reshape(HEADS * HD, hits)
```

```python
import functools

import jax
import jax.numpy as jnp
from jax import lax
from jax.experimental import pallas as pl
from jax.experimental.pallas import tpu as pltpu
from jax.sharding import PartitionSpec as P

HD = 32
KSIZE = 7
PROJ = 100

floor_pt = 0.1
mass_offset = 0.1
masked_score = -1e30
LOG2E = 1.4426950408889634

DEPTH = 128
ROW_M = 64
ROW_MASK = 79
ROW_D = 80
ROW_TS = 105
ROW_C = 108

GRAIN = 16
PROBE = 64
LIMIT = 2.0**100

PAIRS = ((0, 0), (0, 1), (1, 0), (1, 1), (0, 2), (2, 0))


def with_halo(block, axis, width):
    count = lax.axis_size(axis)
    forward = [(i, i + 1) for i in range(count - 1)]
    backward = [(target, source) for source, target in forward]
    low = lax.ppermute(block[:, block.shape[1] - width :], axis, forward)
    high = lax.ppermute(block[:, :width], axis, backward)
    return jnp.concatenate([low, block, high], axis=1)


def passed_along(block, axis, distance):
    devices = range(lax.axis_size(axis))
    route = [((i - distance) % len(devices), i) for i in devices]
    return lax.ppermute(block, axis, route)


def split3(x):
    high = x.astype(jnp.bfloat16).astype(jnp.float32)
    rest = x - high
    mid = rest.astype(jnp.bfloat16).astype(jnp.float32)
    low = (rest - mid).astype(jnp.bfloat16).astype(jnp.float32)
    return high, mid, low


def kinematics(a0, along_x, along_y, along_z):
    softplus = jnp.maximum(a0, 0.0) + jnp.log1p(jnp.exp(-jnp.abs(a0)))
    hit_mass = mass_offset + softplus
    mass_sq = hit_mass * hit_mass
    trans_sq = along_x * along_x + along_y * along_y
    energy = jnp.sqrt(mass_sq + trans_sq + along_z * along_z)
    trans_mass = jnp.sqrt(mass_sq + trans_sq)
    magnitude = jnp.log((jnp.abs(along_z) + energy) / trans_mass)
    rapidity = jnp.where(along_z < 0.0, -magnitude, magnitude)
    inverse_pt = 1.0 / jnp.maximum(jnp.sqrt(trans_sq), floor_pt)
    return energy, mass_sq, rapidity, along_x * inverse_pt, along_y * inverse_pt, trans_sq


def key_rows(energy, mass_sq, rapidity, unit_x, unit_y, trans_sq, momentum):
    one = jnp.ones_like(energy)
    parts = split3(energy)
    rows = [parts[a] for a, _ in PAIRS]
    rows += momentum
    rows += list(split3(mass_sq)) + [one] * 3
    rows += [None]
    rows += list(split3(rapidity * rapidity)) + [one] * 3
    for value in (rapidity, unit_x, unit_y):
        parts = split3(value)
        rows += [parts[a] for a, _ in PAIRS]
    return rows + [one] + list(split3(trans_sq))


def query_rows(energy, mass_sq, rapidity, unit_x, unit_y, momentum):
    one = jnp.ones_like(energy)
    parts = split3(energy)
    rows = [2.0 * parts[b] for _, b in PAIRS]
    rows += [-2.0 * value for value in momentum]
    rows += [one] * 3 + list(split3(mass_sq))
    rows += [one]
    rows += [one] * 3 + list(split3(rapidity * rapidity))
    for value in (rapidity, unit_x, unit_y):
        parts = split3(value)
        rows += [-2.0 * parts[b] for _, b in PAIRS]
    return rows + [2.0 * one]


def build_queries(own_head, kin, stacked, feats, q_s, q_m, q_d, rows):
    own_rows = query_rows(*[v[0:1] for v in kin[:5]], [v[0:1] for v in stacked[1:]])
    scaled = own_head[0:HD, :].astype(jnp.float32) * (LOG2E * HD**-0.5)
    high = scaled.astype(jnp.bfloat16).astype(jnp.float32)
    feats[0:HD, :] = high
    feats[HD:2*HD, :] = scaled - high
    feats[ROW_TS-1:, :] = jnp.zeros((DEPTH-ROW_TS+1, rows), jnp.float32)
    for offset, row in enumerate(own_rows):
        feats[ROW_M+offset:ROW_M+offset+1, :] = row
    both = feats[...]
    at_row = lax.broadcasted_iota(jnp.int32, (DEPTH, rows), 0)
    in_m = (at_row >= ROW_M) & (at_row < ROW_MASK)
    in_s = (at_row < ROW_M) | (at_row == ROW_MASK)
    q_s[...] = jnp.where(in_s, both, 0.0).astype(jnp.bfloat16)
    q_m[...] = jnp.where(in_m, both, 0.0).astype(jnp.bfloat16)
    q_d[...] = jnp.where(at_row >= ROW_D, both, 0.0).astype(jnp.bfloat16)

def kernel(starts_at, chunk, piece, lag, unit, ahead, vk, has_state, last, counts, pairw, own, *refs):
    nb = len(starts_at)
    blocks, refs = refs[:nb], refs[nb:]
    if has_state:
        state_in, refs = refs[:3], refs[3:]
    if last:
        out_ref, refs = refs[0], refs[1:]
    else:
        state_out, refs = refs[:3], refs[3:]
    feats, keys, key_ts, values, q_s, q_m, q_d, q_ts, best, total, summed, wlow, *held3 = refs
    rows = own.shape[2]
    head = pl.program_id(0)
    dot = functools.partial(jnp.dot, preferred_element_type=jnp.float32)
    starts=[0]
    for i in range(nb):
        starts.append(starts[-1] + (counts[i] - starts_at[i] + GRAIN-1)//GRAIN*GRAIN)
    reached = starts[-1]

    lanes = lax.broadcasted_iota(jnp.int32, (1, rows), 1)
    sources=[(own, 3*HD)] + [(b, b.shape[1]-4) for b in blocks]
    raw=[ref[head, at:at+4, :].astype(jnp.float32) for ref, at in sources]
    stacked=[jnp.concatenate([r[i:i+1] for r in raw], axis=0) for i in range(4)]
    kin=kinematics(*stacked)
    keyed=key_rows(*kin, stacked[1:])
    q_ts[...] = jnp.broadcast_to(kin[5][0:1], (8, rows))
    build_queries(own[head], kin, stacked, feats, q_s, q_m, q_d, rows)
    feat_row = lax.broadcasted_iota(jnp.int32, (DEPTH, 128), 0)
    pick = (feat_row >= ROW_TS) & (feat_row < ROW_TS+3)
    pick = jnp.where(pick, 1.0, 0.0).astype(jnp.bfloat16)
    for i, block in enumerate(blocks):
        at = block.shape[1]-4-2*HD
        low = block[head, at:at+HD, :].astype(jnp.float32)
        feats[0:HD, :] = low
        feats[HD:2*HD, :] = low
        for offset, row in enumerate(keyed):
            value = jnp.where(lanes < counts[i], 0.0, masked_score) if row is None else row[i+1:i+2]
            feats[ROW_M+offset:ROW_M+offset+1, :] = value
        feats[ROW_C:ROW_C+3, :] = jnp.ones((3, rows), jnp.float32)
        turned = jnp.transpose(feats[...].astype(jnp.bfloat16))
        turned = turned[starts_at[i]:]
        n = rows - starts_at[i]
        start = pl.multiple_of(starts[i], GRAIN)
        keys[pl.ds(start, n), :] = turned
        key_ts[pl.ds(start, n), :] = dot(turned, pick)
        v = block[head, at+HD:at+2*HD, starts_at[i]:].astype(jnp.float32)
        if i == 0:
            values[:, 0:n] = v.astype(jnp.bfloat16)
        else:
            shift = start % 128
            base = pl.multiple_of(start - shift, 128)
            v = jnp.concatenate([v, jnp.zeros((HD, 128), jnp.float32)], axis=1)
            v = pltpu.roll(v, shift, 1)
            old = values[:, pl.ds(base, 128)].astype(jnp.float32)
            lane = lax.broadcasted_iota(jnp.int32, (HD, 128), 1)
            firstv = jnp.where(lane < shift, old, v[:, :128])
            values[:, pl.ds(base, 128)] = firstv.astype(jnp.bfloat16)
            values[:, pl.ds(base+128, n)] = v[:, 128:].astype(jnp.bfloat16)
    start = pl.multiple_of(reached, GRAIN)
    lane = lax.broadcasted_iota(jnp.int32, (2*chunk, DEPTH), 1)
    empty = jnp.where(lane == ROW_MASK, masked_score, jnp.where((lane == ROW_M+9), 1.0, 0.0))
    keys[pl.ds(start, 2*chunk), :] = empty.astype(jnp.bfloat16)
    key_ts[pl.ds(start, 2*chunk), :] = jnp.zeros((2*chunk, 128), jnp.float32)
    shift = start % 128
    base = pl.multiple_of(start - shift, 128)
    old = values[:, pl.ds(base, 128)].astype(jnp.float32)
    lane = lax.broadcasted_iota(jnp.int32, (HD, 128), 1)
    values[:, pl.ds(base, 128)] = jnp.where(lane < shift, old, 0.0).astype(jnp.bfloat16)
    values[:, pl.ds(base+128, chunk)] = jnp.zeros((HD, chunk), jnp.bfloat16)

    w0, w1, w2 = [pairw[head, i] for i in range(3)]

    def products(at, count, cols):
        lhs = keys[pl.ds(at, count), :]
        return [dot(lhs, q[:, cols]) for q in (q_d, q_m, q_s)]

    def combine(three, at, count, cols):
        separation, invariant, raw_score = three
        width = separation.shape[1]
        ts_key = jnp.concatenate([key_ts[pl.ds(at, count), :]]*(width//128), axis=1)
        ts_query = jnp.concatenate([q_ts[:, cols]]*(count//8), axis=0)
        kt_sq = jnp.minimum(ts_key, ts_query)*separation
        score = raw_score + w0*lax.log2(invariant)
        return score + w1*lax.log2(1.0+kt_sq) + w2*lax.log2(1.0+separation)

    def scores(at, count, cols):
        return combine(products(at, count, cols), at, count, cols)

    if has_state:
        best[...] = state_in[0][head]
    else:
        best[...] = jnp.full((8, rows), masked_score, jnp.float32)

    def attempt(number, go):
        @pl.when(go == 1)
        def _():
            old = best[...]
            def probe(index, carry):
                at = pl.multiple_of(index*PROBE, PROBE)
                for lo in range(0, rows, piece):
                    cols = pl.ds(lo, piece)
                    s = scores(at, PROBE, cols)
                    top = jnp.max(s.reshape(PROBE//8, 8, piece), axis=0)
                    best[:, cols] = jnp.maximum(best[:, cols], top)
                return carry
            npr = jnp.where(number == 0, 0 if has_state else 1, (reached + PROBE - 1)//PROBE)
            q_s[ROW_C-12:ROW_C+4, :] = jnp.zeros((16, rows), jnp.bfloat16)
            lax.fori_loop(0, npr, probe, 0)
            top = jnp.max(best[...], axis=0, keepdims=True)
            best[...] = jnp.broadcast_to(top, (8, rows))
            parts = split3(-top)
            q_s[ROW_C-12:ROW_C+4, :] = jnp.concatenate([jnp.zeros((12, rows), jnp.float32), *parts, jnp.zeros((1, rows), jnp.float32)], axis=0).astype(jnp.bfloat16)
            if has_state:
                fade = jnp.exp2(old - best[...])
                total[...] = state_in[1][head]*fade
                summed[...] = state_in[2][head]*jnp.concatenate([fade]*(HD//8), axis=0)
            else:
                total[...] = jnp.zeros((8, rows), jnp.float32)
                summed[...] = jnp.zeros((HD, rows), jnp.float32)

            def fill(at, lo):
                cols = pl.ds(lo, piece)
                for ref, value in zip(held3, products(at, chunk, cols)):
                    ref[:, cols] = value

            def gather(at, lo):
                cols = pl.ds(lo, piece)
                summed[:, cols] += dot(values[:, pl.ds(at, chunk)], wlow[:, cols])

            def one_chunk(index, carry):
                at = pl.multiple_of(index*chunk, chunk)
                before = pl.multiple_of(jnp.maximum(index-1, 0)*chunk, chunk)
                after = pl.multiple_of(at + chunk, chunk)
                waiting = [(before, rows - piece*(k+1)) for k in reversed(range(lag))]
                for lo in range(0, rows, piece):
                    cols = pl.ds(lo, piece)
                    w = jnp.exp2(combine([ref[:, cols] for ref in held3], at, chunk, cols))
                    total[:, cols] += jnp.sum(w.reshape(chunk//8, 8, piece), axis=0)
                    wlow[:, cols] = w.astype(jnp.bfloat16)
                    waiting.append((at, lo))
                    fill(after, lo)
                    gather(*waiting.pop(0))
                return carry
            for lo in range(0, rows, piece):
                fill(0, lo)
            wlow[...] = jnp.zeros((chunk, rows), jnp.bfloat16)
            n_chunks = (reached + chunk - 1)//chunk
            lax.fori_loop(0, n_chunks, one_chunk, 0)
            for lo in range(rows - lag*piece, rows, piece):
                gather(pl.multiple_of((n_chunks-1)*chunk, chunk), lo)
        over = jnp.logical_not(jnp.max(total[...]) < LIMIT)
        return over.astype(jnp.int32)
    lax.fori_loop(0, 2, attempt, jnp.int32(1))
    if last:
        t = jnp.sum(total[...], axis=0, keepdims=True)
        out_ref[...] = (summed[...]/t).astype(jnp.bfloat16)
    else:
        state_out[0][0] = best[...]
        state_out[1][0] = total[...]
        state_out[2][0] = summed[...]

def attend(counts, pairw, own, blocks, starts_at, state, last, chunk=256, piece=256, lag=2, unit=256, ahead=1, vk=256):
    heads,_,rows = own.shape
    nb=len(blocks)
    held = nb*rows + 2*chunk + 256
    whole = lambda a: pl.BlockSpec(a.shape, lambda h: (0,)*a.ndim)
    sizes=(8,8,HD)
    smem=pl.BlockSpec(memory_space=pltpu.SMEM)
    operands=[counts, pairw, own, *blocks] + (list(state) if state is not None else [])
    in_specs=[smem, smem]+[whole(a) for a in operands[2:]]
    if last:
        out_shape=jax.ShapeDtypeStruct((heads*HD, rows), jnp.bfloat16)
        out_specs=pl.BlockSpec((HD, rows), lambda h:(h,0))
    else:
        out_shape=[jax.ShapeDtypeStruct((heads,s,rows), jnp.float32) for s in sizes]
        out_specs=[pl.BlockSpec((1,s,rows), lambda h:(h,0,0)) for s in sizes]
    pairs=heads*rows*nb*rows
    return pl.pallas_call(
        functools.partial(kernel, tuple(starts_at), chunk, piece, lag, unit, ahead, vk, state is not None, last),
        grid=(heads,), in_specs=in_specs, out_specs=out_specs, out_shape=out_shape,
        scratch_shapes=[
            pltpu.VMEM((DEPTH, rows), jnp.float32),
            pltpu.VMEM((held, DEPTH), jnp.bfloat16),
            pltpu.VMEM((held, 128), jnp.float32),
            pltpu.VMEM((HD, held), jnp.bfloat16),
            pltpu.VMEM((DEPTH, rows), jnp.bfloat16),
            pltpu.VMEM((DEPTH, rows), jnp.bfloat16),
            pltpu.VMEM((DEPTH, rows), jnp.bfloat16),
            pltpu.VMEM((8, rows), jnp.float32),
            pltpu.VMEM((8, rows), jnp.float32),
            pltpu.VMEM((8, rows), jnp.float32),
            pltpu.VMEM((HD, rows), jnp.float32),
            pltpu.VMEM((chunk, rows), jnp.bfloat16),
            *[pltpu.VMEM((chunk, rows), jnp.float32)]*3,
        ],
        compiler_params=pltpu.CompilerParams(vmem_limit_bytes=48*1024*1024),
        cost_estimate=pl.CostEstimate(flops=pairs*2*DEPTH*4, bytes_accessed=1<<20, transcendentals=4*pairs),
        name="attend_last" if last else "attend_own",
    )(*operands)


def shards(hit_features, depth_kernel, point_weight, pair_weight, hit_order, valid_counts):
    rows = hit_features.shape[1]
    heads_here = point_weight.shape[0] // PROJ
    position = jnp.arange(rows, dtype=jnp.int32)
    chosen = (position[:, None] == hit_order[None, :]).astype(jnp.bfloat16)
    ordered = jnp.dot(hit_features, chosen, preferred_element_type=jnp.float32)
    ordered = ordered.astype(jnp.bfloat16)
    half = KSIZE // 2
    padded = with_halo(ordered, "seq", half).astype(jnp.float32)
    taps = depth_kernel.astype(jnp.float32)
    summed = jnp.zeros((ordered.shape[0], rows), jnp.float32)
    for offset in range(KSIZE):
        summed = summed + taps[offset][:, None] * padded[:, offset : offset + rows]
    smoothed = summed.astype(jnp.bfloat16)
    projected = jnp.dot(
        point_weight,
        lax.all_gather(smoothed, "head", axis=0, tiled=True),
        preferred_element_type=jnp.float32,
    )
    stored = projected.reshape(heads_here, PROJ, rows).astype(jnp.bfloat16)
    distances = (1, -1, -2)
    counts = jnp.concatenate([passed_along(valid_counts, "seq", d) for d in distances])
    mine = [stored[h : h + 1] for h in range(heads_here)]
    weights = [pair_weight[h : h + 1] for h in range(heads_here)]
    arrived = [[passed_along(one[:, HD:], "seq", d) for d in distances] for one in mine]
    states = [attend(valid_counts, w, one, [one], (0,), None, False) for w, one in zip(weights, mine)]
    results = [
        attend(counts, w, one, blocks, (0, 0, 0), state, True)
        for w, one, blocks, state in zip(weights, mine, arrived, states)
    ]
    return jnp.concatenate(results, axis=0)


def solution(mesh):
    in_specs = (
        P("head", ("groups", "seq")),
        P(None, "head"),
        P("head", None),
        P("head", None),
        P(("groups", "seq")),
        P(("groups", "seq")),
    )
    out_specs = P("head", ("groups", "seq"))
    return jax.shard_map(shards, mesh=mesh, in_specs=in_specs, out_specs=out_specs, check_vma=False)
```

```python
import functools

import jax
import jax.numpy as jnp
from jax import lax
from jax.experimental import pallas as pl
from jax.experimental.pallas import tpu as pltpu
from jax.sharding import PartitionSpec as P

HD = 32
KSIZE = 7
PROJ = 100

floor_pt = 0.1
mass_offset = 0.1
masked_score = -1e30
LOG2E = 1.4426950408889634

DEPTH = 128
ROW_M = 64
ROW_MASK = 79
ROW_D = 80
ROW_TS = 105
ROW_C = 108

GRAIN = 16
PROBE = 64
LIMIT = 2.0**100

PAIRS = ((0, 0), (0, 1), (1, 0), (1, 1), (0, 2), (2, 0))


def split3(x):
    high = x.astype(jnp.bfloat16).astype(jnp.float32)
    rest = x - high
    mid = rest.astype(jnp.bfloat16).astype(jnp.float32)
    low = (rest - mid).astype(jnp.bfloat16).astype(jnp.float32)
    return high, mid, low


def kinematics(a0, along_x, along_y, along_z):
    softplus = jnp.maximum(a0, 0.0) + jnp.log1p(jnp.exp(-jnp.abs(a0)))
    hit_mass = mass_offset + softplus
    mass_sq = hit_mass * hit_mass
    trans_sq = along_x * along_x + along_y * along_y
    energy = jnp.sqrt(mass_sq + trans_sq + along_z * along_z)
    trans_mass = jnp.sqrt(mass_sq + trans_sq)
    magnitude = jnp.log((jnp.abs(along_z) + energy) / trans_mass)
    rapidity = jnp.where(along_z < 0.0, -magnitude, magnitude)
    inverse_pt = 1.0 / jnp.maximum(jnp.sqrt(trans_sq), floor_pt)
    return energy, mass_sq, rapidity, along_x * inverse_pt, along_y * inverse_pt, trans_sq


def key_rows(energy, mass_sq, rapidity, unit_x, unit_y, trans_sq, momentum):
    one = jnp.ones_like(energy)
    parts = split3(energy)
    rows = [parts[a] for a, _ in PAIRS]
    rows += momentum
    rows += list(split3(mass_sq)) + [one] * 3
    rows += [None]
    rows += list(split3(rapidity * rapidity)) + [one] * 3
    for value in (rapidity, unit_x, unit_y):
        parts = split3(value)
        rows += [parts[a] for a, _ in PAIRS]
    return rows + [one] + list(split3(trans_sq))


def query_rows(energy, mass_sq, rapidity, unit_x, unit_y, momentum):
    one = jnp.ones_like(energy)
    parts = split3(energy)
    rows = [2.0 * parts[b] for _, b in PAIRS]
    rows += [-2.0 * value for value in momentum]
    rows += [one] * 3 + list(split3(mass_sq))
    rows += [one]
    rows += [one] * 3 + list(split3(rapidity * rapidity))
    for value in (rapidity, unit_x, unit_y):
        parts = split3(value)
        rows += [-2.0 * parts[b] for _, b in PAIRS]
    return rows + [2.0 * one]


MESH = pl.DeviceIdType.MESH
DISTANCES = (1, -1, -2)
EDGE = 128


def gather_kernel(
    nblocks, chips,
    feats, order, taps, count,
    gathered, counts,
    wide, halo, halo_send, halo_recv, z_send, z_recv, n_send, n_recv, x_send, x_recv, c_send, c_recv,
):
    group, block, head = [lax.axis_index(name) for name in ("groups", "seq", "head")]
    chip, core = head // 2, head % 2
    channels, rows = feats.shape
    partner = chip * 2 + 1 - core

    def at_block(distance):
        return (group, lax.rem(block + distance + nblocks, nblocks), head)

    def at_head(where):
        return (group, block, where)

    def other(offset):
        return lax.rem(chip + offset, chips) * 2 + core

    halo[0] = jnp.zeros((channels, EDGE), jnp.bfloat16)
    halo[1] = jnp.zeros((channels, EDGE), jnp.bfloat16)
    barrier = pltpu.get_barrier_semaphore()
    steps = sorted({d % nblocks for d in (1, -1, 2, -2)} - {0})
    peers = [(group, lax.rem(block + d, nblocks), head) for d in steps]
    peers += [at_head(other(e)) for e in range(1, chips)] + [at_head(partner)]
    for peer in peers:
        pl.semaphore_signal(barrier, inc=1, device_id=peer, device_id_type=MESH)

    counts[0] = jnp.full((8, 128), count[0].astype(jnp.float32), jnp.float32)
    position = lax.broadcasted_iota(jnp.int32, (rows, 256), 0)
    for lo in range(0, rows, 256):
        chosen = jnp.where(position == order[:, lo : lo + 256], 1.0, 0.0).astype(jnp.bfloat16)
        some = jnp.dot(feats[...], chosen, preferred_element_type=jnp.float32)
        wide[:, EDGE + lo : EDGE + lo + 256] = some.astype(jnp.bfloat16)

    pl.semaphore_wait(barrier, len(peers))

    def remote(source, target, send, recv, device):
        return pltpu.make_async_remote_copy(
            src_ref=source, dst_ref=target, send_sem=send, recv_sem=recv,
            device_id=device, device_id_type=MESH,
        )

    small = [
        remote(counts.at[0], counts.at[k + 1], n_send.at[k], n_recv.at[k], at_block(d))
        for k, d in enumerate(DISTANCES)
    ]
    for copy in small:
        copy.start()
    to_right = remote(wide.at[:, rows : rows + EDGE], halo.at[0], halo_send.at[0], halo_recv.at[0], at_block(1))
    to_left = remote(wide.at[:, EDGE : 2 * EDGE], halo.at[1], halo_send.at[1], halo_recv.at[1], at_block(-1))
    has_right, has_left = block < nblocks - 1, block > 0

    @pl.when(has_right)
    def _():
        to_right.start()

    @pl.when(has_left)
    def _():
        to_left.start()

    @pl.when(has_left)
    def _():
        to_right.wait_recv()

    @pl.when(has_right)
    def _():
        to_left.wait_recv()

    low = jnp.where(has_left, halo[0].astype(jnp.float32), 0.0)
    high = jnp.where(has_right, halo[1].astype(jnp.float32), 0.0)
    middle = wide[:, EDGE : EDGE + rows].astype(jnp.float32)
    padded = jnp.concatenate([low, middle, high], axis=1)
    tap = jnp.concatenate([taps[...].astype(jnp.float32), jnp.zeros((1, channels), jnp.float32)], axis=0)
    tap = jnp.concatenate([tap, jnp.zeros((8, 128 - channels), jnp.float32)], axis=1)
    tap = jnp.transpose(tap)
    half = KSIZE // 2
    total = jnp.zeros((channels, rows), jnp.float32)
    for offset in range(KSIZE):
        moved = pltpu.roll(padded, (half - offset) % padded.shape[1], 1)
        total = total + tap[:channels, offset : offset + 1] * moved[:, EDGE : EDGE + rows]
    gathered[0, head] = total.astype(jnp.bfloat16)

    @pl.when(has_right)
    def _():
        to_right.wait_send()

    @pl.when(has_left)
    def _():
        to_left.wait_send()

    along = [
        remote(gathered.at[0, head], gathered.at[k + 1, head], z_send.at[k], z_recv.at[k], at_block(d))
        for k, d in enumerate(DISTANCES)
    ]
    started = []

    def spread(k):
        source = gathered.at[k, head]
        for e in range(1, chips):
            started.append(remote(source, source, x_send.at[k, e - 1], x_recv.at[k, e - 1], at_head(other(e))))
            started[-1].start()
        started.append(remote(source, source, c_send.at[k, 0], c_recv.at[k, 0], at_head(partner)))
        started[-1].start()

    def pass_on(k):
        for e in range(1, chips):
            here = gathered.at[k, other(chips - e)]
            remote(here, here, x_send.at[k, e - 1], x_recv.at[k, e - 1], at_head(other(e))).wait_recv()
            started.append(remote(here, here, c_send.at[k, e], c_recv.at[k, e], at_head(partner)))
            started[-1].start()

    for copy in along:
        copy.start()
    spread(0)
    pass_on(0)
    for k, copy in enumerate(along):
        copy.wait_recv()
        spread(k + 1)
        if k:
            pass_on(k)
    pass_on(len(along))
    for k in range(len(along) + 1):
        for e in range(chips):
            here = gathered.at[k, lax.rem(chip - e + chips, chips) * 2 + 1 - core]
            remote(here, here, c_send.at[k, e], c_recv.at[k, e], at_head(partner)).wait_recv()
    for copy in small:
        copy.wait()
    for copy in along + started:
        copy.wait_send()


def gather(feats, order, taps, count):
    channels, rows = feats.shape
    nblocks, heads = lax.axis_size("seq"), lax.axis_size("head")
    chips = heads // 2
    slots = len(DISTANCES) + 1
    vmem = pl.BlockSpec(memory_space=pltpu.VMEM)
    dma = pltpu.SemaphoreType.DMA
    return pl.pallas_call(
        functools.partial(gather_kernel, nblocks, chips),
        in_specs=[vmem, vmem, vmem, pl.BlockSpec(memory_space=pltpu.SMEM)],
        out_specs=[vmem, vmem],
        out_shape=[
            jax.ShapeDtypeStruct((slots, heads, channels, rows), jnp.bfloat16),
            jax.ShapeDtypeStruct((slots, 8, 128), jnp.float32),
        ],
        scratch_shapes=[
            pltpu.VMEM((channels, rows + 2 * EDGE), jnp.bfloat16),
            pltpu.VMEM((2, channels, EDGE), jnp.bfloat16),
            dma((2,)), dma((2,)),
            dma((slots - 1,)), dma((slots - 1,)),
            dma((slots - 1,)), dma((slots - 1,)),
            dma((slots, max(chips - 1, 1))), dma((slots, max(chips - 1, 1))),
            dma((slots, chips)), dma((slots, chips)),
        ],
        compiler_params=pltpu.CompilerParams(
            collective_id=0, has_side_effects=True, vmem_limit_bytes=40 * 1024 * 1024
        ),
        name="gather",
    )(feats, order, taps, count)


def build_queries(own_head, kin, stacked, feats, q_s, q_m, q_d, rows):
    own_rows = query_rows(*[v[0:1] for v in kin[:5]], [v[0:1] for v in stacked[1:]])
    scaled = own_head[0:HD, :] * (LOG2E * HD**-0.5)
    high = scaled.astype(jnp.bfloat16).astype(jnp.float32)
    feats[0:HD, :] = high
    feats[HD:2*HD, :] = scaled - high
    feats[ROW_TS-1:, :] = jnp.zeros((DEPTH-ROW_TS+1, rows), jnp.float32)
    for offset, row in enumerate(own_rows):
        feats[ROW_M+offset:ROW_M+offset+1, :] = row
    both = feats[...]
    at_row = lax.broadcasted_iota(jnp.int32, (DEPTH, rows), 0)
    in_m = (at_row >= ROW_M) & (at_row < ROW_MASK)
    in_s = (at_row < ROW_M) | (at_row == ROW_MASK)
    q_s[...] = jnp.where(in_s, both, 0.0).astype(jnp.bfloat16)
    q_m[...] = jnp.where(in_m, both, 0.0).astype(jnp.bfloat16)
    q_d[...] = jnp.where(at_row >= ROW_D, both, 0.0).astype(jnp.bfloat16)

def attention_kernel(chunk, piece, lag, counts_ref, pairw, weight, gathered, out_ref, *refs):
    feats, keys, key_ts, values, q_s, q_m, q_d, q_ts, best, total, summed, wlow, *held3 = refs
    nb, _, rows = gathered.shape
    head = pl.program_id(0)
    dot = functools.partial(jnp.dot, preferred_element_type=jnp.float32)
    counts = [jnp.max(counts_ref[i]).astype(jnp.int32) for i in range(nb)]
    starts=[0]
    for i in range(nb):
        starts.append(starts[-1] + (counts[i] + GRAIN-1)//GRAIN*GRAIN)
    reached = starts[-1]

    lanes = lax.broadcasted_iota(jnp.int32, (1, rows), 1)
    stored = [
        dot(weight[head], gathered[i]).astype(jnp.bfloat16).astype(jnp.float32) for i in range(nb)
    ]
    raw = [one[3 * HD : 3 * HD + 4] for one in stored]
    stacked=[jnp.concatenate([r[i:i+1] for r in raw], axis=0) for i in range(4)]
    kin=kinematics(*stacked)
    keyed=key_rows(*kin, stacked[1:])
    q_ts[...] = jnp.broadcast_to(kin[5][0:1], (8, rows))
    build_queries(stored[0], kin, stacked, feats, q_s, q_m, q_d, rows)
    feat_row = lax.broadcasted_iota(jnp.int32, (DEPTH, 128), 0)
    pick = (feat_row >= ROW_TS) & (feat_row < ROW_TS+3)
    pick = jnp.where(pick, 1.0, 0.0).astype(jnp.bfloat16)
    for i, block in enumerate(stored):
        low = block[HD:2*HD]
        feats[0:HD, :] = low
        feats[HD:2*HD, :] = low
        for offset, row in enumerate(keyed):
            value = jnp.where(lanes < counts[i], 0.0, masked_score) if row is None else row[i:i+1]
            feats[ROW_M+offset:ROW_M+offset+1, :] = value
        feats[ROW_C:ROW_C+3, :] = jnp.ones((3, rows), jnp.float32)
        turned = jnp.transpose(feats[...].astype(jnp.bfloat16))
        n = rows
        start = pl.multiple_of(starts[i], GRAIN)
        keys[pl.ds(start, n), :] = turned
        key_ts[pl.ds(start, n), :] = dot(turned, pick)
        v = block[2*HD:3*HD]
        if i == 0:
            values[0:HD, 0:n] = v.astype(jnp.bfloat16)
        else:
            shift = start % 128
            base = pl.multiple_of(start - shift, 128)
            v = jnp.concatenate([v, jnp.zeros((HD, 128), jnp.float32)], axis=1)
            v = pltpu.roll(v, shift, 1)
            old = values[0:HD, pl.ds(base, 128)].astype(jnp.float32)
            lane = lax.broadcasted_iota(jnp.int32, (HD, 128), 1)
            firstv = jnp.where(lane < shift, old, v[:, :128])
            values[0:HD, pl.ds(base, 128)] = firstv.astype(jnp.bfloat16)
            values[0:HD, pl.ds(base+128, n)] = v[:, 128:].astype(jnp.bfloat16)
    start = pl.multiple_of(reached, GRAIN)
    lane = lax.broadcasted_iota(jnp.int32, (2*chunk, DEPTH), 1)
    empty = jnp.where(lane == ROW_MASK, masked_score, jnp.where((lane == ROW_M+9), 1.0, 0.0))
    keys[pl.ds(start, 2*chunk), :] = empty.astype(jnp.bfloat16)
    key_ts[pl.ds(start, 2*chunk), :] = jnp.zeros((2*chunk, 128), jnp.float32)
    shift = start % 128
    base = pl.multiple_of(start - shift, 128)
    old = values[0:HD, pl.ds(base, 128)].astype(jnp.float32)
    lane = lax.broadcasted_iota(jnp.int32, (HD, 128), 1)
    values[0:HD, pl.ds(base, 128)] = jnp.where(lane < shift, old, 0.0).astype(jnp.bfloat16)
    values[0:HD, pl.ds(base+128, chunk)] = jnp.zeros((HD, chunk), jnp.bfloat16)

    values[HD:, :] = jnp.where(lax.broadcasted_iota(jnp.int32, (16, values.shape[1]), 0) == 0, 1.0, 0.0).astype(jnp.bfloat16)
    w0, w1, w2 = [pairw[head, i] for i in range(3)]

    def products(at, count, cols):
        lhs = keys[pl.ds(at, count), :]
        return [dot(lhs, q[:, cols]) for q in (q_d, q_m, q_s)]

    def combine(three, at, count, cols):
        separation, invariant, raw_score = three
        width = separation.shape[1]
        ts_key = jnp.concatenate([key_ts[pl.ds(at, count), :]]*(width//128), axis=1)
        ts_query = jnp.concatenate([q_ts[:, cols]]*(count//8), axis=0)
        kt_sq = jnp.minimum(ts_key, ts_query)*separation
        score = raw_score + w0*lax.log2(invariant)
        return score + w1*lax.log2(1.0+kt_sq) + w2*lax.log2(1.0+separation)

    def scores(at, count, cols):
        return combine(products(at, count, cols), at, count, cols)

    best[...] = jnp.full((8, rows), masked_score, jnp.float32)

    def attempt(number, go):
        @pl.when(go == 1)
        def _():
            def probe(index, carry):
                at = pl.multiple_of(index*PROBE, PROBE)
                for lo in range(0, rows, piece):
                    cols = pl.ds(lo, piece)
                    s = scores(at, PROBE, cols)
                    top = jnp.max(s.reshape(PROBE//8, 8, piece), axis=0)
                    best[:, cols] = jnp.maximum(best[:, cols], top)
                return carry
            npr = jnp.where(number == 0, 1, (reached + PROBE - 1)//PROBE)
            q_s[ROW_C-12:ROW_C+4, :] = jnp.zeros((16, rows), jnp.bfloat16)
            lax.fori_loop(0, npr, probe, 0)
            top = jnp.max(best[...], axis=0, keepdims=True)
            best[...] = jnp.broadcast_to(top, (8, rows))
            parts = split3(-top)
            q_s[ROW_C-12:ROW_C+4, :] = jnp.concatenate([jnp.zeros((12, rows), jnp.float32), *parts, jnp.zeros((1, rows), jnp.float32)], axis=0).astype(jnp.bfloat16)
            total[...] = jnp.zeros((8, rows), jnp.float32)
            summed[...] = jnp.zeros((HD, rows), jnp.float32)

            def fill(at, lo):
                cols = pl.ds(lo, piece)
                for ref, value in zip(held3, products(at, chunk, cols)):
                    ref[:, cols] = value

            def gather(at, lo):
                cols = pl.ds(lo, piece)
                both = dot(values[:, pl.ds(at, chunk)], wlow[:, cols])
                summed[:, cols] += both[:HD]
                total[:, cols] += both[HD:HD+8]

            def one_chunk(index, carry):
                at = pl.multiple_of(index*chunk, chunk)
                before = pl.multiple_of(jnp.maximum(index-1, 0)*chunk, chunk)
                after = pl.multiple_of(at + chunk, chunk)
                waiting = [(before, rows - piece*(k+1)) for k in reversed(range(lag))]
                for lo in range(0, rows, piece):
                    cols = pl.ds(lo, piece)
                    w = jnp.exp2(combine([ref[:, cols] for ref in held3], at, chunk, cols))
                    wlow[:, cols] = w.astype(jnp.bfloat16)
                    waiting.append((at, lo))
                    fill(after, lo)
                    gather(*waiting.pop(0))
                return carry
            for lo in range(0, rows, piece):
                fill(0, lo)
            wlow[...] = jnp.zeros((chunk, rows), jnp.bfloat16)
            n_chunks = (reached + chunk - 1)//chunk
            lax.fori_loop(0, n_chunks, one_chunk, 0)
            for lo in range(rows - lag*piece, rows, piece):
                gather(pl.multiple_of((n_chunks-1)*chunk, chunk), lo)
        over = jnp.logical_not(jnp.max(total[...]) < LIMIT)
        return over.astype(jnp.int32)
    lax.fori_loop(0, 2, attempt, jnp.int32(1))
    out_ref[...] = (summed[...] / total[0:1, :]).astype(jnp.bfloat16)


def attend(counts, pairw, weight, gathered, chunk=256, piece=256, lag=1):
    heads = weight.shape[0]
    nb, _, rows = gathered.shape
    held = nb * rows + 2 * chunk + 256
    pairs = heads * rows * nb * rows
    whole = pl.BlockSpec(memory_space=pltpu.VMEM)
    return pl.pallas_call(
        functools.partial(attention_kernel, chunk, piece, lag),
        grid=(heads,),
        in_specs=[whole, pl.BlockSpec(memory_space=pltpu.SMEM), whole, whole],
        out_specs=pl.BlockSpec((HD, rows), lambda h: (h, 0)),
        out_shape=jax.ShapeDtypeStruct((heads * HD, rows), jnp.bfloat16),
        scratch_shapes=[
            pltpu.VMEM((DEPTH, rows), jnp.float32),
            pltpu.VMEM((held, DEPTH), jnp.bfloat16),
            pltpu.VMEM((held, 128), jnp.float32),
            pltpu.VMEM((HD + 16, held), jnp.bfloat16),
            pltpu.VMEM((DEPTH, rows), jnp.bfloat16),
            pltpu.VMEM((DEPTH, rows), jnp.bfloat16),
            pltpu.VMEM((DEPTH, rows), jnp.bfloat16),
            pltpu.VMEM((8, rows), jnp.float32),
            pltpu.VMEM((8, rows), jnp.float32),
            pltpu.VMEM((8, rows), jnp.float32),
            pltpu.VMEM((HD, rows), jnp.float32),
            pltpu.VMEM((chunk, rows), jnp.bfloat16),
            *[pltpu.VMEM((chunk, rows), jnp.float32)] * 3,
        ],
        compiler_params=pltpu.CompilerParams(vmem_limit_bytes=48 * 1024 * 1024),
        cost_estimate=pl.CostEstimate(
            flops=pairs * 2 * DEPTH * 4, bytes_accessed=1 << 20, transcendentals=4 * pairs
        ),
        name="attend",
    )(counts, pairw, weight, gathered)


def shards(hit_features, depth_kernel, point_weight, pair_weight, hit_order, valid_counts):
    rows = hit_features.shape[1]
    inputs = point_weight.shape[1]
    gathered, counts = gather(hit_features, hit_order.reshape(1, rows), depth_kernel, valid_counts)
    gathered = gathered.reshape(gathered.shape[0], inputs, rows)
    return attend(counts, pair_weight, point_weight.reshape(-1, PROJ, inputs), gathered)


def solution(mesh):
    in_specs = (
        P("head", ("groups", "seq")),
        P(None, "head"),
        P("head", None),
        P("head", None),
        P(("groups", "seq")),
        P(("groups", "seq")),
    )
    out_specs = P("head", ("groups", "seq"))
    return jax.shard_map(shards, mesh=mesh, in_specs=in_specs, out_specs=out_specs, check_vma=False)
```

```python
import functools

import jax
import jax.numpy as jnp
from jax import lax
from jax.experimental import pallas as pl
from jax.experimental.pallas import tpu as pltpu
from jax.sharding import PartitionSpec as P

HD = 32
KSIZE = 7
PROJ = 100

floor_pt = 0.1
mass_offset = 0.1
masked_score = -1e30
LOG2E = 1.4426950408889634

DEPTH = 128
ROW_M = 64
ROW_MASK = 79
ROW_D = 80
ROW_TS = 105
ROW_C = 108

GRAIN = 16
PROBE = 64
LIMIT = 2.0**100

PAIRS = ((0, 0), (0, 1), (1, 0), (1, 1), (0, 2), (2, 0))


def split3(x):
    high = x.astype(jnp.bfloat16).astype(jnp.float32)
    rest = x - high
    mid = rest.astype(jnp.bfloat16).astype(jnp.float32)
    low = (rest - mid).astype(jnp.bfloat16).astype(jnp.float32)
    return high, mid, low


def kinematics(a0, along_x, along_y, along_z):
    softplus = jnp.maximum(a0, 0.0) + jnp.log1p(jnp.exp(-jnp.abs(a0)))
    hit_mass = mass_offset + softplus
    mass_sq = hit_mass * hit_mass
    trans_sq = along_x * along_x + along_y * along_y
    energy = jnp.sqrt(mass_sq + trans_sq + along_z * along_z)
    trans_mass = jnp.sqrt(mass_sq + trans_sq)
    magnitude = jnp.log((jnp.abs(along_z) + energy) / trans_mass)
    rapidity = jnp.where(along_z < 0.0, -magnitude, magnitude)
    inverse_pt = 1.0 / jnp.maximum(jnp.sqrt(trans_sq), floor_pt)
    return energy, mass_sq, rapidity, along_x * inverse_pt, along_y * inverse_pt, trans_sq


def key_rows(energy, mass_sq, rapidity, unit_x, unit_y, trans_sq, momentum):
    one = jnp.ones_like(energy)
    parts = split3(energy)
    rows = [parts[a] for a, _ in PAIRS]
    rows += momentum
    rows += list(split3(mass_sq)) + [one] * 3
    rows += [None]
    rows += list(split3(rapidity * rapidity)) + [one] * 3
    for value in (rapidity, unit_x, unit_y):
        parts = split3(value)
        rows += [parts[a] for a, _ in PAIRS]
    return rows + [one] + list(split3(trans_sq))


def query_rows(energy, mass_sq, rapidity, unit_x, unit_y, momentum):
    one = jnp.ones_like(energy)
    parts = split3(energy)
    rows = [2.0 * parts[b] for _, b in PAIRS]
    rows += [-2.0 * value for value in momentum]
    rows += [one] * 3 + list(split3(mass_sq))
    rows += [one]
    rows += [one] * 3 + list(split3(rapidity * rapidity))
    for value in (rapidity, unit_x, unit_y):
        parts = split3(value)
        rows += [-2.0 * parts[b] for _, b in PAIRS]
    return rows + [2.0 * one]


MESH = pl.DeviceIdType.MESH
DISTANCES = (1, -1, -2)
EDGE = 128


def gather_kernel(
    nblocks, chips,
    feats_at, order_at, taps_at, count,
    gathered, counts,
    feats, order, taps, in_sem, smoothed, tally, wide, halo, halo_send, halo_recv, z_send, z_recv, n_send, n_recv, x_send, x_recv, c_send, c_recv,
):
    group, block, head = [lax.axis_index(name) for name in ("groups", "seq", "head")]
    chip, core = head // 2, head % 2
    channels, rows = feats.shape
    loads = [
        pltpu.make_async_copy(order_at, order.at[0], in_sem.at[0]),
        pltpu.make_async_copy(feats_at, feats, in_sem.at[1]),
        pltpu.make_async_copy(taps_at, taps, in_sem.at[2]),
    ]
    for load in loads:
        load.start()
    partner = chip * 2 + 1 - core

    def at_block(distance):
        return (group, lax.rem(block + distance + nblocks, nblocks), head)

    def at_head(where):
        return (group, block, where)

    def other(offset):
        return lax.rem(chip + offset, chips) * 2 + core

    halo[0] = jnp.zeros((channels, EDGE), jnp.bfloat16)
    halo[1] = jnp.zeros((channels, EDGE), jnp.bfloat16)
    barrier = pltpu.get_barrier_semaphore()
    steps = sorted({d % nblocks for d in (1, -1, 2, -2)} - {0})
    peers = [(group, lax.rem(block + d, nblocks), head) for d in steps]
    peers += [at_head(other(e)) for e in range(1, chips)] + [at_head(partner)]
    for peer in peers:
        pl.semaphore_signal(barrier, inc=1, device_id=peer, device_id_type=MESH)

    tally[...] = jnp.full((8, 128), count[0].astype(jnp.float32), jnp.float32)
    for load in loads:
        load.wait()

    def reorder(lo, width):
        position = lax.broadcasted_iota(jnp.int32, (rows, width), 0)
        chosen = jnp.where(position == order[:, lo : lo + width], 1.0, 0.0).astype(jnp.bfloat16)
        some = jnp.dot(feats[...], chosen, preferred_element_type=jnp.float32)
        wide[:, EDGE + lo : EDGE + lo + width] = some.astype(jnp.bfloat16)

    reorder(0, EDGE)
    reorder(rows - EDGE, EDGE)
    pl.semaphore_wait(barrier, len(peers))

    def remote(source, target, send, recv, device):
        return pltpu.make_async_remote_copy(
            src_ref=source, dst_ref=target, send_sem=send, recv_sem=recv,
            device_id=device, device_id_type=MESH,
        )

    to_right = remote(wide.at[:, rows : rows + EDGE], halo.at[0], halo_send.at[0], halo_recv.at[0], at_block(1))
    to_left = remote(wide.at[:, EDGE : 2 * EDGE], halo.at[1], halo_send.at[1], halo_recv.at[1], at_block(-1))
    has_right, has_left = block < nblocks - 1, block > 0

    @pl.when(has_right)
    def _():
        to_right.start()

    @pl.when(has_left)
    def _():
        to_left.start()

    for lo in range(EDGE, rows - EDGE, 256):
        reorder(lo, 256)

    @pl.when(has_left)
    def _():
        to_right.wait_recv()

    @pl.when(has_right)
    def _():
        to_left.wait_recv()

    low = jnp.where(has_left, halo[0].astype(jnp.float32), 0.0)
    high = jnp.where(has_right, halo[1].astype(jnp.float32), 0.0)
    middle = wide[:, EDGE : EDGE + rows].astype(jnp.float32)
    padded = jnp.concatenate([low, middle, high], axis=1)
    tap = jnp.concatenate([taps[...].astype(jnp.float32), jnp.zeros((1, channels), jnp.float32)], axis=0)
    tap = jnp.concatenate([tap, jnp.zeros((8, 128 - channels), jnp.float32)], axis=1)
    tap = jnp.transpose(tap)
    half = KSIZE // 2
    total = jnp.zeros((channels, rows), jnp.float32)
    for offset in range(KSIZE):
        moved = pltpu.roll(padded, (half - offset) % padded.shape[1], 1)
        total = total + tap[:channels, offset : offset + 1] * moved[:, EDGE : EDGE + rows]
    smoothed[...] = total.astype(jnp.bfloat16)
    kept = [
        pltpu.make_async_copy(smoothed, gathered.at[0, head], in_sem.at[0]),
        pltpu.make_async_copy(tally, counts.at[0], in_sem.at[1]),
    ]

    @pl.when(has_right)
    def _():
        to_right.wait_send()

    @pl.when(has_left)
    def _():
        to_left.wait_send()

    along = [
        remote(smoothed, gathered.at[k + 1, head], z_send.at[k], z_recv.at[k], at_block(d))
        for k, d in enumerate(DISTANCES)
    ]
    started = []

    def spread(k):
        target = gathered.at[k, head]
        source = target if k else smoothed
        for e in range(1, chips):
            started.append(remote(source, target, x_send.at[k, e - 1], x_recv.at[k, e - 1], at_head(other(e))))
            started[-1].start()
        started.append(remote(source, target, c_send.at[k, 0], c_recv.at[k, 0], at_head(partner)))
        started[-1].start()

    def pass_on(k):
        for e in range(1, chips):
            here = gathered.at[k, other(chips - e)]
            remote(here, here, x_send.at[k, e - 1], x_recv.at[k, e - 1], at_head(other(e))).wait_recv()
            started.append(remote(here, here, c_send.at[k, e], c_recv.at[k, e], at_head(partner)))
            started[-1].start()

    small = [
        remote(tally, counts.at[k + 1], n_send.at[k], n_recv.at[k], at_block(d))
        for k, d in enumerate(DISTANCES)
    ]
    spread(0)
    for copy in along + small + kept:
        copy.start()
    pass_on(0)
    for k, copy in enumerate(along):
        copy.wait_recv()
        spread(k + 1)
        if k:
            pass_on(k)
    pass_on(len(along))
    for k in range(len(along) + 1):
        for e in range(chips):
            here = gathered.at[k, lax.rem(chip - e + chips, chips) * 2 + 1 - core]
            remote(here, here, c_send.at[k, e], c_recv.at[k, e], at_head(partner)).wait_recv()
    for copy in small + kept:
        copy.wait()
    for copy in along + started:
        copy.wait_send()


def gather(feats, order, taps, count):
    channels, rows = feats.shape
    nblocks, heads = lax.axis_size("seq"), lax.axis_size("head")
    chips = heads // 2
    slots = len(DISTANCES) + 1
    anywhere = pl.BlockSpec(memory_space=pltpu.HBM)
    dma = pltpu.SemaphoreType.DMA
    return pl.pallas_call(
        functools.partial(gather_kernel, nblocks, chips),
        in_specs=[anywhere, anywhere, anywhere, pl.BlockSpec(memory_space=pltpu.SMEM)],
        out_specs=[anywhere, anywhere],
        out_shape=[
            jax.ShapeDtypeStruct((slots, heads, channels, rows), jnp.bfloat16),
            jax.ShapeDtypeStruct((slots, 8, 128), jnp.float32),
        ],
        scratch_shapes=[
            pltpu.VMEM((channels, rows), jnp.bfloat16),
            pltpu.VMEM((1, rows), jnp.int32),
            pltpu.VMEM(taps.shape, taps.dtype),
            dma((3,)),
            pltpu.VMEM((channels, rows), jnp.bfloat16),
            pltpu.VMEM((8, 128), jnp.float32),
            pltpu.VMEM((channels, rows + 2 * EDGE), jnp.bfloat16),
            pltpu.VMEM((2, channels, EDGE), jnp.bfloat16),
            dma((2,)), dma((2,)),
            dma((slots - 1,)), dma((slots - 1,)),
            dma((slots - 1,)), dma((slots - 1,)),
            dma((slots, max(chips - 1, 1))), dma((slots, max(chips - 1, 1))),
            dma((slots, chips)), dma((slots, chips)),
        ],
        compiler_params=pltpu.CompilerParams(
            collective_id=0, has_side_effects=True, vmem_limit_bytes=60 * 1024 * 1024
        ),
        name="gather",
    )(feats, order, taps, count)


def build_queries(own_head, kin, stacked, feats, q_s, q_m, q_d, rows):
    own_rows = query_rows(*[v[0:1] for v in kin[:5]], [v[0:1] for v in stacked[1:]])
    scaled = own_head[0:HD, :] * (LOG2E * HD**-0.5)
    high = scaled.astype(jnp.bfloat16).astype(jnp.float32)
    feats[0:HD, :] = high
    feats[HD:2*HD, :] = scaled - high
    feats[ROW_TS-1:, :] = jnp.zeros((DEPTH-ROW_TS+1, rows), jnp.float32)
    for offset, row in enumerate(own_rows):
        feats[ROW_M+offset:ROW_M+offset+1, :] = row
    both = feats[...]
    at_row = lax.broadcasted_iota(jnp.int32, (DEPTH, rows), 0)
    in_m = (at_row >= ROW_M) & (at_row < ROW_MASK)
    in_s = (at_row < ROW_M) | (at_row == ROW_MASK)
    q_s[...] = jnp.where(in_s, both, 0.0).astype(jnp.bfloat16)
    q_m[...] = jnp.where(in_m, both, 0.0).astype(jnp.bfloat16)
    q_d[...] = jnp.where(at_row >= ROW_D, both, 0.0).astype(jnp.bfloat16)

def attention_kernel(chunk, piece, lag, counts_at, pairw_at, weight_at, gathered_at, out_ref, *refs):
    counts_ref, gathered, pairw, weight, in_sem, feats, keys, key_ts, values, q_s, q_m, q_d, q_ts, best, total, summed, wlow, *held3 = refs
    nb, _, rows = gathered.shape
    head = pl.program_id(0)
    dot = functools.partial(jnp.dot, preferred_element_type=jnp.float32)
    loads = [
        pltpu.make_async_copy(source, target, in_sem.at[k])
        for k, (source, target) in enumerate(
            [(counts_at, counts_ref), (weight_at, weight), (pairw_at, pairw)]
            + [(gathered_at.at[i], gathered.at[i]) for i in range(nb)]
        )
    ]

    @pl.when(head == 0)
    def _():
        for load in loads:
            load.start()
        for load in loads:
            load.wait()

    project = weight[0:PROJ, :]
    for other in range(1, weight.shape[0] // PROJ):
        project = jnp.where(head == other, weight[other * PROJ : (other + 1) * PROJ, :], project)
    counts = [jnp.max(counts_ref[i]).astype(jnp.int32) for i in range(nb)]
    starts=[0]
    for i in range(nb):
        starts.append(starts[-1] + (counts[i] + GRAIN-1)//GRAIN*GRAIN)
    reached = starts[-1]

    lanes = lax.broadcasted_iota(jnp.int32, (1, rows), 1)
    stored = [
        dot(project, gathered[i]).astype(jnp.bfloat16).astype(jnp.float32) for i in range(nb)
    ]
    raw = [one[3 * HD : 3 * HD + 4] for one in stored]
    stacked=[jnp.concatenate([r[i:i+1] for r in raw], axis=0) for i in range(4)]
    kin=kinematics(*stacked)
    keyed=key_rows(*kin, stacked[1:])
    q_ts[...] = jnp.broadcast_to(kin[5][0:1], (8, rows))
    build_queries(stored[0], kin, stacked, feats, q_s, q_m, q_d, rows)
    feat_row = lax.broadcasted_iota(jnp.int32, (DEPTH, 128), 0)
    pick = (feat_row >= ROW_TS) & (feat_row < ROW_TS+3)
    pick = jnp.where(pick, 1.0, 0.0).astype(jnp.bfloat16)
    for i, block in enumerate(stored):
        low = block[HD:2*HD]
        feats[0:HD, :] = low
        feats[HD:2*HD, :] = low
        for offset, row in enumerate(keyed):
            value = jnp.where(lanes < counts[i], 0.0, masked_score) if row is None else row[i:i+1]
            feats[ROW_M+offset:ROW_M+offset+1, :] = value
        feats[ROW_C:ROW_C+3, :] = jnp.ones((3, rows), jnp.float32)
        turned = jnp.transpose(feats[...].astype(jnp.bfloat16))
        n = rows
        start = pl.multiple_of(starts[i], GRAIN)
        keys[pl.ds(start, n), :] = turned
        key_ts[pl.ds(start, n), :] = dot(turned, pick)
        v = block[2*HD:3*HD]
        if i == 0:
            values[0:HD, 0:n] = v.astype(jnp.bfloat16)
        else:
            shift = start % 128
            base = pl.multiple_of(start - shift, 128)
            v = jnp.concatenate([v, jnp.zeros((HD, 128), jnp.float32)], axis=1)
            v = pltpu.roll(v, shift, 1)
            old = values[0:HD, pl.ds(base, 128)].astype(jnp.float32)
            lane = lax.broadcasted_iota(jnp.int32, (HD, 128), 1)
            firstv = jnp.where(lane < shift, old, v[:, :128])
            values[0:HD, pl.ds(base, 128)] = firstv.astype(jnp.bfloat16)
            values[0:HD, pl.ds(base+128, n)] = v[:, 128:].astype(jnp.bfloat16)
    start = pl.multiple_of(reached, GRAIN)
    lane = lax.broadcasted_iota(jnp.int32, (2*chunk, DEPTH), 1)
    empty = jnp.where(lane == ROW_MASK, masked_score, jnp.where((lane == ROW_M+9), 1.0, 0.0))
    keys[pl.ds(start, 2*chunk), :] = empty.astype(jnp.bfloat16)
    key_ts[pl.ds(start, 2*chunk), :] = jnp.zeros((2*chunk, 128), jnp.float32)
    shift = start % 128
    base = pl.multiple_of(start - shift, 128)
    old = values[0:HD, pl.ds(base, 128)].astype(jnp.float32)
    lane = lax.broadcasted_iota(jnp.int32, (HD, 128), 1)
    values[0:HD, pl.ds(base, 128)] = jnp.where(lane < shift, old, 0.0).astype(jnp.bfloat16)
    values[0:HD, pl.ds(base+128, chunk)] = jnp.zeros((HD, chunk), jnp.bfloat16)

    values[HD:, :] = jnp.where(lax.broadcasted_iota(jnp.int32, (16, values.shape[1]), 0) == 0, 1.0, 0.0).astype(jnp.bfloat16)
    w0, w1, w2 = [pairw[head, i] for i in range(3)]

    def products(at, count, cols):
        lhs = keys[pl.ds(at, count), :]
        return [dot(lhs, q[:, cols]) for q in (q_d, q_m, q_s)]

    def combine(three, at, count, cols):
        separation, invariant, raw_score = three
        width = separation.shape[1]
        ts_key = jnp.concatenate([key_ts[pl.ds(at, count), :]]*(width//128), axis=1)
        ts_query = jnp.concatenate([q_ts[:, cols]]*(count//8), axis=0)
        kt_sq = jnp.minimum(ts_key, ts_query)*separation
        score = raw_score + w0*lax.log2(invariant)
        return score + w1*lax.log2(1.0+kt_sq) + w2*lax.log2(1.0+separation)

    def scores(at, count, cols):
        return combine(products(at, count, cols), at, count, cols)

    best[...] = jnp.full((8, rows), masked_score, jnp.float32)

    def attempt(number, go):
        @pl.when(go == 1)
        def _():
            def probe(index, carry):
                at = pl.multiple_of(index*PROBE, PROBE)
                for lo in range(0, rows, piece):
                    cols = pl.ds(lo, piece)
                    s = scores(at, PROBE, cols)
                    top = jnp.max(s.reshape(PROBE//8, 8, piece), axis=0)
                    best[:, cols] = jnp.maximum(best[:, cols], top)
                return carry
            npr = jnp.where(number == 0, 1, (reached + PROBE - 1)//PROBE)
            q_s[ROW_C-12:ROW_C+4, :] = jnp.zeros((16, rows), jnp.bfloat16)
            lax.fori_loop(0, npr, probe, 0)
            top = jnp.max(best[...], axis=0, keepdims=True)
            best[...] = jnp.broadcast_to(top, (8, rows))
            parts = split3(-top)
            q_s[ROW_C-12:ROW_C+4, :] = jnp.concatenate([jnp.zeros((12, rows), jnp.float32), *parts, jnp.zeros((1, rows), jnp.float32)], axis=0).astype(jnp.bfloat16)
            total[...] = jnp.zeros((8, rows), jnp.float32)
            summed[...] = jnp.zeros((HD, rows), jnp.float32)

            def fill(at, lo):
                cols = pl.ds(lo, piece)
                for ref, value in zip(held3, products(at, chunk, cols)):
                    ref[:, cols] = value

            def gather(at, lo):
                cols = pl.ds(lo, piece)
                both = dot(values[:, pl.ds(at, chunk)], wlow[:, cols])
                summed[:, cols] += both[:HD]
                total[:, cols] += both[HD:HD+8]

            def one_chunk(index, carry):
                at = pl.multiple_of(index*chunk, chunk)
                before = pl.multiple_of(jnp.maximum(index-1, 0)*chunk, chunk)
                after = pl.multiple_of(at + chunk, chunk)
                waiting = [(before, rows - piece*(k+1)) for k in reversed(range(lag))]
                for lo in range(0, rows, piece):
                    cols = pl.ds(lo, piece)
                    w = jnp.exp2(combine([ref[:, cols] for ref in held3], at, chunk, cols))
                    wlow[:, cols] = w.astype(jnp.bfloat16)
                    waiting.append((at, lo))
                    fill(after, lo)
                    gather(*waiting.pop(0))
                return carry
            for lo in range(0, rows, piece):
                fill(0, lo)
            wlow[...] = jnp.zeros((chunk, rows), jnp.bfloat16)
            n_chunks = (reached + chunk - 1)//chunk
            lax.fori_loop(0, n_chunks, one_chunk, 0)
            for lo in range(rows - lag*piece, rows, piece):
                gather(pl.multiple_of((n_chunks-1)*chunk, chunk), lo)
        over = jnp.logical_not(jnp.max(total[...]) < LIMIT)
        return over.astype(jnp.int32)
    lax.fori_loop(0, 2, attempt, jnp.int32(1))
    out_ref[...] = (summed[...] / total[0:1, :]).astype(jnp.bfloat16)


def attend(counts, pairw, weight, gathered, chunk=256, piece=256, lag=1):
    heads = weight.shape[0] // PROJ
    nb, _, rows = gathered.shape
    held = nb * rows + 2 * chunk + 256
    pairs = heads * rows * nb * rows
    anywhere = pl.BlockSpec(memory_space=pltpu.HBM)
    return pl.pallas_call(
        functools.partial(attention_kernel, chunk, piece, lag),
        grid=(heads,),
        in_specs=[anywhere] * 4,
        out_specs=pl.BlockSpec((HD, rows), lambda h: (h, 0)),
        out_shape=jax.ShapeDtypeStruct((heads * HD, rows), jnp.bfloat16),
        scratch_shapes=[
            pltpu.VMEM(counts.shape, counts.dtype),
            pltpu.VMEM(gathered.shape, gathered.dtype),
            pltpu.SMEM(pairw.shape, pairw.dtype),
            pltpu.VMEM(weight.shape, weight.dtype),
            pltpu.SemaphoreType.DMA((3 + nb,)),
            pltpu.VMEM((DEPTH, rows), jnp.float32),
            pltpu.VMEM((held, DEPTH), jnp.bfloat16),
            pltpu.VMEM((held, 128), jnp.float32),
            pltpu.VMEM((HD + 16, held), jnp.bfloat16),
            pltpu.VMEM((DEPTH, rows), jnp.bfloat16),
            pltpu.VMEM((DEPTH, rows), jnp.bfloat16),
            pltpu.VMEM((DEPTH, rows), jnp.bfloat16),
            pltpu.VMEM((8, rows), jnp.float32),
            pltpu.VMEM((8, rows), jnp.float32),
            pltpu.VMEM((8, rows), jnp.float32),
            pltpu.VMEM((HD, rows), jnp.float32),
            pltpu.VMEM((chunk, rows), jnp.bfloat16),
            *[pltpu.VMEM((chunk, rows), jnp.float32)] * 3,
        ],
        compiler_params=pltpu.CompilerParams(vmem_limit_bytes=58 * 1024 * 1024),
        cost_estimate=pl.CostEstimate(
            flops=pairs * 2 * DEPTH * 4, bytes_accessed=1 << 20, transcendentals=4 * pairs
        ),
        name="attend",
    )(counts, pairw, weight, gathered)


def shards(hit_features, depth_kernel, point_weight, pair_weight, hit_order, valid_counts):
    rows = hit_features.shape[1]
    inputs = point_weight.shape[1]
    gathered, counts = gather(hit_features, hit_order, depth_kernel, valid_counts)
    gathered = gathered.reshape(gathered.shape[0], inputs, rows)
    return attend(counts, pair_weight, point_weight, gathered)


def solution(mesh):
    in_specs = (
        P("head", ("groups", "seq")),
        P(None, "head"),
        P("head", None),
        P("head", None),
        P(("groups", "seq")),
        P(("groups", "seq")),
    )
    out_specs = P("head", ("groups", "seq"))
    return jax.shard_map(shards, mesh=mesh, in_specs=in_specs, out_specs=out_specs, check_vma=False)
```

```python
import functools

import jax
import jax.numpy as jnp
from jax import lax
from jax.experimental import pallas as pl
from jax.experimental.pallas import tpu as pltpu
from jax.sharding import PartitionSpec as P

HD = 32
KSIZE = 7
PROJ = 100

floor_pt = 0.1
mass_offset = 0.1
masked_score = -1e30
LOG2E = 1.4426950408889634

DEPTH = 128
ROW_M = 64
ROW_MASK = 79
ROW_D = 80
ROW_TS = 105
ROW_C = 108

GRAIN = 16
PROBE = 64
LIMIT = 2.0**100

PAIRS = ((0, 0), (0, 1), (1, 0), (1, 1), (0, 2), (2, 0))


def split3(x):
    high = x.astype(jnp.bfloat16).astype(jnp.float32)
    rest = x - high
    mid = rest.astype(jnp.bfloat16).astype(jnp.float32)
    low = (rest - mid).astype(jnp.bfloat16).astype(jnp.float32)
    return high, mid, low


def kinematics(a0, along_x, along_y, along_z):
    softplus = jnp.maximum(a0, 0.0) + jnp.log1p(jnp.exp(-jnp.abs(a0)))
    hit_mass = mass_offset + softplus
    mass_sq = hit_mass * hit_mass
    trans_sq = along_x * along_x + along_y * along_y
    energy = jnp.sqrt(mass_sq + trans_sq + along_z * along_z)
    trans_mass = jnp.sqrt(mass_sq + trans_sq)
    magnitude = jnp.log((jnp.abs(along_z) + energy) / trans_mass)
    rapidity = jnp.where(along_z < 0.0, -magnitude, magnitude)
    inverse_pt = 1.0 / jnp.maximum(jnp.sqrt(trans_sq), floor_pt)
    return energy, mass_sq, rapidity, along_x * inverse_pt, along_y * inverse_pt, trans_sq


def key_rows(energy, mass_sq, rapidity, unit_x, unit_y, trans_sq, momentum):
    one = jnp.ones_like(energy)
    parts = split3(energy)
    rows = [parts[a] for a, _ in PAIRS]
    rows += momentum
    rows += list(split3(mass_sq)) + [one] * 3
    rows += [None]
    rows += list(split3(rapidity * rapidity)) + [one] * 3
    for value in (rapidity, unit_x, unit_y):
        parts = split3(value)
        rows += [parts[a] for a, _ in PAIRS]
    return rows + [one] + list(split3(trans_sq))


def query_rows(energy, mass_sq, rapidity, unit_x, unit_y, momentum):
    one = jnp.ones_like(energy)
    parts = split3(energy)
    rows = [2.0 * parts[b] for _, b in PAIRS]
    rows += [-2.0 * value for value in momentum]
    rows += [one] * 3 + list(split3(mass_sq))
    rows += [one]
    rows += [one] * 3 + list(split3(rapidity * rapidity))
    for value in (rapidity, unit_x, unit_y):
        parts = split3(value)
        rows += [-2.0 * parts[b] for _, b in PAIRS]
    return rows + [2.0 * one]


def ones_row(width):
    at_row = lax.broadcasted_iota(jnp.int32, (16, width), 0)
    return jnp.where(at_row == 0, 1.0, 0.0).astype(jnp.bfloat16)


def ts_pick():
    at_row = lax.broadcasted_iota(jnp.int32, (DEPTH, 128), 0)
    pick = (at_row >= ROW_TS) & (at_row < ROW_TS + 3)
    return jnp.where(pick, 1.0, 0.0).astype(jnp.bfloat16)


def vector_of(block):
    raw = block[3 * HD : 3 * HD + 4]
    return [raw[i : i + 1] for i in range(4)]


def build_queries(block, lines, q_s, q_m, q_d, q_ts):
    rows = block.shape[1]
    vector = vector_of(block)
    kin = kinematics(*vector)
    q_ts[...] = jnp.broadcast_to(kin[5], (8, rows))
    scaled = block[0:HD] * (LOG2E * HD**-0.5)
    high = scaled.astype(jnp.bfloat16).astype(jnp.float32)
    lines[0:HD, :] = high
    lines[HD : 2 * HD, :] = scaled - high
    lines[ROW_TS - 1 :, :] = jnp.zeros((DEPTH - ROW_TS + 1, rows), jnp.float32)
    for offset, row in enumerate(query_rows(*kin[:5], vector[1:])):
        lines[ROW_M + offset : ROW_M + offset + 1, :] = row
    both = lines[...]
    at_row = lax.broadcasted_iota(jnp.int32, (DEPTH, rows), 0)
    in_m = (at_row >= ROW_M) & (at_row < ROW_MASK)
    in_s = (at_row < ROW_M) | (at_row == ROW_MASK)
    q_s[...] = jnp.where(in_s, both, 0.0).astype(jnp.bfloat16)
    q_m[...] = jnp.where(in_m, both, 0.0).astype(jnp.bfloat16)
    q_d[...] = jnp.where(at_row >= ROW_D, both, 0.0).astype(jnp.bfloat16)


def build_keys(block, lines, mask):
    width = block.shape[1]
    vector = vector_of(block)
    lines[0:HD, 0:width] = block[HD : 2 * HD]
    lines[HD : 2 * HD, 0:width] = block[HD : 2 * HD]
    lines[ROW_C - 4 :, 0:width] = jnp.ones((DEPTH - ROW_C + 4, width), jnp.float32)
    for offset, row in enumerate(key_rows(*kinematics(*vector), vector[1:])):
        lines[ROW_M + offset : ROW_M + offset + 1, 0:width] = mask if row is None else row
    return jnp.transpose(lines[:, 0:width].astype(jnp.bfloat16))


def products(views, at, count, cols):
    lhs = views[0][pl.ds(at, count), :]
    return [
        jnp.dot(lhs, q[:, cols], preferred_element_type=jnp.float32)
        for q in (views[5], views[4], views[3])
    ]


def combine(views, w, three, at, count, cols):
    separation, invariant, score = three
    key_ts, q_ts = views[1], views[6]
    ts_key = jnp.concatenate([key_ts[pl.ds(at, count), :]] * (score.shape[1] // 128), axis=1)
    ts_query = jnp.concatenate([q_ts[:, cols]] * (count // 8), axis=0)
    kt_sq = jnp.minimum(ts_key, ts_query) * separation
    score = score + w[0] * lax.log2(invariant)
    return score + w[1] * lax.log2(1.0 + kt_sq) + w[2] * lax.log2(1.0 + separation)


def probe(views, w, best, count, piece):
    rows = best.shape[1]

    def one(index, carry):
        at = pl.multiple_of(index * PROBE, PROBE)
        for lo in range(0, rows, piece):
            cols = pl.ds(lo, piece)
            score = combine(views, w, products(views, at, PROBE, cols), at, PROBE, cols)
            top = jnp.max(score.reshape(PROBE // 8, 8, piece), axis=0)
            best[:, cols] = jnp.maximum(best[:, cols], top)
        return carry

    lax.fori_loop(0, count, one, 0)
    best[...] = jnp.broadcast_to(jnp.max(best[...], axis=0, keepdims=True), best.shape)


def set_reference(best, q_s):
    rows = best.shape[1]
    parts = split3(-best[0:1, :])
    block = [jnp.zeros((12, rows), jnp.float32), *parts, jnp.zeros((1, rows), jnp.float32)]
    q_s[ROW_C - 12 : ROW_C + 4, :] = jnp.concatenate(block, axis=0).astype(jnp.bfloat16)


def visit(views, w, total, summed, wlow, held, chunks, chunk, piece):
    rows = total.shape[1]
    values = views[2]

    def fill(at, lo):
        cols = pl.ds(lo, piece)
        for ref, value in zip(held, products(views, at, chunk, cols)):
            ref[:, cols] = value

    def collect(at, lo):
        cols = pl.ds(lo, piece)
        both = jnp.dot(values[:, pl.ds(at, chunk)], wlow[:, cols], preferred_element_type=jnp.float32)
        summed[:, cols] += both[:HD]
        total[:, cols] += both[HD : HD + 8]

    def one_chunk(index, carry):
        at = pl.multiple_of(index * chunk, chunk)
        after = pl.multiple_of(at + chunk, chunk)
        waiting = (pl.multiple_of(jnp.maximum(index - 1, 0) * chunk, chunk), rows - piece)
        for lo in range(0, rows, piece):
            cols = pl.ds(lo, piece)
            score = combine(views, w, [ref[:, cols] for ref in held], at, chunk, cols)
            wlow[:, cols] = jnp.exp2(score).astype(jnp.bfloat16)
            fill(after, lo)
            collect(*waiting)
            waiting = (at, lo)
        return carry

    for lo in range(0, rows, piece):
        fill(0, lo)
    wlow[:, rows - piece :] = jnp.zeros((chunk, piece), jnp.bfloat16)
    lax.fori_loop(0, chunks, one_chunk, 0)
    collect(pl.multiple_of(jnp.maximum(chunks - 1, 0) * chunk, chunk), rows - piece)


MESH = pl.DeviceIdType.MESH
DISTANCES = (1, -1, -2)
EDGE = 128


def begin_kernel(
    nblocks, chips, chunk, piece,
    feats_at, order_at, taps_at, weight_at, pairw_at, count,
    kept, counts, best, total, summed,
    feats, order, taps, weight, pairw, in_sem, out_sem, tally, wide, halo, gathered, project,
    halo_send, halo_recv, z_send, z_recv, n_send, n_recv, x_send, x_recv, c_send, c_recv,
    lines, keys, key_ts, values, q_s, q_m, q_d, q_ts, wlow, *held,
):
    group, block, head = [lax.axis_index(name) for name in ("groups", "seq", "head")]
    chip, core = head // 2, head % 2
    channels, rows = feats.shape
    loads = [
        pltpu.make_async_copy(order_at, order.at[0], in_sem.at[0]),
        pltpu.make_async_copy(feats_at, feats, in_sem.at[1]),
        pltpu.make_async_copy(taps_at, taps, in_sem.at[2]),
        pltpu.make_async_copy(weight_at, weight, in_sem.at[3]),
        pltpu.make_async_copy(pairw_at, pairw, in_sem.at[4]),
    ]
    for load in loads:
        load.start()
    partner = chip * 2 + 1 - core

    def at_block(distance):
        return (group, lax.rem(block + distance + nblocks, nblocks), head)

    def at_head(where):
        return (group, block, where)

    def other(offset):
        return lax.rem(chip + offset, chips) * 2 + core

    halo[0] = jnp.zeros((channels, EDGE), jnp.bfloat16)
    halo[1] = jnp.zeros((channels, EDGE), jnp.bfloat16)
    barrier = pltpu.get_barrier_semaphore()
    steps = sorted({d % nblocks for d in (1, -1, 2, -2)} - {0})
    peers = [(group, lax.rem(block + d, nblocks), head) for d in steps]
    peers += [at_head(other(e)) for e in range(1, chips)] + [at_head(partner)]
    for peer in peers:
        pl.semaphore_signal(barrier, inc=1, device_id=peer, device_id_type=MESH)

    tally[...] = jnp.full((8, 128), count[0].astype(jnp.float32), jnp.float32)
    for load in loads:
        load.wait()

    def reorder(lo, width):
        position = lax.broadcasted_iota(jnp.int32, (rows, width), 0)
        chosen = jnp.where(position == order[:, lo : lo + width], 1.0, 0.0).astype(jnp.bfloat16)
        some = jnp.dot(feats[...], chosen, preferred_element_type=jnp.float32)
        wide[:, EDGE + lo : EDGE + lo + width] = some.astype(jnp.bfloat16)

    for lo in range(0, rows, 256):
        reorder(lo, 256)
    heads = weight.shape[0] // PROJ
    for h in range(heads):
        part = weight[...].astype(jnp.float32)[h * PROJ : (h + 1) * PROJ]
        project[h, 0:PROJ, :] = part
    middle = wide[:, EDGE : EDGE + rows].astype(jnp.float32)
    tap = jnp.concatenate([taps[...].astype(jnp.float32), jnp.zeros((1, channels), jnp.float32)], axis=0)
    tap = jnp.concatenate([tap, jnp.zeros((8, 128 - channels), jnp.float32)], axis=1)
    tap = jnp.transpose(tap)
    values[HD:, :] = ones_row(values.shape[1])
    pl.semaphore_wait(barrier, len(peers))

    def remote(source, target, send, recv, device):
        return pltpu.make_async_remote_copy(
            src_ref=source, dst_ref=target, send_sem=send, recv_sem=recv,
            device_id=device, device_id_type=MESH,
        )

    to_right = remote(wide.at[:, rows : rows + EDGE], halo.at[0], halo_send.at[0], halo_recv.at[0], at_block(1))
    to_left = remote(wide.at[:, EDGE : 2 * EDGE], halo.at[1], halo_send.at[1], halo_recv.at[1], at_block(-1))
    has_right, has_left = block < nblocks - 1, block > 0

    @pl.when(has_right)
    def _():
        to_right.start()

    @pl.when(has_left)
    def _():
        to_left.start()

    @pl.when(has_left)
    def _():
        to_right.wait_recv()

    @pl.when(has_right)
    def _():
        to_left.wait_recv()

    low = jnp.where(has_left, halo[0].astype(jnp.float32), 0.0)
    high = jnp.where(has_right, halo[1].astype(jnp.float32), 0.0)
    padded = jnp.concatenate([low, middle, high], axis=1)
    half = KSIZE // 2
    conv = jnp.zeros((channels, rows), jnp.float32)
    for offset in range(KSIZE):
        moved = pltpu.roll(padded, (half - offset) % padded.shape[1], 1)
        conv = conv + tap[:channels, offset : offset + 1] * moved[:, EDGE : EDGE + rows]
    gathered[0, head] = conv.astype(jnp.bfloat16)

    @pl.when(has_right)
    def _():
        to_right.wait_send()

    @pl.when(has_left)
    def _():
        to_left.wait_send()

    along = [
        remote(gathered.at[0, head], gathered.at[k + 1, head], z_send.at[k], z_recv.at[k], at_block(d))
        for k, d in enumerate(DISTANCES)
    ]
    small = [
        remote(tally, counts.at[k + 1], n_send.at[k], n_recv.at[k], at_block(d))
        for k, d in enumerate(DISTANCES)
    ]
    here = pltpu.make_async_copy(tally, counts.at[0], in_sem.at[0])
    out = [pltpu.make_async_copy(gathered.at[k], kept.at[k], out_sem.at[k]) for k in range(len(along) + 1)]

    def spread(k):
        mine = gathered.at[k, head]
        for e in range(1, chips):
            remote(mine, mine, x_send.at[k, e - 1], x_recv.at[k, e - 1], at_head(other(e))).start()
        remote(mine, mine, c_send.at[k, 0], c_recv.at[k, 0], at_head(partner)).start()

    def pass_on(k):
        for e in range(1, chips):
            there = gathered.at[k, other(chips - e)]
            remote(there, there, x_send.at[k, e - 1], x_recv.at[k, e - 1], at_head(other(e))).wait_recv()
            remote(there, there, c_send.at[k, e], c_recv.at[k, e], at_head(partner)).start()

    def complete(k):
        for e in range(chips):
            there = gathered.at[k, lax.rem(chip - e + chips, chips) * 2 + 1 - core]
            remote(there, there, c_send.at[k, e], c_recv.at[k, e], at_head(partner)).wait_recv()
        out[k].start()

    def next_block(k):
        if k < len(along):
            along[k].wait_recv()
            spread(k + 1)
        if k + 1 < len(along):
            along[k].wait_send()
            along[k + 1].start()

    spread(0)
    along[0].start()
    pass_on(0)
    next_block(0)
    complete(0)
    for copy in small + [here]:
        copy.start()

    first = rows // 2
    dot = functools.partial(jnp.dot, preferred_element_type=jnp.float32)

    def one_head(number, carry):
        k, h = number // heads, lax.rem(number, heads)
        for step in range(len(along) + 1):
            if step:
                @pl.when(number == step * heads)
                def _():
                    complete(step)
            if step + 1 <= len(along):
                @pl.when(number == step * heads + heads - 1)
                def _():
                    next_block(step + 1)
                    pass_on(step + 1)

        weight_here = project[h].astype(jnp.bfloat16)
        w = [pairw[h, i] for i in range(3)]
        views = (keys, key_ts, values, q_s.at[h], q_m.at[h], q_d.at[h], q_ts.at[h])

        @pl.when(k == 0)
        def _():
            block = dot(weight_here, gathered[0].reshape(-1, rows)).astype(jnp.bfloat16).astype(jnp.float32)
            build_queries(block, lines, q_s.at[h], q_m.at[h], q_d.at[h], q_ts.at[h])

        some = gathered[k, :, :, 0:first].reshape(-1, first)
        block = dot(weight_here, some).astype(jnp.bfloat16).astype(jnp.float32)
        turned = build_keys(block, lines, jnp.zeros((1, first), jnp.float32))
        keys[0:first, :] = turned
        key_ts[0:first, :] = dot(turned, ts_pick())
        values[0:HD, 0:first] = block[2 * HD : 3 * HD].astype(jnp.bfloat16)

        @pl.when(number < heads)
        def _():
            keys[first : first + chunk, :] = jnp.zeros((chunk, DEPTH), jnp.bfloat16)
            best[h] = jnp.full((8, rows), masked_score, jnp.float32)
            probe(views, w, best.at[h], 1, piece)
            set_reference(best.at[h], q_s.at[h])
            total[h] = jnp.zeros((8, rows), jnp.float32)
            summed[h] = jnp.zeros((HD, rows), jnp.float32)

        visit(views, w, total.at[h], summed.at[h], wlow, held, first // chunk, chunk, piece)
        return carry

    lax.fori_loop(0, heads * (len(along) + 1), one_head, 0)
    for copy in small + [here]:
        copy.wait()
    for copy in out:
        copy.wait()
    along[-1].wait_send()
    for k in range(len(along) + 1):
        for e in range(chips):
            there = gathered.at[k, other(chips - e) if e else head]
            if e:
                mine = gathered.at[k, head]
                remote(mine, mine, x_send.at[k, e - 1], x_recv.at[k, e - 1], at_head(other(e))).wait_send()
            remote(there, there, c_send.at[k, e], c_recv.at[k, e], at_head(partner)).wait_send()


def begin(feats, order, taps, weight, pairw, count, chunk=256, piece=256):
    channels, rows = feats.shape
    nblocks, places = lax.axis_size("seq"), lax.axis_size("head")
    heads = weight.shape[0] // PROJ
    chips = places // 2
    slots = len(DISTANCES) + 1
    held = rows // 2 + chunk
    anywhere = pl.BlockSpec(memory_space=pltpu.HBM)
    vmem = pl.BlockSpec(memory_space=pltpu.VMEM)
    dma = pltpu.SemaphoreType.DMA
    return pl.pallas_call(
        functools.partial(begin_kernel, nblocks, chips, chunk, piece),
        in_specs=[anywhere] * 5 + [pl.BlockSpec(memory_space=pltpu.SMEM)],
        out_specs=[anywhere, anywhere, vmem, vmem, vmem],
        out_shape=[
            jax.ShapeDtypeStruct((slots, places, channels, rows), jnp.bfloat16),
            jax.ShapeDtypeStruct((slots, 8, 128), jnp.float32),
            *[jax.ShapeDtypeStruct((heads, size, rows), jnp.float32) for size in (8, 8, HD)],
        ],
        scratch_shapes=[
            pltpu.VMEM((channels, rows), jnp.bfloat16),
            pltpu.VMEM((1, rows), jnp.int32),
            pltpu.VMEM(taps.shape, taps.dtype),
            pltpu.VMEM(weight.shape, weight.dtype),
            pltpu.SMEM(pairw.shape, pairw.dtype),
            dma((5,)),
            dma((slots,)),
            pltpu.VMEM((8, 128), jnp.float32),
            pltpu.VMEM((channels, rows + 2 * EDGE), jnp.bfloat16),
            pltpu.VMEM((2, channels, EDGE), jnp.bfloat16),
            pltpu.VMEM((slots, places, channels, rows), jnp.bfloat16),
            pltpu.VMEM((heads, PROJ + 4, weight.shape[1]), jnp.float32),
            dma((2,)), dma((2,)),
            dma((slots - 1,)), dma((slots - 1,)),
            dma((slots - 1,)), dma((slots - 1,)),
            dma((slots, max(chips - 1, 1))), dma((slots, max(chips - 1, 1))),
            dma((slots, chips)), dma((slots, chips)),
            pltpu.VMEM((DEPTH, rows), jnp.float32),
            pltpu.VMEM((held, DEPTH), jnp.bfloat16),
            pltpu.VMEM((held, 128), jnp.float32),
            pltpu.VMEM((HD + 16, held), jnp.bfloat16),
            *[pltpu.VMEM((heads, DEPTH, rows), jnp.bfloat16)] * 3,
            pltpu.VMEM((heads, 8, rows), jnp.float32),
            pltpu.VMEM((chunk, rows), jnp.bfloat16),
            *[pltpu.VMEM((chunk, rows), jnp.float32)] * 3,
        ],
        compiler_params=pltpu.CompilerParams(
            collective_id=0, has_side_effects=True, vmem_limit_bytes=58 * 1024 * 1024
        ),
        name="begin",
    )(feats, order, taps, weight, pairw, count)


def finish_kernel(
    chunk, piece,
    counts_at, pairw_at, weight_at, gathered_at, best_at, total_at, summed_at,
    out_ref,
    counts_ref, pairw, weight, gathered, best_in, total_in, summed_in, in_sem,
    lines, keys, key_ts, values, q_s, q_m, q_d, q_ts, best, total, summed, wlow, *held,
):
    nb, _, rows = gathered.shape
    head = pl.program_id(0)
    dot = functools.partial(jnp.dot, preferred_element_type=jnp.float32)
    loads = [
        pltpu.make_async_copy(source, target, in_sem.at[k])
        for k, (source, target) in enumerate([
            (counts_at, counts_ref), (pairw_at, pairw), (weight_at, weight),
            (best_at, best_in), (total_at, total_in), (summed_at, summed_in),
            *[(gathered_at.at[i], gathered.at[i]) for i in range(nb)],
        ])
    ]

    @pl.when(head == 0)
    def _():
        for load in loads:
            load.start()
        for load in loads:
            load.wait()

    project = weight[0:PROJ, :]
    for other in range(1, weight.shape[0] // PROJ):
        project = jnp.where(head == other, weight[other * PROJ : (other + 1) * PROJ, :], project)
    counts = [jnp.max(counts_ref[i]).astype(jnp.int32) for i in range(nb)]
    w = [pairw[head, i] for i in range(3)]
    values[HD:, :] = ones_row(values.shape[1])

    def stored(i, low):
        return dot(project, gathered[i, :, low:]).astype(jnp.bfloat16).astype(jnp.float32)

    build_queries(stored(0, 0), lines, q_s, q_m, q_d, q_ts)
    views = (keys, key_ts, values, q_s, q_m, q_d, q_ts)

    def lay_out(low):
        width = rows - low
        start = jnp.int32(0)
        lanes = lax.broadcasted_iota(jnp.int32, (1, width), 1) + low
        for i in range(nb):
            block = stored(i, low)
            turned = build_keys(block, lines, jnp.where(lanes < counts[i], 0.0, masked_score))
            at = pl.multiple_of(start, GRAIN)
            keys[pl.ds(at, width), :] = turned
            key_ts[pl.ds(at, width), :] = dot(turned, ts_pick())
            v = block[2 * HD : 3 * HD]
            if i == 0:
                values[0:HD, 0:width] = v.astype(jnp.bfloat16)
            else:
                place(v, at)
            start = start + (counts[i] - low + GRAIN - 1) // GRAIN * GRAIN
        at = pl.multiple_of(start, GRAIN)
        lane = lax.broadcasted_iota(jnp.int32, (2 * chunk, DEPTH), 1)
        empty = jnp.where(lane == ROW_MASK, masked_score, jnp.where(lane == ROW_M + 9, 1.0, 0.0))
        keys[pl.ds(at, 2 * chunk), :] = empty.astype(jnp.bfloat16)
        key_ts[pl.ds(at, 2 * chunk), :] = jnp.zeros((2 * chunk, 128), jnp.float32)
        place(jnp.zeros((HD, chunk), jnp.float32), at)
        return start

    def place(v, at):
        width = v.shape[1]
        shift = at % 128
        base = pl.multiple_of(at - shift, 128)
        v = pltpu.roll(jnp.concatenate([v, jnp.zeros((HD, 128), jnp.float32)], axis=1), shift, 1)
        old = values[0:HD, pl.ds(base, 128)].astype(jnp.float32)
        lane = lax.broadcasted_iota(jnp.int32, (HD, 128), 1)
        joined = jnp.where(lane < shift, old, v[:, :128])
        values[0:HD, pl.ds(base, 128)] = joined.astype(jnp.bfloat16)
        values[0:HD, pl.ds(base + 128, width)] = v[:, 128:].astype(jnp.bfloat16)

    def attempt(number, go):
        reached = jnp.int32(0)
        for i in range(nb):
            left = counts[i] - jnp.where(number == 0, rows // 2, 0)
            reached = reached + (left + GRAIN - 1) // GRAIN * GRAIN

        @pl.when((go == 1) & (number == 0))
        def _():
            lay_out(rows // 2)
            best[...] = best_in[head]
            total[...] = total_in[head]
            summed[...] = summed_in[head]

        @pl.when((go == 1) & (number == 1))
        def _():
            lay_out(0)
            best[...] = jnp.full((8, rows), masked_score, jnp.float32)
            q_s[ROW_C - 12 : ROW_C + 4, :] = jnp.zeros((16, rows), jnp.bfloat16)
            probe(views, w, best, (reached + PROBE - 1) // PROBE, piece)
            total[...] = jnp.zeros((8, rows), jnp.float32)
            summed[...] = jnp.zeros((HD, rows), jnp.float32)

        @pl.when(go == 1)
        def _():
            set_reference(best, q_s)
            visit(views, w, total, summed, wlow, held, (reached + chunk - 1) // chunk, chunk, piece)

        return jnp.logical_not(jnp.max(total[...]) < LIMIT).astype(jnp.int32)

    lax.fori_loop(0, 2, attempt, jnp.int32(1))
    out_ref[...] = (summed[...] / total[0:1, :]).astype(jnp.bfloat16)


def finish(counts, pairw, weight, gathered, state, chunk=256, piece=256):
    heads = weight.shape[0] // PROJ
    nb, _, rows = gathered.shape
    held = nb * rows + 2 * chunk + 256
    pairs = heads * rows * nb * rows
    operands = [counts, pairw, weight, gathered, *state]
    scratch = [pltpu.VMEM(one.shape, one.dtype) for one in operands]
    scratch[1] = pltpu.SMEM(pairw.shape, pairw.dtype)
    return pl.pallas_call(
        functools.partial(finish_kernel, chunk, piece),
        grid=(heads,),
        in_specs=[pl.BlockSpec(memory_space=pltpu.HBM)] * len(operands),
        out_specs=pl.BlockSpec((HD, rows), lambda h: (h, 0)),
        out_shape=jax.ShapeDtypeStruct((heads * HD, rows), jnp.bfloat16),
        scratch_shapes=[
            *scratch,
            pltpu.SemaphoreType.DMA((len(operands) - 1 + nb,)),
            pltpu.VMEM((DEPTH, rows), jnp.float32),
            pltpu.VMEM((held, DEPTH), jnp.bfloat16),
            pltpu.VMEM((held, 128), jnp.float32),
            pltpu.VMEM((HD + 16, held), jnp.bfloat16),
            *[pltpu.VMEM((DEPTH, rows), jnp.bfloat16)] * 3,
            *[pltpu.VMEM((8, rows), jnp.float32)] * 3,
            pltpu.VMEM((HD, rows), jnp.float32),
            pltpu.VMEM((chunk, rows), jnp.bfloat16),
            *[pltpu.VMEM((chunk, rows), jnp.float32)] * 3,
        ],
        compiler_params=pltpu.CompilerParams(vmem_limit_bytes=58 * 1024 * 1024),
        cost_estimate=pl.CostEstimate(
            flops=pairs * 2 * DEPTH * 4, bytes_accessed=1 << 20, transcendentals=4 * pairs
        ),
        name="finish",
    )(*operands)


def shards(hit_features, depth_kernel, point_weight, pair_weight, hit_order, valid_counts):
    rows = hit_features.shape[1]
    gathered, counts, *state = begin(
        hit_features, hit_order, depth_kernel, point_weight, pair_weight, valid_counts
    )
    gathered = gathered.reshape(gathered.shape[0], point_weight.shape[1], rows)
    return finish(counts, pair_weight, point_weight, gathered, state)


def solution(mesh):
    in_specs = (
        P("head", ("groups", "seq")),
        P(None, "head"),
        P("head", None),
        P("head", None),
        P(("groups", "seq")),
        P(("groups", "seq")),
    )
    out_specs = P("head", ("groups", "seq"))
    return jax.shard_map(shards, mesh=mesh, in_specs=in_specs, out_specs=out_specs, check_vma=False)
```

```python
import functools

import jax
import jax.numpy as jnp
from jax import lax
from jax.experimental import pallas as pl
from jax.experimental.pallas import tpu as pltpu
from jax.sharding import PartitionSpec as P

HD = 32
KSIZE = 7
PROJ = 100

floor_pt = 0.1
mass_offset = 0.1
masked_score = -1e30
LOG2E = 1.4426950408889634

DEPTH = 128
GROUPS = 2 * HD
ROW_TOP = 112
ROW_MASK = 123
PARTS = ((0, 0), (0, 1), (1, 0), (1, 1), (0, 2), (2, 0))
ONCE = (0, 2, 5)

GRAIN = 16
PROBE = 64
LIMIT = 2.0**100


def split3(x):
    high = x.astype(jnp.bfloat16).astype(jnp.float32)
    rest = x - high
    mid = rest.astype(jnp.bfloat16).astype(jnp.float32)
    low = (rest - mid).astype(jnp.bfloat16).astype(jnp.float32)
    return high, mid, low


def kinematics(a0, along_x, along_y, along_z):
    softplus = jnp.maximum(a0, 0.0) + jnp.log1p(jnp.exp(-jnp.abs(a0)))
    hit_mass = mass_offset + softplus
    mass_sq = hit_mass * hit_mass
    trans_sq = along_x * along_x + along_y * along_y
    energy = jnp.sqrt(mass_sq + trans_sq + along_z * along_z)
    trans_mass = jnp.sqrt(mass_sq + trans_sq)
    magnitude = jnp.log((jnp.abs(along_z) + energy) / trans_mass)
    rapidity = jnp.where(along_z < 0.0, -magnitude, magnitude)
    inverse_pt = 1.0 / jnp.maximum(jnp.sqrt(trans_sq), floor_pt)
    return energy, mass_sq, rapidity, along_x * inverse_pt, along_y * inverse_pt, trans_sq


def ones_row(width):
    at_row = lax.broadcasted_iota(jnp.int32, (16, width), 0)
    return jnp.where(at_row == 0, 1.0, 0.0).astype(jnp.bfloat16)


def ts_pick():
    at_row = lax.broadcasted_iota(jnp.int32, (DEPTH, 128), 0)
    pick = at_row == GROUPS + 6
    for number in ONCE[1:]:
        pick = pick | (at_row == GROUPS + 8 * number + 6)
    return jnp.where(pick, 1.0, 0.0).astype(jnp.bfloat16)


def vector_of(block):
    raw = block[3 * HD : 3 * HD + 4]
    return [raw[i : i + 1] for i in range(4)]


def quantities(block):
    vector = vector_of(block)
    energy, mass_sq, rapidity, unit_x, unit_y, trans_sq = kinematics(*vector)
    none = jnp.zeros_like(energy)
    stacked = [energy, rapidity, unit_x, unit_y, mass_sq, rapidity * rapidity, trans_sq, none]
    return split3(jnp.concatenate(stacked, axis=0)), vector[1:], trans_sq


def build_queries(block, q_s, q_m, q_d, q_ts):
    rows = block.shape[1]
    parts, momentum, trans_sq = quantities(block)
    q_ts[...] = jnp.broadcast_to(trans_sq, (8, rows))
    scaled = block[0:HD] * (LOG2E * HD**-0.5)
    high = scaled.astype(jnp.bfloat16).astype(jnp.float32)
    at_row = lax.broadcasted_iota(jnp.int32, (8, rows), 0)
    zero = jnp.zeros((8, rows), jnp.float32)
    for_m, for_d = [zero] * (GROUPS // 8), [zero] * (GROUPS // 8)
    for number, (_, b) in enumerate(PARTS):
        once = 1.0 if number in ONCE else 0.0
        for_m.append(jnp.where(at_row == 0, 2.0 * parts[b], jnp.where(at_row == 4, once, 0.0)))
        twice = jnp.where((at_row >= 1) & (at_row <= 3), -2.0 * parts[b], 0.0)
        for_d.append(jnp.where(at_row == 5, once, twice))
    none = jnp.zeros((1, rows), jnp.float32)
    for_m.append(jnp.concatenate([part[4:5] for part in parts] + [none] * 5, axis=0))
    squares = [part[5:6] for part in parts]
    for_d.append(jnp.concatenate([none] * 3 + squares + [none + 2.0, none], axis=0))
    for_m.append(jnp.concatenate([-2.0 * value for value in momentum] + [none] * 5, axis=0))
    for_d.append(zero)
    for_s = [high, scaled - high] + [zero] * 7 + [jnp.where(at_row == ROW_MASK % 8, 1.0, 0.0)]
    for ref, groups in ((q_s, for_s), (q_m, for_m), (q_d, for_d)):
        ref[...] = jnp.concatenate(groups, axis=0).astype(jnp.bfloat16)


def build_keys(block, mask):
    width = block.shape[1]
    parts, momentum, _ = quantities(block)
    key = block[HD : 2 * HD]
    one = jnp.ones((8, width), jnp.float32)
    none = jnp.zeros((4, width), jnp.float32)
    groups = [key, key] + [parts[a] for a, _ in PARTS]
    groups += [one, jnp.concatenate([*momentum, mask, none], axis=0)]
    return jnp.transpose(jnp.concatenate(groups, axis=0).astype(jnp.bfloat16))


def no_keys(count):
    lane = lax.broadcasted_iota(jnp.int32, (count, DEPTH), 1)
    empty = jnp.where(lane == ROW_MASK, masked_score, jnp.where(lane == GROUPS + 4, 1.0, 0.0))
    return empty.astype(jnp.bfloat16)


def products(keys, queries, at, count, cols):
    lhs = keys[pl.ds(at, count), :]
    return [
        jnp.dot(lhs, q[:, cols], preferred_element_type=jnp.float32)
        for q in (queries[2], queries[1], queries[0])
    ]


def combine(key_ts, queries, w, three, at, count, cols):
    separation, invariant, score = three
    ts_key = jnp.concatenate([key_ts[pl.ds(at, count), :]] * (score.shape[1] // 128), axis=1)
    ts_query = jnp.concatenate([queries[3][:, cols]] * (count // 8), axis=0)
    kt_sq = jnp.minimum(ts_key, ts_query) * separation
    score = score + w[0] * lax.log2(invariant)
    return score + w[1] * lax.log2(1.0 + kt_sq) + w[2] * lax.log2(1.0 + separation)


def probe(keys, key_ts, queries, w, best, start, count, piece):
    rows = best.shape[1]

    def one(index, carry):
        at = pl.multiple_of(start + index * PROBE, PROBE)
        for lo in range(0, rows, piece):
            cols = pl.ds(lo, piece)
            three = products(keys, queries, at, PROBE, cols)
            score = combine(key_ts, queries, w, three, at, PROBE, cols)
            top = jnp.max(score.reshape(PROBE // 8, 8, piece), axis=0)
            best[:, cols] = jnp.maximum(best[:, cols], top)
        return carry

    lax.fori_loop(0, count, one, 0)
    best[...] = jnp.broadcast_to(jnp.max(best[...], axis=0, keepdims=True), best.shape)


def set_reference(best, q_s):
    rows = best.shape[1]
    none = jnp.zeros((1, rows), jnp.float32)
    block = [*split3(-best[0:1, :]), *[none] * 5, *[none] * 3, none + 1.0, *[none] * 4]
    q_s[ROW_TOP:, :] = jnp.concatenate(block, axis=0).astype(jnp.bfloat16)


def fill(keys, queries, held, at, lo, chunk, piece):
    cols = pl.ds(lo, piece)
    for ref, value in zip(held, products(keys, queries, at, chunk, cols)):
        ref[:, cols] = value


def fill_all(keys, queries, held, at, chunk, piece):
    for lo in range(0, held[0].shape[1], piece):
        fill(keys, queries, held, at, lo, chunk, piece)


def visit(
    keys, key_ts, values, every_head, here, w, total, summed, wlow, held,
    start, chunks, next_start, next_here, chunk, piece,
):
    rows = total.shape[1]
    queries = [ref.at[here] for ref in every_head]

    def collect(at, lo):
        cols = pl.ds(lo, piece)
        both = jnp.dot(values[:, pl.ds(at, chunk)], wlow[:, cols], preferred_element_type=jnp.float32)
        summed[:, cols] += both[:HD]
        total[:, cols] += both[HD : HD + 8]

    def one_chunk(index, carry):
        at = pl.multiple_of(start + index * chunk, chunk)
        waiting = (pl.multiple_of(start + jnp.maximum(index - 1, 0) * chunk, chunk), rows - piece)
        is_last = index == chunks - 1
        following = pl.multiple_of(jnp.where(is_last, next_start, at + chunk), chunk)
        next_queries = [ref.at[jnp.where(is_last, next_here, here)] for ref in every_head]
        for lo in range(0, rows, piece):
            cols = pl.ds(lo, piece)
            score = combine(key_ts, queries, w, [ref[:, cols] for ref in held], at, chunk, cols)
            wlow[:, cols] = jnp.exp2(score).astype(jnp.bfloat16)
            fill(keys, next_queries, held, following, lo, chunk, piece)
            collect(*waiting)
            waiting = (at, lo)
        return carry

    wlow[:, rows - piece :] = jnp.zeros((chunk, piece), jnp.bfloat16)
    lax.fori_loop(0, chunks, one_chunk, 0)
    collect(pl.multiple_of(start + jnp.maximum(chunks - 1, 0) * chunk, chunk), rows - piece)


MESH = pl.DeviceIdType.MESH
DISTANCES = (1, -1, -2)
EDGE = 128


def begin_kernel(
    nblocks, chips, chunk, piece,
    feats_at, order_at, taps_at, weight_at, pairw_at, count,
    kept, counts, best, total, summed,
    feats, order, taps, weight, pairw, in_sem, out_sem, tally, wide, halo, gathered, project,
    halo_send, halo_recv, z_send, z_recv, n_send, n_recv, x_send, x_recv, c_send, c_recv,
    keys, key_ts, values, q_s, q_m, q_d, q_ts, wlow, *held,
):
    group, block, head = [lax.axis_index(name) for name in ("groups", "seq", "head")]
    chip, core = head // 2, head % 2
    channels, rows = feats.shape
    loads = [
        pltpu.make_async_copy(order_at, order.at[0], in_sem.at[0]),
        pltpu.make_async_copy(feats_at, feats, in_sem.at[1]),
        pltpu.make_async_copy(taps_at, taps, in_sem.at[2]),
        pltpu.make_async_copy(weight_at, weight, in_sem.at[3]),
        pltpu.make_async_copy(pairw_at, pairw, in_sem.at[4]),
    ]
    for load in loads:
        load.start()
    partner = chip * 2 + 1 - core

    def at_block(distance):
        return (group, lax.rem(block + distance + nblocks, nblocks), head)

    def at_head(where):
        return (group, block, where)

    def other(offset):
        return lax.rem(chip + offset, chips) * 2 + core

    halo[0] = jnp.zeros((channels, EDGE), jnp.bfloat16)
    halo[1] = jnp.zeros((channels, EDGE), jnp.bfloat16)
    barrier = pltpu.get_barrier_semaphore()
    steps = sorted({d % nblocks for d in (1, -1, 2, -2)} - {0})
    peers = [(group, lax.rem(block + d, nblocks), head) for d in steps]
    peers += [at_head(other(e)) for e in range(1, chips)] + [at_head(partner)]
    for peer in peers:
        pl.semaphore_signal(barrier, inc=1, device_id=peer, device_id_type=MESH)

    tally[...] = jnp.full((8, 128), count[0].astype(jnp.float32), jnp.float32)
    for load in loads:
        load.wait()

    def reorder(lo, width):
        position = lax.broadcasted_iota(jnp.int32, (rows, width), 0)
        chosen = jnp.where(position == order[:, lo : lo + width], 1.0, 0.0).astype(jnp.bfloat16)
        some = jnp.dot(feats[...], chosen, preferred_element_type=jnp.float32)
        wide[:, EDGE + lo : EDGE + lo + width] = some.astype(jnp.bfloat16)

    for lo in range(0, rows, 256):
        reorder(lo, 256)
    heads = weight.shape[0] // PROJ
    for h in range(heads):
        part = weight[...].astype(jnp.float32)[h * PROJ : (h + 1) * PROJ]
        project[h, 0:PROJ, :] = part
    middle = wide[:, EDGE : EDGE + rows].astype(jnp.float32)
    tap = jnp.concatenate([taps[...].astype(jnp.float32), jnp.zeros((1, channels), jnp.float32)], axis=0)
    tap = jnp.concatenate([tap, jnp.zeros((8, 128 - channels), jnp.float32)], axis=1)
    tap = jnp.transpose(tap)
    values[HD:, :] = ones_row(values.shape[1])
    pl.semaphore_wait(barrier, len(peers))

    def remote(source, target, send, recv, device):
        return pltpu.make_async_remote_copy(
            src_ref=source, dst_ref=target, send_sem=send, recv_sem=recv,
            device_id=device, device_id_type=MESH,
        )

    to_right = remote(wide.at[:, rows : rows + EDGE], halo.at[0], halo_send.at[0], halo_recv.at[0], at_block(1))
    to_left = remote(wide.at[:, EDGE : 2 * EDGE], halo.at[1], halo_send.at[1], halo_recv.at[1], at_block(-1))
    has_right, has_left = block < nblocks - 1, block > 0

    @pl.when(has_right)
    def _():
        to_right.start()

    @pl.when(has_left)
    def _():
        to_left.start()

    @pl.when(has_left)
    def _():
        to_right.wait_recv()

    @pl.when(has_right)
    def _():
        to_left.wait_recv()

    low = jnp.where(has_left, halo[0].astype(jnp.float32), 0.0)
    high = jnp.where(has_right, halo[1].astype(jnp.float32), 0.0)
    padded = jnp.concatenate([low, middle, high], axis=1)
    half = KSIZE // 2
    conv = jnp.zeros((channels, rows), jnp.float32)
    for offset in range(KSIZE):
        moved = pltpu.roll(padded, (half - offset) % padded.shape[1], 1)
        conv = conv + tap[:channels, offset : offset + 1] * moved[:, EDGE : EDGE + rows]
    gathered[0, head] = conv.astype(jnp.bfloat16)

    @pl.when(has_right)
    def _():
        to_right.wait_send()

    @pl.when(has_left)
    def _():
        to_left.wait_send()

    along = [
        remote(gathered.at[0, head], gathered.at[k + 1, head], z_send.at[k], z_recv.at[k], at_block(d))
        for k, d in enumerate(DISTANCES)
    ]
    small = [
        remote(tally, counts.at[k + 1], n_send.at[k], n_recv.at[k], at_block(d))
        for k, d in enumerate(DISTANCES)
    ]
    here = pltpu.make_async_copy(tally, counts.at[0], in_sem.at[0])
    out = [pltpu.make_async_copy(gathered.at[k], kept.at[k], out_sem.at[k]) for k in range(len(along) + 1)]

    def spread(k):
        mine = gathered.at[k, head]
        for e in range(1, chips):
            remote(mine, mine, x_send.at[k, e - 1], x_recv.at[k, e - 1], at_head(other(e))).start()
        remote(mine, mine, c_send.at[k, 0], c_recv.at[k, 0], at_head(partner)).start()

    def pass_on(k):
        for e in range(1, chips):
            there = gathered.at[k, other(chips - e)]
            remote(there, there, x_send.at[k, e - 1], x_recv.at[k, e - 1], at_head(other(e))).wait_recv()
            remote(there, there, c_send.at[k, e], c_recv.at[k, e], at_head(partner)).start()

    def complete(k):
        for e in range(chips):
            there = gathered.at[k, lax.rem(chip - e + chips, chips) * 2 + 1 - core]
            remote(there, there, c_send.at[k, e], c_recv.at[k, e], at_head(partner)).wait_recv()
        out[k].start()

    def next_block(k):
        if k < len(along):
            along[k].wait_recv()
            spread(k + 1)
        if k + 1 < len(along):
            along[k].wait_send()
            along[k + 1].start()

    spread(0)
    along[0].start()
    pass_on(0)
    next_block(0)
    complete(0)
    for copy in small + [here]:
        copy.start()

    first = rows // 2
    dot = functools.partial(jnp.dot, preferred_element_type=jnp.float32)
    every_head = (q_s, q_m, q_d, q_ts)
    steps = heads * (len(along) + 1)

    def weights_of(h):
        return [pairw[h, i] for i in range(3)]

    def prepare(number):
        k, h = number // heads, lax.rem(number, heads)
        low = pl.multiple_of(lax.rem(number, 2) * first, first)
        weight_here = project[h].astype(jnp.bfloat16)
        some = gathered[k, :, :, 0:first].reshape(-1, first)
        block = dot(weight_here, some).astype(jnp.bfloat16).astype(jnp.float32)
        turned = build_keys(block, jnp.zeros((1, first), jnp.float32))
        keys[pl.ds(low, first), :] = turned
        key_ts[pl.ds(low, first), :] = dot(turned, ts_pick())
        values[0:HD, pl.ds(low, first)] = block[2 * HD : 3 * HD].astype(jnp.bfloat16)

        @pl.when(number < heads)
        def _():
            everywhere = gathered[0].reshape(-1, rows)
            block = dot(weight_here, everywhere).astype(jnp.bfloat16).astype(jnp.float32)
            queries = [ref.at[h] for ref in every_head]
            build_queries(block, *queries)
            best[h] = jnp.full((8, rows), masked_score, jnp.float32)
            probe(keys, key_ts, queries, weights_of(h), best.at[h], low, 1, piece)
            set_reference(best.at[h], q_s.at[h])
            total[h] = jnp.zeros((8, rows), jnp.float32)
            summed[h] = jnp.zeros((HD, rows), jnp.float32)

    def one_step(number, carry):
        for k in range(1, len(along) + 1):
            @pl.when(number == k * heads - 1)
            def _():
                pass_on(k)
                next_block(k)
                complete(k)

        @pl.when(number + 1 < steps)
        def _():
            prepare(number + 1)

        h, low = lax.rem(number, heads), lax.rem(number, 2) * first
        visit(
            keys, key_ts, values, every_head, h, weights_of(h), total.at[h], summed.at[h], wlow, held,
            low, first // chunk, first - low, lax.rem(number + 1, heads), chunk, piece,
        )
        return carry

    prepare(jnp.int32(0))
    fill_all(keys, [ref.at[0] for ref in every_head], held, 0, chunk, piece)
    lax.fori_loop(0, steps, one_step, 0)
    for copy in small + [here]:
        copy.wait()
    for copy in out:
        copy.wait()
    along[-1].wait_send()
    for k in range(len(along) + 1):
        for e in range(chips):
            there = gathered.at[k, other(chips - e) if e else head]
            if e:
                mine = gathered.at[k, head]
                remote(mine, mine, x_send.at[k, e - 1], x_recv.at[k, e - 1], at_head(other(e))).wait_send()
            remote(there, there, c_send.at[k, e], c_recv.at[k, e], at_head(partner)).wait_send()


def begin(feats, order, taps, weight, pairw, count, chunk=256, piece=256):
    channels, rows = feats.shape
    nblocks, places = lax.axis_size("seq"), lax.axis_size("head")
    heads = weight.shape[0] // PROJ
    chips = places // 2
    slots = len(DISTANCES) + 1
    held = rows // 2 * 2
    anywhere = pl.BlockSpec(memory_space=pltpu.HBM)
    vmem = pl.BlockSpec(memory_space=pltpu.VMEM)
    dma = pltpu.SemaphoreType.DMA
    return pl.pallas_call(
        functools.partial(begin_kernel, nblocks, chips, chunk, piece),
        in_specs=[anywhere] * 5 + [pl.BlockSpec(memory_space=pltpu.SMEM)],
        out_specs=[anywhere, anywhere, vmem, vmem, vmem],
        out_shape=[
            jax.ShapeDtypeStruct((slots, places, channels, rows), jnp.bfloat16),
            jax.ShapeDtypeStruct((slots, 8, 128), jnp.float32),
            *[jax.ShapeDtypeStruct((heads, size, rows), jnp.float32) for size in (8, 8, HD)],
        ],
        scratch_shapes=[
            pltpu.VMEM((channels, rows), jnp.bfloat16),
            pltpu.VMEM((1, rows), jnp.int32),
            pltpu.VMEM(taps.shape, taps.dtype),
            pltpu.VMEM(weight.shape, weight.dtype),
            pltpu.SMEM(pairw.shape, pairw.dtype),
            dma((5,)),
            dma((slots,)),
            pltpu.VMEM((8, 128), jnp.float32),
            pltpu.VMEM((channels, rows + 2 * EDGE), jnp.bfloat16),
            pltpu.VMEM((2, channels, EDGE), jnp.bfloat16),
            pltpu.VMEM((slots, places, channels, rows), jnp.bfloat16),
            pltpu.VMEM((heads, PROJ + 4, weight.shape[1]), jnp.float32),
            dma((2,)), dma((2,)),
            dma((slots - 1,)), dma((slots - 1,)),
            dma((slots - 1,)), dma((slots - 1,)),
            dma((slots, max(chips - 1, 1))), dma((slots, max(chips - 1, 1))),
            dma((slots, chips)), dma((slots, chips)),
            pltpu.VMEM((held, DEPTH), jnp.bfloat16),
            pltpu.VMEM((held, 128), jnp.float32),
            pltpu.VMEM((HD + 16, held), jnp.bfloat16),
            *[pltpu.VMEM((heads, DEPTH, rows), jnp.bfloat16)] * 3,
            pltpu.VMEM((heads, 8, rows), jnp.float32),
            pltpu.VMEM((chunk, rows), jnp.bfloat16),
            *[pltpu.VMEM((chunk, rows), jnp.float32)] * 3,
        ],
        compiler_params=pltpu.CompilerParams(
            collective_id=0, has_side_effects=True, vmem_limit_bytes=58 * 1024 * 1024
        ),
        name="begin",
    )(feats, order, taps, weight, pairw, count)


def finish_kernel(
    chunk, piece, held_rows,
    counts_at, pairw_at, weight_at, gathered_at, best_at, total_at, summed_at,
    out_ref,
    counts_ref, pairw, weight, gathered, best, total, summed, old, in_sem,
    keys, key_ts, values, q_s, q_m, q_d, q_ts, wlow, *held,
):
    nb, _, rows = gathered.shape
    heads = weight.shape[0] // PROJ
    dot = functools.partial(jnp.dot, preferred_element_type=jnp.float32)
    loads = [
        pltpu.make_async_copy(source, target, in_sem.at[k])
        for k, (source, target) in enumerate([
            (counts_at, counts_ref), (pairw_at, pairw), (weight_at, weight), (best_at, best),
            *[(gathered_at.at[i], gathered.at[i]) for i in range(nb)],
            (total_at, total), (summed_at, summed),
        ])
    ]
    for load in loads:
        load.start()
    values[HD:, :] = ones_row(values.shape[1])
    for load in loads:
        load.wait()
    counts = [jnp.max(counts_ref[i]).astype(jnp.int32) for i in range(nb)]
    every_head = (q_s, q_m, q_d, q_ts)

    def project(h):
        part = weight[0:PROJ, :]
        for other in range(1, heads):
            part = jnp.where(h == other, weight[other * PROJ : (other + 1) * PROJ, :], part)
        return part

    def weights_of(h):
        return [pairw[h, i] for i in range(3)]

    def place(v, at):
        width = v.shape[1]
        shift = at % 128
        base = pl.multiple_of(at - shift, 128)
        v = pltpu.roll(jnp.concatenate([v, jnp.zeros((HD, 128), jnp.float32)], axis=1), shift, 1)
        before = values[0:HD, pl.ds(base, 128)].astype(jnp.float32)
        lane = lax.broadcasted_iota(jnp.int32, (HD, 128), 1)
        joined = jnp.where(lane < shift, before, v[:, :128])
        values[0:HD, pl.ds(base, 128)] = joined.astype(jnp.bfloat16)
        values[0:HD, pl.ds(base + 128, width)] = v[:, 128:].astype(jnp.bfloat16)

    def lay_out(h, low):
        width = rows - low
        start = h * held_rows
        part = project(h)
        lanes = lax.broadcasted_iota(jnp.int32, (1, width), 1) + low
        for i in range(nb):
            block = dot(part, gathered[i, :, low:]).astype(jnp.bfloat16).astype(jnp.float32)
            turned = build_keys(block, jnp.where(lanes < counts[i], 0.0, masked_score))
            at = pl.multiple_of(start, GRAIN)
            keys[pl.ds(at, width), :] = turned
            key_ts[pl.ds(at, width), :] = dot(turned, ts_pick())
            place(block[2 * HD : 3 * HD], at)
            start = start + (counts[i] - low + GRAIN - 1) // GRAIN * GRAIN
        at = pl.multiple_of(start, GRAIN)
        keys[pl.ds(at, chunk), :] = no_keys(chunk)
        key_ts[pl.ds(at, chunk), :] = jnp.zeros((chunk, 128), jnp.float32)
        place(jnp.zeros((HD, chunk), jnp.float32), at)

    def attempt(number, go):
        reached = jnp.int32(0)
        for i in range(nb):
            left = counts[i] - jnp.where(number == 0, rows // 2, 0)
            reached = reached + (left + GRAIN - 1) // GRAIN * GRAIN
        chunks = (reached + chunk - 1) // chunk

        def prepare(h, carry):
            queries = [ref.at[h] for ref in every_head]

            @pl.when(number == 0)
            def _():
                block = dot(project(h), gathered[0]).astype(jnp.bfloat16).astype(jnp.float32)
                build_queries(block, *queries)
                lay_out(h, rows // 2)

            @pl.when(number == 1)
            def _():
                lay_out(h, 0)
                none = jnp.zeros((8, rows), jnp.float32)
                best[h] = none + masked_score
                set_reference(old, q_s.at[h])
                probes = (reached + PROBE - 1) // PROBE
                probe(keys, key_ts, queries, weights_of(h), best.at[h], h * held_rows, probes, piece)
                total[h] = none
                summed[h] = jnp.zeros((HD, rows), jnp.float32)

            set_reference(best.at[h], q_s.at[h])
            return carry

        def one_head(h, carry):
            after = lax.rem(h + 1, heads)
            visit(
                keys, key_ts, values, every_head, h, weights_of(h), total.at[h], summed.at[h], wlow, held,
                h * held_rows, chunks, after * held_rows, after, chunk, piece,
            )
            return carry

        @pl.when(go == 1)
        def _():
            lax.fori_loop(0, heads, prepare, 0)
            fill_all(keys, [ref.at[0] for ref in every_head], held, 0, chunk, piece)
            lax.fori_loop(0, heads, one_head, 0)

        return jnp.logical_not(jnp.max(total[...]) < LIMIT).astype(jnp.int32)

    old[...] = jnp.zeros((8, rows), jnp.float32)
    lax.fori_loop(0, 2, attempt, jnp.int32(1))
    for h in range(heads):
        out_ref[h * HD : (h + 1) * HD, :] = (summed[h] / total[h, 0:1, :]).astype(jnp.bfloat16)


def finish(counts, pairw, weight, gathered, state, chunk=256, piece=256):
    heads = weight.shape[0] // PROJ
    nb, _, rows = gathered.shape
    held = nb * rows + 2 * chunk
    pairs = heads * rows * nb * rows
    operands = [counts, pairw, weight, gathered, *state]
    scratch = [pltpu.VMEM(one.shape, one.dtype) for one in operands]
    scratch[1] = pltpu.SMEM(pairw.shape, pairw.dtype)
    return pl.pallas_call(
        functools.partial(finish_kernel, chunk, piece, held),
        in_specs=[pl.BlockSpec(memory_space=pltpu.HBM)] * len(operands),
        out_specs=pl.BlockSpec(memory_space=pltpu.VMEM),
        out_shape=jax.ShapeDtypeStruct((heads * HD, rows), jnp.bfloat16),
        scratch_shapes=[
            *scratch,
            pltpu.VMEM((8, rows), jnp.float32),
            pltpu.SemaphoreType.DMA((len(operands) - 1 + nb,)),
            pltpu.VMEM((heads * held, DEPTH), jnp.bfloat16),
            pltpu.VMEM((heads * held, 128), jnp.float32),
            pltpu.VMEM((HD + 16, heads * held), jnp.bfloat16),
            *[pltpu.VMEM((heads, DEPTH, rows), jnp.bfloat16)] * 3,
            pltpu.VMEM((heads, 8, rows), jnp.float32),
            pltpu.VMEM((chunk, rows), jnp.bfloat16),
            *[pltpu.VMEM((chunk, rows), jnp.float32)] * 3,
        ],
        compiler_params=pltpu.CompilerParams(vmem_limit_bytes=58 * 1024 * 1024),
        cost_estimate=pl.CostEstimate(
            flops=pairs * 2 * DEPTH * 4, bytes_accessed=1 << 20, transcendentals=4 * pairs
        ),
        name="finish",
    )(*operands)


def shards(hit_features, depth_kernel, point_weight, pair_weight, hit_order, valid_counts):
    rows = hit_features.shape[1]
    gathered, counts, *state = begin(
        hit_features, hit_order, depth_kernel, point_weight, pair_weight, valid_counts
    )
    gathered = gathered.reshape(gathered.shape[0], point_weight.shape[1], rows)
    return finish(counts, pair_weight, point_weight, gathered, state)


def solution(mesh):
    in_specs = (
        P("head", ("groups", "seq")),
        P(None, "head"),
        P("head", None),
        P("head", None),
        P(("groups", "seq")),
        P(("groups", "seq")),
    )
    out_specs = P("head", ("groups", "seq"))
    return jax.shard_map(shards, mesh=mesh, in_specs=in_specs, out_specs=out_specs, check_vma=False)
```

```python
import functools

import jax
import jax.numpy as jnp
from jax import lax
from jax.experimental import pallas as pl
from jax.experimental.pallas import tpu as pltpu
from jax.sharding import PartitionSpec as P

HD = 32
KSIZE = 7
PROJ = 100

floor_pt = 0.1
mass_offset = 0.1
masked_score = -1e30
LOG2E = 1.4426950408889634

DEPTH = 128
GROUPS = 2 * HD
ROW_TOP = 112
ROW_MASK = 123
PARTS = ((0, 0), (0, 1), (1, 0), (1, 1), (0, 2), (2, 0))
ONCE = (0, 2, 5)

GRAIN = 16
PROBE = 64
LIMIT = 2.0**100


def split3(x):
    high = x.astype(jnp.bfloat16).astype(jnp.float32)
    rest = x - high
    mid = rest.astype(jnp.bfloat16).astype(jnp.float32)
    low = (rest - mid).astype(jnp.bfloat16).astype(jnp.float32)
    return high, mid, low


def kinematics(a0, along_x, along_y, along_z):
    softplus = jnp.maximum(a0, 0.0) + jnp.log1p(jnp.exp(-jnp.abs(a0)))
    hit_mass = mass_offset + softplus
    mass_sq = hit_mass * hit_mass
    trans_sq = along_x * along_x + along_y * along_y
    energy = jnp.sqrt(mass_sq + trans_sq + along_z * along_z)
    trans_mass = jnp.sqrt(mass_sq + trans_sq)
    magnitude = jnp.log((jnp.abs(along_z) + energy) / trans_mass)
    rapidity = jnp.where(along_z < 0.0, -magnitude, magnitude)
    inverse_pt = 1.0 / jnp.maximum(jnp.sqrt(trans_sq), floor_pt)
    return energy, mass_sq, rapidity, along_x * inverse_pt, along_y * inverse_pt, trans_sq


def ones_row(width):
    at_row = lax.broadcasted_iota(jnp.int32, (16, width), 0)
    return jnp.where(at_row == 0, 1.0, 0.0).astype(jnp.bfloat16)


def ts_pick():
    at_row = lax.broadcasted_iota(jnp.int32, (DEPTH, 128), 0)
    pick = at_row == GROUPS + 6
    for number in ONCE[1:]:
        pick = pick | (at_row == GROUPS + 8 * number + 6)
    return jnp.where(pick, 1.0, 0.0).astype(jnp.bfloat16)


def vector_of(block):
    raw = block[3 * HD : 3 * HD + 4]
    return [raw[i : i + 1] for i in range(4)]


def quantities(block):
    vector = vector_of(block)
    energy, mass_sq, rapidity, unit_x, unit_y, trans_sq = kinematics(*vector)
    none = jnp.zeros_like(energy)
    stacked = [energy, rapidity, unit_x, unit_y, mass_sq, rapidity * rapidity, trans_sq, none]
    return split3(jnp.concatenate(stacked, axis=0)), vector[1:], trans_sq


def build_queries(block, q_s, q_m, q_d, q_ts):
    rows = block.shape[1]
    parts, momentum, trans_sq = quantities(block)
    q_ts[...] = jnp.broadcast_to(trans_sq, (8, rows))
    scaled = block[0:HD] * (LOG2E * HD**-0.5)
    high = scaled.astype(jnp.bfloat16).astype(jnp.float32)
    at_row = lax.broadcasted_iota(jnp.int32, (8, rows), 0)
    zero = jnp.zeros((8, rows), jnp.float32)
    for_m, for_d = [zero] * (GROUPS // 8), [zero] * (GROUPS // 8)
    for number, (_, b) in enumerate(PARTS):
        once = 1.0 if number in ONCE else 0.0
        for_m.append(jnp.where(at_row == 0, 2.0 * parts[b], jnp.where(at_row == 4, once, 0.0)))
        twice = jnp.where((at_row >= 1) & (at_row <= 3), -2.0 * parts[b], 0.0)
        for_d.append(jnp.where(at_row == 5, once, twice))
    none = jnp.zeros((1, rows), jnp.float32)
    for_m.append(jnp.concatenate([part[4:5] for part in parts] + [none] * 5, axis=0))
    squares = [part[5:6] for part in parts]
    for_d.append(jnp.concatenate([none] * 3 + squares + [none + 2.0, none], axis=0))
    for_m.append(jnp.concatenate([-2.0 * value for value in momentum] + [none] * 5, axis=0))
    for_d.append(zero)
    for_s = [high, scaled - high] + [zero] * 7 + [jnp.where(at_row == ROW_MASK % 8, 1.0, 0.0)]
    for ref, groups in ((q_s, for_s), (q_m, for_m), (q_d, for_d)):
        ref[...] = jnp.concatenate(groups, axis=0).astype(jnp.bfloat16)


def build_keys(block, mask):
    width = block.shape[1]
    parts, momentum, _ = quantities(block)
    key = block[HD : 2 * HD]
    one = jnp.ones((8, width), jnp.float32)
    none = jnp.zeros((4, width), jnp.float32)
    groups = [key, key] + [parts[a] for a, _ in PARTS]
    groups += [one, jnp.concatenate([*momentum, mask, none], axis=0)]
    return jnp.transpose(jnp.concatenate(groups, axis=0).astype(jnp.bfloat16))


def no_keys(count):
    lane = lax.broadcasted_iota(jnp.int32, (count, DEPTH), 1)
    empty = jnp.where(lane == ROW_MASK, masked_score, jnp.where(lane == GROUPS + 4, 1.0, 0.0))
    return empty.astype(jnp.bfloat16)


def products(keys, queries, at, count, cols):
    lhs = keys[pl.ds(at, count), :]
    return [
        jnp.dot(lhs, q[:, cols], preferred_element_type=jnp.float32)
        for q in (queries[2], queries[1], queries[0])
    ]


def combine(key_ts, queries, w, three, at, count, cols):
    separation, invariant, score = three
    ts_key = jnp.concatenate([key_ts[pl.ds(at, count), :]] * (score.shape[1] // 128), axis=1)
    ts_query = jnp.concatenate([queries[3][:, cols]] * (count // 8), axis=0)
    kt_sq = jnp.minimum(ts_key, ts_query) * separation
    score = score + w[0] * lax.log2(invariant)
    return score + w[1] * lax.log2(1.0 + kt_sq) + w[2] * lax.log2(1.0 + separation)


def probe(keys, key_ts, queries, w, best, start, count, piece):
    rows = best.shape[1]

    def one(index, carry):
        at = pl.multiple_of(start + index * PROBE, PROBE)
        for lo in range(0, rows, piece):
            cols = pl.ds(lo, piece)
            three = products(keys, queries, at, PROBE, cols)
            score = combine(key_ts, queries, w, three, at, PROBE, cols)
            top = jnp.max(score.reshape(PROBE // 8, 8, piece), axis=0)
            best[:, cols] = jnp.maximum(best[:, cols], top)
        return carry

    lax.fori_loop(0, count, one, 0)
    best[...] = jnp.broadcast_to(jnp.max(best[...], axis=0, keepdims=True), best.shape)


def set_reference(best, q_s):
    rows = best.shape[1]
    none = jnp.zeros((1, rows), jnp.float32)
    block = [*split3(-best[0:1, :]), *[none] * 5, *[none] * 3, none + 1.0, *[none] * 4]
    q_s[ROW_TOP:, :] = jnp.concatenate(block, axis=0).astype(jnp.bfloat16)


def fill(keys, queries, held, at, lo, chunk, piece):
    cols = pl.ds(lo, piece)
    for ref, value in zip(held, products(keys, queries, at, chunk, cols)):
        ref[:, cols] = value


def fill_all(keys, queries, held, at, chunk, piece):
    for lo in range(0, held[0].shape[1], piece):
        fill(keys, queries, held, at, lo, chunk, piece)


def visit(
    keys, key_ts, values, every_head, here, w, total, summed, wlow, held,
    start, chunks, next_start, next_here, chunk, piece,
):
    rows = total.shape[1]
    queries = [ref.at[here] for ref in every_head]

    def collect(at, lo):
        cols = pl.ds(lo, piece)
        both = jnp.dot(values[:, pl.ds(at, chunk)], wlow[:, cols], preferred_element_type=jnp.float32)
        summed[:, cols] += both[:HD]
        total[:, cols] += both[HD : HD + 8]

    def one_chunk(index, carry):
        at = pl.multiple_of(start + index * chunk, chunk)
        waiting = (pl.multiple_of(start + jnp.maximum(index - 1, 0) * chunk, chunk), rows - piece)
        is_last = index == chunks - 1
        following = pl.multiple_of(jnp.where(is_last, next_start, at + chunk), chunk)
        next_queries = [ref.at[jnp.where(is_last, next_here, here)] for ref in every_head]
        for lo in range(0, rows, piece):
            cols = pl.ds(lo, piece)
            score = combine(key_ts, queries, w, [ref[:, cols] for ref in held], at, chunk, cols)
            wlow[:, cols] = jnp.exp2(score).astype(jnp.bfloat16)
            fill(keys, next_queries, held, following, lo, chunk, piece)
            collect(*waiting)
            waiting = (at, lo)
        return carry

    wlow[:, rows - piece :] = jnp.zeros((chunk, piece), jnp.bfloat16)
    lax.fori_loop(0, chunks, one_chunk, 0)
    collect(pl.multiple_of(start + jnp.maximum(chunks - 1, 0) * chunk, chunk), rows - piece)


MESH = pl.DeviceIdType.MESH
DISTANCES = (-1, 1, -2)
EDGE = 128


def begin_kernel(
    nblocks, chips, chunk, piece,
    feats_at, order_at, taps_at, weight_at, pairw_at, count,
    kept, counts, best, total, summed,
    feats, order, taps, weight, pairw, in_sem, out_sem, tally, wide, halo, gathered, project,
    halo_send, halo_recv, z_send, z_recv, n_send, n_recv, x_send, x_recv, c_send, c_recv,
    keys, key_ts, values, q_s, q_m, q_d, q_ts, wlow, *held,
):
    group, block, head = [lax.axis_index(name) for name in ("groups", "seq", "head")]
    chip, core = head // 2, head % 2
    channels, rows = feats.shape
    loads = [
        pltpu.make_async_copy(order_at, order.at[0], in_sem.at[0]),
        pltpu.make_async_copy(feats_at, feats, in_sem.at[1]),
        pltpu.make_async_copy(taps_at, taps, in_sem.at[2]),
        pltpu.make_async_copy(weight_at, weight, in_sem.at[3]),
        pltpu.make_async_copy(pairw_at, pairw, in_sem.at[4]),
    ]
    for load in loads:
        load.start()
    partner = chip * 2 + 1 - core

    def at_block(distance):
        return (group, lax.rem(block + distance + nblocks, nblocks), head)

    def at_head(where):
        return (group, block, where)

    def other(offset):
        return lax.rem(chip + offset, chips) * 2 + core

    halo[0] = jnp.zeros((channels, EDGE), jnp.bfloat16)
    halo[1] = jnp.zeros((channels, EDGE), jnp.bfloat16)
    barrier = pltpu.get_barrier_semaphore()
    steps = sorted({d % nblocks for d in (1, -1, 2, -2)} - {0})
    peers = [(group, lax.rem(block + d, nblocks), head) for d in steps]
    peers += [at_head(other(e)) for e in range(1, chips)] + [at_head(partner)]
    for peer in peers:
        pl.semaphore_signal(barrier, inc=1, device_id=peer, device_id_type=MESH)

    tally[...] = jnp.full((8, 128), count[0].astype(jnp.float32), jnp.float32)
    for load in loads:
        load.wait()

    def reorder(lo, width):
        position = lax.broadcasted_iota(jnp.int32, (rows, width), 0)
        chosen = jnp.where(position == order[:, lo : lo + width], 1.0, 0.0).astype(jnp.bfloat16)
        some = jnp.dot(feats[...], chosen, preferred_element_type=jnp.float32)
        wide[:, EDGE + lo : EDGE + lo + width] = some.astype(jnp.bfloat16)

    for lo in range(0, rows, 256):
        reorder(lo, 256)
    heads = weight.shape[0] // PROJ
    for h in range(heads):
        part = weight[...].astype(jnp.float32)[h * PROJ : (h + 1) * PROJ]
        project[h, 0:PROJ, :] = part
    middle = wide[:, EDGE : EDGE + rows].astype(jnp.float32)
    tap = jnp.concatenate([taps[...].astype(jnp.float32), jnp.zeros((1, channels), jnp.float32)], axis=0)
    tap = jnp.concatenate([tap, jnp.zeros((8, 128 - channels), jnp.float32)], axis=1)
    tap = jnp.transpose(tap)
    values[HD:, :] = ones_row(values.shape[1])
    pl.semaphore_wait(barrier, len(peers))

    def remote(source, target, send, recv, device):
        return pltpu.make_async_remote_copy(
            src_ref=source, dst_ref=target, send_sem=send, recv_sem=recv,
            device_id=device, device_id_type=MESH,
        )

    to_right = remote(wide.at[:, rows : rows + EDGE], halo.at[0], halo_send.at[0], halo_recv.at[0], at_block(1))
    to_left = remote(wide.at[:, EDGE : 2 * EDGE], halo.at[1], halo_send.at[1], halo_recv.at[1], at_block(-1))
    has_right, has_left = block < nblocks - 1, block > 0

    @pl.when(has_right)
    def _():
        to_right.start()

    @pl.when(has_left)
    def _():
        to_left.start()

    @pl.when(has_left)
    def _():
        to_right.wait_recv()

    @pl.when(has_right)
    def _():
        to_left.wait_recv()

    low = jnp.where(has_left, halo[0].astype(jnp.float32), 0.0)
    high = jnp.where(has_right, halo[1].astype(jnp.float32), 0.0)
    padded = jnp.concatenate([low, middle, high], axis=1)
    half = KSIZE // 2
    conv = jnp.zeros((channels, rows), jnp.float32)
    for offset in range(KSIZE):
        moved = pltpu.roll(padded, (half - offset) % padded.shape[1], 1)
        conv = conv + tap[:channels, offset : offset + 1] * moved[:, EDGE : EDGE + rows]
    gathered[0, head] = conv.astype(jnp.bfloat16)

    @pl.when(has_right)
    def _():
        to_right.wait_send()

    @pl.when(has_left)
    def _():
        to_left.wait_send()

    along = [
        remote(gathered.at[0, head], gathered.at[1, head], z_send.at[0], z_recv.at[0], at_block(-1)),
        remote(gathered.at[0, head], gathered.at[2, head], z_send.at[1], z_recv.at[1], at_block(1)),
        remote(gathered.at[1, head], gathered.at[3, head], z_send.at[2], z_recv.at[2], at_block(-1)),
    ]
    small = [
        remote(tally, counts.at[k + 1], n_send.at[k], n_recv.at[k], at_block(d))
        for k, d in enumerate(DISTANCES)
    ]
    here = pltpu.make_async_copy(tally, counts.at[0], in_sem.at[0])
    out = [pltpu.make_async_copy(gathered.at[k], kept.at[k], out_sem.at[k]) for k in range(len(along) + 1)]

    def spread(k):
        mine = gathered.at[k, head]
        for e in range(1, chips):
            remote(mine, mine, x_send.at[k, e - 1], x_recv.at[k, e - 1], at_head(other(e))).start()
        remote(mine, mine, c_send.at[k, 0], c_recv.at[k, 0], at_head(partner)).start()

    def pass_on(k):
        for e in range(1, chips):
            there = gathered.at[k, other(chips - e)]
            remote(there, there, x_send.at[k, e - 1], x_recv.at[k, e - 1], at_head(other(e))).wait_recv()
            remote(there, there, c_send.at[k, e], c_recv.at[k, e], at_head(partner)).start()

    def complete(k):
        for e in range(chips):
            there = gathered.at[k, lax.rem(chip - e + chips, chips) * 2 + 1 - core]
            remote(there, there, c_send.at[k, e], c_recv.at[k, e], at_head(partner)).wait_recv()
        out[k].start()

    def next_block(k):
        if k < len(along):
            along[k].wait_recv()
            spread(k + 1)
        if k + 1 < len(along):
            along[k].wait_send()
            along[k + 1].start()

    spread(0)
    along[0].start()
    pass_on(0)
    next_block(0)
    complete(0)
    for copy in small + [here]:
        copy.start()

    first = rows // 2
    dot = functools.partial(jnp.dot, preferred_element_type=jnp.float32)
    every_head = (q_s, q_m, q_d, q_ts)
    steps = heads * (len(along) + 1)

    def weights_of(h):
        return [pairw[h, i] for i in range(3)]

    def prepare(number):
        k, h = number // heads, lax.rem(number, heads)
        low = pl.multiple_of(lax.rem(number, 2) * first, first)
        weight_here = project[h].astype(jnp.bfloat16)
        some = gathered[k, :, :, 0:first].reshape(-1, first)
        block = dot(weight_here, some).astype(jnp.bfloat16).astype(jnp.float32)
        turned = build_keys(block, jnp.zeros((1, first), jnp.float32))
        keys[pl.ds(low, first), :] = turned
        key_ts[pl.ds(low, first), :] = dot(turned, ts_pick())
        values[0:HD, pl.ds(low, first)] = block[2 * HD : 3 * HD].astype(jnp.bfloat16)

        @pl.when(number < heads)
        def _():
            everywhere = gathered[0].reshape(-1, rows)
            block = dot(weight_here, everywhere).astype(jnp.bfloat16).astype(jnp.float32)
            queries = [ref.at[h] for ref in every_head]
            build_queries(block, *queries)
            best[h] = jnp.full((8, rows), masked_score, jnp.float32)
            probe(keys, key_ts, queries, weights_of(h), best.at[h], low, 1, piece)
            set_reference(best.at[h], q_s.at[h])
            total[h] = jnp.zeros((8, rows), jnp.float32)
            summed[h] = jnp.zeros((HD, rows), jnp.float32)

    def one_step(number, carry):
        for k in range(1, len(along) + 1):
            @pl.when(number == k * heads - 1)
            def _():
                pass_on(k)
                next_block(k)
                complete(k)

        @pl.when(number + 1 < steps)
        def _():
            prepare(number + 1)

        h, low = lax.rem(number, heads), lax.rem(number, 2) * first
        visit(
            keys, key_ts, values, every_head, h, weights_of(h), total.at[h], summed.at[h], wlow, held,
            low, first // chunk, first - low, lax.rem(number + 1, heads), chunk, piece,
        )
        return carry

    prepare(jnp.int32(0))
    fill_all(keys, [ref.at[0] for ref in every_head], held, 0, chunk, piece)
    lax.fori_loop(0, steps, one_step, 0)
    for copy in small + [here]:
        copy.wait()
    for copy in out:
        copy.wait()
    along[-1].wait_send()
    for k in range(len(along) + 1):
        for e in range(chips):
            there = gathered.at[k, other(chips - e) if e else head]
            if e:
                mine = gathered.at[k, head]
                remote(mine, mine, x_send.at[k, e - 1], x_recv.at[k, e - 1], at_head(other(e))).wait_send()
            remote(there, there, c_send.at[k, e], c_recv.at[k, e], at_head(partner)).wait_send()


def begin(feats, order, taps, weight, pairw, count, chunk=256, piece=256):
    channels, rows = feats.shape
    nblocks, places = lax.axis_size("seq"), lax.axis_size("head")
    heads = weight.shape[0] // PROJ
    chips = places // 2
    slots = len(DISTANCES) + 1
    held = rows // 2 * 2
    anywhere = pl.BlockSpec(memory_space=pltpu.HBM)
    vmem = pl.BlockSpec(memory_space=pltpu.VMEM)
    dma = pltpu.SemaphoreType.DMA
    return pl.pallas_call(
        functools.partial(begin_kernel, nblocks, chips, chunk, piece),
        in_specs=[anywhere] * 5 + [pl.BlockSpec(memory_space=pltpu.SMEM)],
        out_specs=[anywhere, anywhere, vmem, vmem, vmem],
        out_shape=[
            jax.ShapeDtypeStruct((slots, places, channels, rows), jnp.bfloat16),
            jax.ShapeDtypeStruct((slots, 8, 128), jnp.float32),
            *[jax.ShapeDtypeStruct((heads, size, rows), jnp.float32) for size in (8, 8, HD)],
        ],
        scratch_shapes=[
            pltpu.VMEM((channels, rows), jnp.bfloat16),
            pltpu.VMEM((1, rows), jnp.int32),
            pltpu.VMEM(taps.shape, taps.dtype),
            pltpu.VMEM(weight.shape, weight.dtype),
            pltpu.SMEM(pairw.shape, pairw.dtype),
            dma((5,)),
            dma((slots,)),
            pltpu.VMEM((8, 128), jnp.float32),
            pltpu.VMEM((channels, rows + 2 * EDGE), jnp.bfloat16),
            pltpu.VMEM((2, channels, EDGE), jnp.bfloat16),
            pltpu.VMEM((slots, places, channels, rows), jnp.bfloat16),
            pltpu.VMEM((heads, PROJ + 4, weight.shape[1]), jnp.float32),
            dma((2,)), dma((2,)),
            dma((slots - 1,)), dma((slots - 1,)),
            dma((slots - 1,)), dma((slots - 1,)),
            dma((slots, max(chips - 1, 1))), dma((slots, max(chips - 1, 1))),
            dma((slots, chips)), dma((slots, chips)),
            pltpu.VMEM((held, DEPTH), jnp.bfloat16),
            pltpu.VMEM((held, 128), jnp.float32),
            pltpu.VMEM((HD + 16, held), jnp.bfloat16),
            *[pltpu.VMEM((heads, DEPTH, rows), jnp.bfloat16)] * 3,
            pltpu.VMEM((heads, 8, rows), jnp.float32),
            pltpu.VMEM((chunk, rows), jnp.bfloat16),
            *[pltpu.VMEM((chunk, rows), jnp.float32)] * 3,
        ],
        compiler_params=pltpu.CompilerParams(
            collective_id=0, has_side_effects=True, vmem_limit_bytes=58 * 1024 * 1024
        ),
        name="begin",
    )(feats, order, taps, weight, pairw, count)


def finish_kernel(
    chunk, piece, held_rows,
    counts_at, pairw_at, weight_at, gathered_at, best_at, total_at, summed_at,
    out_ref,
    counts_ref, pairw, weight, gathered, best, total, summed, old, in_sem,
    keys, key_ts, values, q_s, q_m, q_d, q_ts, wlow, *held,
):
    nb, _, rows = gathered.shape
    heads = weight.shape[0] // PROJ
    dot = functools.partial(jnp.dot, preferred_element_type=jnp.float32)
    loads = [
        pltpu.make_async_copy(source, target, in_sem.at[k])
        for k, (source, target) in enumerate([
            (counts_at, counts_ref), (pairw_at, pairw), (weight_at, weight), (best_at, best),
            *[(gathered_at.at[i], gathered.at[i]) for i in range(nb)],
            (total_at, total), (summed_at, summed),
        ])
    ]
    for load in loads:
        load.start()
    values[HD:, :] = ones_row(values.shape[1])
    for load in loads:
        load.wait()
    counts = [jnp.max(counts_ref[i]).astype(jnp.int32) for i in range(nb)]
    every_head = (q_s, q_m, q_d, q_ts)

    def project(h):
        part = weight[0:PROJ, :]
        for other in range(1, heads):
            part = jnp.where(h == other, weight[other * PROJ : (other + 1) * PROJ, :], part)
        return part

    def weights_of(h):
        return [pairw[h, i] for i in range(3)]

    def place(v, at):
        width = v.shape[1]
        shift = at % 128
        base = pl.multiple_of(at - shift, 128)
        v = pltpu.roll(jnp.concatenate([v, jnp.zeros((HD, 128), jnp.float32)], axis=1), shift, 1)
        before = values[0:HD, pl.ds(base, 128)].astype(jnp.float32)
        lane = lax.broadcasted_iota(jnp.int32, (HD, 128), 1)
        joined = jnp.where(lane < shift, before, v[:, :128])
        values[0:HD, pl.ds(base, 128)] = joined.astype(jnp.bfloat16)
        values[0:HD, pl.ds(base + 128, width)] = v[:, 128:].astype(jnp.bfloat16)

    def lay_out(h, low):
        width = rows - low
        start = h * held_rows
        part = project(h)
        lanes = lax.broadcasted_iota(jnp.int32, (1, width), 1) + low
        for i in range(nb):
            block = dot(part, gathered[i, :, low:]).astype(jnp.bfloat16).astype(jnp.float32)
            turned = build_keys(block, jnp.where(lanes < counts[i], 0.0, masked_score))
            at = pl.multiple_of(start, GRAIN)
            keys[pl.ds(at, width), :] = turned
            key_ts[pl.ds(at, width), :] = dot(turned, ts_pick())
            place(block[2 * HD : 3 * HD], at)
            start = start + (counts[i] - low + GRAIN - 1) // GRAIN * GRAIN
        at = pl.multiple_of(start, GRAIN)
        keys[pl.ds(at, chunk), :] = no_keys(chunk)
        key_ts[pl.ds(at, chunk), :] = jnp.zeros((chunk, 128), jnp.float32)
        place(jnp.zeros((HD, chunk), jnp.float32), at)

    def attempt(number, go):
        reached = jnp.int32(0)
        for i in range(nb):
            left = counts[i] - jnp.where(number == 0, rows // 2, 0)
            reached = reached + (left + GRAIN - 1) // GRAIN * GRAIN
        chunks = (reached + chunk - 1) // chunk

        def prepare(h, carry):
            queries = [ref.at[h] for ref in every_head]

            @pl.when(number == 0)
            def _():
                block = dot(project(h), gathered[0]).astype(jnp.bfloat16).astype(jnp.float32)
                build_queries(block, *queries)
                lay_out(h, rows // 2)

            @pl.when(number == 1)
            def _():
                lay_out(h, 0)
                none = jnp.zeros((8, rows), jnp.float32)
                best[h] = none + masked_score
                set_reference(old, q_s.at[h])
                probes = (reached + PROBE - 1) // PROBE
                probe(keys, key_ts, queries, weights_of(h), best.at[h], h * held_rows, probes, piece)
                total[h] = none
                summed[h] = jnp.zeros((HD, rows), jnp.float32)

            set_reference(best.at[h], q_s.at[h])
            return carry

        def one_head(h, carry):
            after = lax.rem(h + 1, heads)
            visit(
                keys, key_ts, values, every_head, h, weights_of(h), total.at[h], summed.at[h], wlow, held,
                h * held_rows, chunks, after * held_rows, after, chunk, piece,
            )
            return carry

        @pl.when(go == 1)
        def _():
            lax.fori_loop(0, heads, prepare, 0)
            fill_all(keys, [ref.at[0] for ref in every_head], held, 0, chunk, piece)
            lax.fori_loop(0, heads, one_head, 0)

        return jnp.logical_not(jnp.max(total[...]) < LIMIT).astype(jnp.int32)

    old[...] = jnp.zeros((8, rows), jnp.float32)
    lax.fori_loop(0, 2, attempt, jnp.int32(1))
    for h in range(heads):
        out_ref[h * HD : (h + 1) * HD, :] = (summed[h] / total[h, 0:1, :]).astype(jnp.bfloat16)


def finish(counts, pairw, weight, gathered, state, chunk=256, piece=256):
    heads = weight.shape[0] // PROJ
    nb, _, rows = gathered.shape
    held = nb * rows + 2 * chunk
    pairs = heads * rows * nb * rows
    operands = [counts, pairw, weight, gathered, *state]
    scratch = [pltpu.VMEM(one.shape, one.dtype) for one in operands]
    scratch[1] = pltpu.SMEM(pairw.shape, pairw.dtype)
    return pl.pallas_call(
        functools.partial(finish_kernel, chunk, piece, held),
        in_specs=[pl.BlockSpec(memory_space=pltpu.HBM)] * len(operands),
        out_specs=pl.BlockSpec(memory_space=pltpu.VMEM),
        out_shape=jax.ShapeDtypeStruct((heads * HD, rows), jnp.bfloat16),
        scratch_shapes=[
            *scratch,
            pltpu.VMEM((8, rows), jnp.float32),
            pltpu.SemaphoreType.DMA((len(operands) - 1 + nb,)),
            pltpu.VMEM((heads * held, DEPTH), jnp.bfloat16),
            pltpu.VMEM((heads * held, 128), jnp.float32),
            pltpu.VMEM((HD + 16, heads * held), jnp.bfloat16),
            *[pltpu.VMEM((heads, DEPTH, rows), jnp.bfloat16)] * 3,
            pltpu.VMEM((heads, 8, rows), jnp.float32),
            pltpu.VMEM((chunk, rows), jnp.bfloat16),
            *[pltpu.VMEM((chunk, rows), jnp.float32)] * 3,
        ],
        compiler_params=pltpu.CompilerParams(vmem_limit_bytes=58 * 1024 * 1024),
        cost_estimate=pl.CostEstimate(
            flops=pairs * 2 * DEPTH * 4, bytes_accessed=1 << 20, transcendentals=4 * pairs
        ),
        name="finish",
    )(*operands)


def shards(hit_features, depth_kernel, point_weight, pair_weight, hit_order, valid_counts):
    rows = hit_features.shape[1]
    gathered, counts, *state = begin(
        hit_features, hit_order, depth_kernel, point_weight, pair_weight, valid_counts
    )
    gathered = gathered.reshape(gathered.shape[0], point_weight.shape[1], rows)
    return finish(counts, pair_weight, point_weight, gathered, state)


def solution(mesh):
    in_specs = (
        P("head", ("groups", "seq")),
        P(None, "head"),
        P("head", None),
        P("head", None),
        P(("groups", "seq")),
        P(("groups", "seq")),
    )
    out_specs = P("head", ("groups", "seq"))
    return jax.shard_map(shards, mesh=mesh, in_specs=in_specs, out_specs=out_specs, check_vma=False)
```

```python
import functools

import jax
import jax.numpy as jnp
from jax import lax
from jax.experimental import pallas as pl
from jax.experimental.pallas import tpu as pltpu
from jax.sharding import PartitionSpec as P

HD = 32
KSIZE = 7
PROJ = 100

floor_pt = 0.1
mass_offset = 0.1
masked_score = -1e30
LOG2E = 1.4426950408889634

DEPTH = 128
GROUPS = 2 * HD
ROW_TOP = 112
ROW_MASK = 123
PARTS = ((0, 0), (0, 1), (1, 0), (1, 1), (0, 2), (2, 0))
ONCE = (0, 2, 5)

GRAIN = 16
PROBE = 64
LIMIT = 2.0**100


def split3(x):
    high = x.astype(jnp.bfloat16).astype(jnp.float32)
    rest = x - high
    mid = rest.astype(jnp.bfloat16).astype(jnp.float32)
    low = (rest - mid).astype(jnp.bfloat16).astype(jnp.float32)
    return high, mid, low


def kinematics(a0, along_x, along_y, along_z):
    softplus = jnp.maximum(a0, 0.0) + jnp.log1p(jnp.exp(-jnp.abs(a0)))
    hit_mass = mass_offset + softplus
    mass_sq = hit_mass * hit_mass
    trans_sq = along_x * along_x + along_y * along_y
    energy = jnp.sqrt(mass_sq + trans_sq + along_z * along_z)
    trans_mass = jnp.sqrt(mass_sq + trans_sq)
    magnitude = jnp.log((jnp.abs(along_z) + energy) / trans_mass)
    rapidity = jnp.where(along_z < 0.0, -magnitude, magnitude)
    inverse_pt = 1.0 / jnp.maximum(jnp.sqrt(trans_sq), floor_pt)
    return energy, mass_sq, rapidity, along_x * inverse_pt, along_y * inverse_pt, trans_sq


def ones_row(width):
    at_row = lax.broadcasted_iota(jnp.int32, (16, width), 0)
    return jnp.where(at_row == 0, 1.0, 0.0).astype(jnp.bfloat16)


def ts_pick():
    at_row = lax.broadcasted_iota(jnp.int32, (DEPTH, 128), 0)
    pick = at_row == GROUPS + 6
    for number in ONCE[1:]:
        pick = pick | (at_row == GROUPS + 8 * number + 6)
    return jnp.where(pick, 1.0, 0.0).astype(jnp.bfloat16)


def vector_of(block):
    raw = block[3 * HD : 3 * HD + 4]
    return [raw[i : i + 1] for i in range(4)]


def quantities(block):
    vector = vector_of(block)
    energy, mass_sq, rapidity, unit_x, unit_y, trans_sq = kinematics(*vector)
    none = jnp.zeros_like(energy)
    stacked = [energy, rapidity, unit_x, unit_y, mass_sq, rapidity * rapidity, trans_sq, none]
    return split3(jnp.concatenate(stacked, axis=0)), vector[1:], trans_sq


def build_queries(block, q_s, q_m, q_d, q_ts):
    rows = block.shape[1]
    parts, momentum, trans_sq = quantities(block)
    q_ts[...] = jnp.broadcast_to(trans_sq, (8, rows))
    scaled = block[0:HD] * (LOG2E * HD**-0.5)
    high = scaled.astype(jnp.bfloat16).astype(jnp.float32)
    at_row = lax.broadcasted_iota(jnp.int32, (8, rows), 0)
    zero = jnp.zeros((8, rows), jnp.float32)
    for_m, for_d = [zero] * (GROUPS // 8), [zero] * (GROUPS // 8)
    for number, (_, b) in enumerate(PARTS):
        once = 1.0 if number in ONCE else 0.0
        for_m.append(jnp.where(at_row == 0, 2.0 * parts[b], jnp.where(at_row == 4, once, 0.0)))
        twice = jnp.where((at_row >= 1) & (at_row <= 3), -2.0 * parts[b], 0.0)
        for_d.append(jnp.where(at_row == 5, once, twice))
    none = jnp.zeros((1, rows), jnp.float32)
    for_m.append(jnp.concatenate([part[4:5] for part in parts] + [none] * 5, axis=0))
    squares = [part[5:6] for part in parts]
    for_d.append(jnp.concatenate([none] * 3 + squares + [none + 2.0, none], axis=0))
    for_m.append(jnp.concatenate([-2.0 * value for value in momentum] + [none] * 5, axis=0))
    for_d.append(zero)
    for_s = [high, scaled - high] + [zero] * 7 + [jnp.where(at_row == ROW_MASK % 8, 1.0, 0.0)]
    for ref, groups in ((q_s, for_s), (q_m, for_m), (q_d, for_d)):
        ref[...] = jnp.concatenate(groups, axis=0).astype(jnp.bfloat16)


def build_keys(block, mask):
    width = block.shape[1]
    parts, momentum, _ = quantities(block)
    key = block[HD : 2 * HD]
    one = jnp.ones((8, width), jnp.float32)
    none = jnp.zeros((4, width), jnp.float32)
    groups = [key, key] + [parts[a] for a, _ in PARTS]
    groups += [one, jnp.concatenate([*momentum, mask, none], axis=0)]
    return jnp.transpose(jnp.concatenate(groups, axis=0).astype(jnp.bfloat16))


def no_keys(count):
    lane = lax.broadcasted_iota(jnp.int32, (count, DEPTH), 1)
    empty = jnp.where(lane == ROW_MASK, masked_score, jnp.where(lane == GROUPS + 4, 1.0, 0.0))
    return empty.astype(jnp.bfloat16)


def products(keys, queries, at, count, cols):
    lhs = keys[pl.ds(at, count), :]
    return [
        jnp.dot(lhs, q[:, cols], preferred_element_type=jnp.float32)
        for q in (queries[2], queries[1], queries[0])
    ]


def combine(key_ts, queries, w, three, at, count, cols):
    separation, invariant, score = three
    ts_key = jnp.concatenate([key_ts[pl.ds(at, count), :]] * (score.shape[1] // 128), axis=1)
    ts_query = jnp.concatenate([queries[3][:, cols]] * (count // 8), axis=0)
    kt_sq = jnp.minimum(ts_key, ts_query) * separation
    score = score + w[0] * lax.log2(invariant)
    return score + w[1] * lax.log2(1.0 + kt_sq) + w[2] * lax.log2(1.0 + separation)


def probe(keys, key_ts, queries, w, best, start, count, piece):
    rows = best.shape[1]

    def one(index, carry):
        at = pl.multiple_of(start + index * PROBE, PROBE)
        for lo in range(0, rows, piece):
            cols = pl.ds(lo, piece)
            three = products(keys, queries, at, PROBE, cols)
            score = combine(key_ts, queries, w, three, at, PROBE, cols)
            top = jnp.max(score.reshape(PROBE // 8, 8, piece), axis=0)
            best[:, cols] = jnp.maximum(best[:, cols], top)
        return carry

    lax.fori_loop(0, count, one, 0)
    best[...] = jnp.broadcast_to(jnp.max(best[...], axis=0, keepdims=True), best.shape)


def set_reference(best, q_s):
    rows = best.shape[1]
    none = jnp.zeros((1, rows), jnp.float32)
    block = [*split3(-best[0:1, :]), *[none] * 5, *[none] * 3, none + 1.0, *[none] * 4]
    q_s[ROW_TOP:, :] = jnp.concatenate(block, axis=0).astype(jnp.bfloat16)


def fill(keys, queries, held, at, lo, chunk, piece):
    cols = pl.ds(lo, piece)
    for ref, value in zip(held, products(keys, queries, at, chunk, cols)):
        ref[:, cols] = value


def fill_all(keys, queries, held, at, chunk, piece):
    for lo in range(0, held[0].shape[1], piece):
        fill(keys, queries, held, at, lo, chunk, piece)


def visit(
    keys, key_ts, values, every_head, here, w, total, summed, wlow, held,
    start, chunks, next_start, next_here, chunk, piece, tail=None,
):
    rows = total.shape[1]
    queries = [ref.at[here] for ref in every_head]

    def collect(at, lo):
        cols = pl.ds(lo, piece)
        both = jnp.dot(values[:, pl.ds(at, chunk)], wlow[:, cols], preferred_element_type=jnp.float32)
        summed[:, cols] += both[:HD]
        total[:, cols] += both[HD : HD + 8]

    def one_chunk(index, carry):
        at = pl.multiple_of(start + index * chunk, chunk)
        waiting = (pl.multiple_of(start + jnp.maximum(index - 1, 0) * chunk, chunk), rows - piece)
        is_last = index == chunks - 1
        if tail is not None:
            is_last = is_last & jnp.logical_not(tail)
        following = pl.multiple_of(jnp.where(is_last, next_start, at + chunk), chunk)
        next_queries = [ref.at[jnp.where(is_last, next_here, here)] for ref in every_head]
        for lo in range(0, rows, piece):
            cols = pl.ds(lo, piece)
            score = combine(key_ts, queries, w, [ref[:, cols] for ref in held], at, chunk, cols)
            wlow[:, cols] = jnp.exp2(score).astype(jnp.bfloat16)
            fill(keys, next_queries, held, following, lo, chunk, piece)
            collect(*waiting)
            waiting = (at, lo)
        return carry

    wlow[:, rows - piece :] = jnp.zeros((chunk, piece), jnp.bfloat16)
    lax.fori_loop(0, chunks, one_chunk, 0)
    collect(pl.multiple_of(start + jnp.maximum(chunks - 1, 0) * chunk, chunk), rows - piece)
    if tail is None:
        return

    @pl.when(tail)
    def _():
        few = chunk // 2
        at = pl.multiple_of(start + chunks * chunk, chunk)
        next_queries = [ref.at[next_here] for ref in every_head]
        for lo in range(0, rows, piece):
            cols = pl.ds(lo, piece)
            some = [ref[0:few, cols] for ref in held]
            weights = jnp.exp2(combine(key_ts, queries, w, some, at, few, cols)).astype(jnp.bfloat16)
            fill(keys, next_queries, held, pl.multiple_of(next_start, chunk), lo, chunk, piece)
            both = jnp.dot(values[:, pl.ds(at, few)], weights, preferred_element_type=jnp.float32)
            summed[:, cols] += both[:HD]
            total[:, cols] += both[HD : HD + 8]


MESH = pl.DeviceIdType.MESH
DISTANCES = (-1, 1, -2)
EDGE = 128


def begin_kernel(
    nblocks, chips, chunk, piece,
    feats_at, order_at, taps_at, weight_at, pairw_at, count,
    kept, counts, best, total, summed,
    feats, order, taps, weight, pairw, in_sem, out_sem, tally, wide, halo, gathered, project,
    halo_send, halo_recv, z_send, z_recv, n_send, n_recv, x_send, x_recv, c_send, c_recv,
    keys, key_ts, values, q_s, q_m, q_d, q_ts, wlow, *held,
):
    group, block, head = [lax.axis_index(name) for name in ("groups", "seq", "head")]
    chip, core = head // 2, head % 2
    channels, rows = feats.shape
    loads = [
        pltpu.make_async_copy(order_at, order.at[0], in_sem.at[0]),
        pltpu.make_async_copy(feats_at, feats, in_sem.at[1]),
        pltpu.make_async_copy(taps_at, taps, in_sem.at[2]),
        pltpu.make_async_copy(weight_at, weight, in_sem.at[3]),
        pltpu.make_async_copy(pairw_at, pairw, in_sem.at[4]),
    ]
    for load in loads:
        load.start()
    partner = chip * 2 + 1 - core

    def at_block(distance):
        return (group, lax.rem(block + distance + nblocks, nblocks), head)

    def at_head(where):
        return (group, block, where)

    def other(offset):
        return lax.rem(chip + offset, chips) * 2 + core

    halo[0] = jnp.zeros((channels, EDGE), jnp.bfloat16)
    halo[1] = jnp.zeros((channels, EDGE), jnp.bfloat16)
    barrier = pltpu.get_barrier_semaphore()
    steps = sorted({d % nblocks for d in (1, -1, 2, -2)} - {0})
    peers = [(group, lax.rem(block + d, nblocks), head) for d in steps]
    peers += [at_head(other(e)) for e in range(1, chips)] + [at_head(partner)]
    for peer in peers:
        pl.semaphore_signal(barrier, inc=1, device_id=peer, device_id_type=MESH)

    tally[...] = jnp.full((8, 128), count[0].astype(jnp.float32), jnp.float32)
    for load in loads:
        load.wait()

    def reorder(lo, width):
        position = lax.broadcasted_iota(jnp.int32, (rows, width), 0)
        chosen = jnp.where(position == order[:, lo : lo + width], 1.0, 0.0).astype(jnp.bfloat16)
        some = jnp.dot(feats[...], chosen, preferred_element_type=jnp.float32)
        wide[:, EDGE + lo : EDGE + lo + width] = some.astype(jnp.bfloat16)

    for lo in range(0, rows, 256):
        reorder(lo, 256)
    heads = weight.shape[0] // PROJ
    for h in range(heads):
        part = weight[...].astype(jnp.float32)[h * PROJ : (h + 1) * PROJ]
        project[h, 0:PROJ, :] = part
    middle = wide[:, EDGE : EDGE + rows].astype(jnp.float32)
    tap = jnp.concatenate([taps[...].astype(jnp.float32), jnp.zeros((1, channels), jnp.float32)], axis=0)
    tap = jnp.concatenate([tap, jnp.zeros((8, 128 - channels), jnp.float32)], axis=1)
    tap = jnp.transpose(tap)
    values[HD:, :] = ones_row(values.shape[1])

    def smooth(padded):
        half, width = KSIZE // 2, padded.shape[1]
        conv = jnp.zeros((channels, width - 2 * EDGE), jnp.float32)
        for offset in range(KSIZE):
            moved = pltpu.roll(padded, (half - offset) % width, 1)
            conv = conv + tap[:channels, offset : offset + 1] * moved[:, EDGE : width - EDGE]
        return conv.astype(jnp.bfloat16)

    pl.semaphore_wait(barrier, len(peers))

    def remote(source, target, send, recv, device):
        return pltpu.make_async_remote_copy(
            src_ref=source, dst_ref=target, send_sem=send, recv_sem=recv,
            device_id=device, device_id_type=MESH,
        )

    to_right = remote(wide.at[:, rows : rows + EDGE], halo.at[0], halo_send.at[0], halo_recv.at[0], at_block(1))
    to_left = remote(wide.at[:, EDGE : 2 * EDGE], halo.at[1], halo_send.at[1], halo_recv.at[1], at_block(-1))
    has_right, has_left = block < nblocks - 1, block > 0

    @pl.when(has_right)
    def _():
        to_right.start()

    @pl.when(has_left)
    def _():
        to_left.start()

    gathered[0, head, :, EDGE : rows - EDGE] = smooth(middle)

    along = [
        remote(gathered.at[0, head], gathered.at[1, head], z_send.at[0], z_recv.at[0], at_block(-1)),
        remote(gathered.at[0, head], gathered.at[2, head], z_send.at[1], z_recv.at[1], at_block(1)),
        remote(gathered.at[1, head], gathered.at[3, head], z_send.at[2], z_recv.at[2], at_block(-1)),
    ]
    small = [
        remote(tally, counts.at[k + 1], n_send.at[k], n_recv.at[k], at_block(d))
        for k, d in enumerate(DISTANCES)
    ]
    here = pltpu.make_async_copy(tally, counts.at[0], in_sem.at[0])
    out = [pltpu.make_async_copy(gathered.at[k], kept.at[k], out_sem.at[k]) for k in range(len(along) + 1)]

    slots = len(along) + 1
    pieces = [(0, EDGE, rows - EDGE)] + [(k, 0, rows) for k in range(1, slots)]
    pieces += [(0, 0, EDGE), (0, rows - EDGE, rows)]

    def over_chips(u, e):
        k, lo, hi = pieces[u]
        mine = gathered.at[k, head, :, lo:hi]
        return remote(mine, mine, x_send.at[u, e - 1], x_recv.at[u, e - 1], at_head(other(e)))

    def to_partner(u, e):
        k, lo, hi = pieces[u]
        there = gathered.at[k, other(chips - e) if e else head, :, lo:hi]
        return remote(there, there, c_send.at[u, e], c_recv.at[u, e], at_head(partner))

    def from_partner(u, e):
        k, lo, hi = pieces[u]
        there = gathered.at[k, lax.rem(chip - e + chips, chips) * 2 + 1 - core, :, lo:hi]
        return remote(there, there, c_send.at[u, e], c_recv.at[u, e], at_head(partner))

    def from_chips(u, e):
        k, lo, hi = pieces[u]
        there = gathered.at[k, other(chips - e), :, lo:hi]
        return remote(there, there, x_send.at[u, e - 1], x_recv.at[u, e - 1], at_head(other(e)))

    def spread(u):
        for e in range(1, chips):
            over_chips(u, e).start()
        to_partner(u, 0).start()

    def pass_on(u):
        for e in range(1, chips):
            from_chips(u, e).wait_recv()
            to_partner(u, e).start()

    def arrive(u):
        for e in range(chips):
            from_partner(u, e).wait_recv()

    def complete(k):
        arrive(k)
        out[k].start()

    def next_block(k):
        if k < len(along):
            along[k].wait_recv()
            spread(k + 1)
        if k + 1 < len(along):
            along[k].wait_send()
            along[k + 1].start()

    spread(0)
    @pl.when(has_left)
    def _():
        to_right.wait_recv()

    @pl.when(has_right)
    def _():
        to_left.wait_recv()

    low = jnp.where(has_left, halo[0].astype(jnp.float32), 0.0)
    high = jnp.where(has_right, halo[1].astype(jnp.float32), 0.0)
    gathered[0, head, :, 0:EDGE] = smooth(jnp.concatenate([low, middle[:, : 2 * EDGE]], axis=1))
    gathered[0, head, :, rows - EDGE :] = smooth(jnp.concatenate([middle[:, rows - 2 * EDGE :], high], axis=1))

    @pl.when(has_right)
    def _():
        to_right.wait_send()

    @pl.when(has_left)
    def _():
        to_left.wait_send()

    for u in (slots, slots + 1):
        spread(u)
    along[0].start()
    for u in (0, slots, slots + 1):
        pass_on(u)
    next_block(0)
    for u in (slots, slots + 1):
        arrive(u)
    complete(0)
    for copy in small + [here]:
        copy.start()

    first = rows // 2
    dot = functools.partial(jnp.dot, preferred_element_type=jnp.float32)
    every_head = (q_s, q_m, q_d, q_ts)
    steps = heads * (len(along) + 1)

    def weights_of(h):
        return [pairw[h, i] for i in range(3)]

    def prepare(number):
        k, h = number // heads, lax.rem(number, heads)
        low = pl.multiple_of(lax.rem(number, 2) * first, first)
        weight_here = project[h].astype(jnp.bfloat16)
        some = gathered[k, :, :, 0:first].reshape(-1, first)
        block = dot(weight_here, some).astype(jnp.bfloat16).astype(jnp.float32)
        turned = build_keys(block, jnp.zeros((1, first), jnp.float32))
        keys[pl.ds(low, first), :] = turned
        key_ts[pl.ds(low, first), :] = dot(turned, ts_pick())
        values[0:HD, pl.ds(low, first)] = block[2 * HD : 3 * HD].astype(jnp.bfloat16)

        @pl.when(number < heads)
        def _():
            everywhere = gathered[0].reshape(-1, rows)
            block = dot(weight_here, everywhere).astype(jnp.bfloat16).astype(jnp.float32)
            queries = [ref.at[h] for ref in every_head]
            build_queries(block, *queries)
            best[h] = jnp.full((8, rows), masked_score, jnp.float32)
            probe(keys, key_ts, queries, weights_of(h), best.at[h], low, 1, piece)
            set_reference(best.at[h], q_s.at[h])
            total[h] = jnp.zeros((8, rows), jnp.float32)
            summed[h] = jnp.zeros((HD, rows), jnp.float32)

    def one_step(number, carry):
        for k in range(1, len(along) + 1):
            @pl.when(number == k * heads - 1)
            def _():
                pass_on(k)
                next_block(k)
                complete(k)

        @pl.when(number + 1 < steps)
        def _():
            prepare(number + 1)

        h, low = lax.rem(number, heads), lax.rem(number, 2) * first
        visit(
            keys, key_ts, values, every_head, h, weights_of(h), total.at[h], summed.at[h], wlow, held,
            low, first // chunk, first - low, lax.rem(number + 1, heads), chunk, piece,
        )
        return carry

    prepare(jnp.int32(0))
    fill_all(keys, [ref.at[0] for ref in every_head], held, 0, chunk, piece)
    lax.fori_loop(0, steps, one_step, 0)
    for copy in small + [here]:
        copy.wait()
    for copy in out:
        copy.wait()
    along[-1].wait_send()
    for u in range(len(pieces)):
        for e in range(chips):
            if e:
                over_chips(u, e).wait_send()
            to_partner(u, e).wait_send()


def begin(feats, order, taps, weight, pairw, count, chunk=256, piece=256):
    channels, rows = feats.shape
    nblocks, places = lax.axis_size("seq"), lax.axis_size("head")
    heads = weight.shape[0] // PROJ
    chips = places // 2
    slots = len(DISTANCES) + 1
    held = rows // 2 * 2
    anywhere = pl.BlockSpec(memory_space=pltpu.HBM)
    vmem = pl.BlockSpec(memory_space=pltpu.VMEM)
    dma = pltpu.SemaphoreType.DMA
    return pl.pallas_call(
        functools.partial(begin_kernel, nblocks, chips, chunk, piece),
        in_specs=[anywhere] * 5 + [pl.BlockSpec(memory_space=pltpu.SMEM)],
        out_specs=[anywhere, anywhere, vmem, vmem, vmem],
        out_shape=[
            jax.ShapeDtypeStruct((slots, places, channels, rows), jnp.bfloat16),
            jax.ShapeDtypeStruct((slots, 8, 128), jnp.float32),
            *[jax.ShapeDtypeStruct((heads, size, rows), jnp.float32) for size in (8, 8, HD)],
        ],
        scratch_shapes=[
            pltpu.VMEM((channels, rows), jnp.bfloat16),
            pltpu.VMEM((1, rows), jnp.int32),
            pltpu.VMEM(taps.shape, taps.dtype),
            pltpu.VMEM(weight.shape, weight.dtype),
            pltpu.SMEM(pairw.shape, pairw.dtype),
            dma((5,)),
            dma((slots,)),
            pltpu.VMEM((8, 128), jnp.float32),
            pltpu.VMEM((channels, rows + 2 * EDGE), jnp.bfloat16),
            pltpu.VMEM((2, channels, EDGE), jnp.bfloat16),
            pltpu.VMEM((slots, places, channels, rows), jnp.bfloat16),
            pltpu.VMEM((heads, PROJ + 4, weight.shape[1]), jnp.float32),
            dma((2,)), dma((2,)),
            dma((slots - 1,)), dma((slots - 1,)),
            dma((slots - 1,)), dma((slots - 1,)),
            dma((slots + 2, max(chips - 1, 1))), dma((slots + 2, max(chips - 1, 1))),
            dma((slots + 2, chips)), dma((slots + 2, chips)),
            pltpu.VMEM((held, DEPTH), jnp.bfloat16),
            pltpu.VMEM((held, 128), jnp.float32),
            pltpu.VMEM((HD + 16, held), jnp.bfloat16),
            *[pltpu.VMEM((heads, DEPTH, rows), jnp.bfloat16)] * 3,
            pltpu.VMEM((heads, 8, rows), jnp.float32),
            pltpu.VMEM((chunk, rows), jnp.bfloat16),
            *[pltpu.VMEM((chunk, rows), jnp.float32)] * 3,
        ],
        compiler_params=pltpu.CompilerParams(
            collective_id=0, has_side_effects=True, vmem_limit_bytes=58 * 1024 * 1024
        ),
        name="begin",
    )(feats, order, taps, weight, pairw, count)


def finish_kernel(
    chunk, piece, held_rows,
    counts_at, pairw_at, weight_at, gathered_at, best_at, total_at, summed_at,
    out_ref,
    counts_ref, pairw, weight, gathered, best, total, summed, old, in_sem,
    keys, key_ts, values, q_s, q_m, q_d, q_ts, wlow, *held,
):
    nb, _, rows = gathered.shape
    heads = weight.shape[0] // PROJ
    dot = functools.partial(jnp.dot, preferred_element_type=jnp.float32)
    loads = [
        pltpu.make_async_copy(source, target, in_sem.at[k])
        for k, (source, target) in enumerate([
            (counts_at, counts_ref), (pairw_at, pairw), (weight_at, weight), (best_at, best),
            *[(gathered_at.at[i], gathered.at[i]) for i in range(nb)],
            (total_at, total), (summed_at, summed),
        ])
    ]
    for load in loads:
        load.start()
    values[HD:, :] = ones_row(values.shape[1])
    for load in loads:
        load.wait()
    counts = [jnp.max(counts_ref[i]).astype(jnp.int32) for i in range(nb)]
    every_head = (q_s, q_m, q_d, q_ts)

    def project(h):
        part = weight[0:PROJ, :]
        for other in range(1, heads):
            part = jnp.where(h == other, weight[other * PROJ : (other + 1) * PROJ, :], part)
        return part

    def weights_of(h):
        return [pairw[h, i] for i in range(3)]

    def place(v, at):
        width = v.shape[1]
        shift = at % 128
        base = pl.multiple_of(at - shift, 128)
        v = pltpu.roll(jnp.concatenate([v, jnp.zeros((HD, 128), jnp.float32)], axis=1), shift, 1)
        before = values[0:HD, pl.ds(base, 128)].astype(jnp.float32)
        lane = lax.broadcasted_iota(jnp.int32, (HD, 128), 1)
        joined = jnp.where(lane < shift, before, v[:, :128])
        values[0:HD, pl.ds(base, 128)] = joined.astype(jnp.bfloat16)
        values[0:HD, pl.ds(base + 128, width)] = v[:, 128:].astype(jnp.bfloat16)

    def lay_out(h, low):
        width = rows - low
        start = h * held_rows
        part = project(h)
        lanes = lax.broadcasted_iota(jnp.int32, (1, width), 1) + low
        for i in range(nb):
            block = dot(part, gathered[i, :, low:]).astype(jnp.bfloat16).astype(jnp.float32)
            turned = build_keys(block, jnp.where(lanes < counts[i], 0.0, masked_score))
            at = pl.multiple_of(start, GRAIN)
            keys[pl.ds(at, width), :] = turned
            key_ts[pl.ds(at, width), :] = dot(turned, ts_pick())
            place(block[2 * HD : 3 * HD], at)
            start = start + (counts[i] - low + GRAIN - 1) // GRAIN * GRAIN
        at = pl.multiple_of(start, GRAIN)
        keys[pl.ds(at, chunk), :] = no_keys(chunk)
        key_ts[pl.ds(at, chunk), :] = jnp.zeros((chunk, 128), jnp.float32)
        place(jnp.zeros((HD, chunk), jnp.float32), at)

    def attempt(number, go):
        reached = jnp.int32(0)
        for i in range(nb):
            left = counts[i] - jnp.where(number == 0, rows // 2, 0)
            reached = reached + (left + GRAIN - 1) // GRAIN * GRAIN
        chunks = (reached + chunk // 2 - 1) // chunk
        tail = reached > chunks * chunk

        def prepare(h, carry):
            queries = [ref.at[h] for ref in every_head]

            @pl.when(number == 0)
            def _():
                block = dot(project(h), gathered[0]).astype(jnp.bfloat16).astype(jnp.float32)
                build_queries(block, *queries)
                lay_out(h, rows // 2)

            @pl.when(number == 1)
            def _():
                lay_out(h, 0)
                none = jnp.zeros((8, rows), jnp.float32)
                best[h] = none + masked_score
                set_reference(old, q_s.at[h])
                probes = (reached + PROBE - 1) // PROBE
                probe(keys, key_ts, queries, weights_of(h), best.at[h], h * held_rows, probes, piece)
                total[h] = none
                summed[h] = jnp.zeros((HD, rows), jnp.float32)

            set_reference(best.at[h], q_s.at[h])
            return carry

        def one_head(h, carry):
            after = lax.rem(h + 1, heads)
            visit(
                keys, key_ts, values, every_head, h, weights_of(h), total.at[h], summed.at[h], wlow, held,
                h * held_rows, chunks, after * held_rows, after, chunk, piece, tail,
            )
            return carry

        @pl.when(go == 1)
        def _():
            lax.fori_loop(0, heads, prepare, 0)
            fill_all(keys, [ref.at[0] for ref in every_head], held, 0, chunk, piece)
            lax.fori_loop(0, heads, one_head, 0)

        return jnp.logical_not(jnp.max(total[...]) < LIMIT).astype(jnp.int32)

    old[...] = jnp.zeros((8, rows), jnp.float32)
    lax.fori_loop(0, 2, attempt, jnp.int32(1))
    for h in range(heads):
        out_ref[h * HD : (h + 1) * HD, :] = (summed[h] / total[h, 0:1, :]).astype(jnp.bfloat16)


def finish(counts, pairw, weight, gathered, state, chunk=256, piece=256):
    heads = weight.shape[0] // PROJ
    nb, _, rows = gathered.shape
    held = nb * rows + 2 * chunk
    pairs = heads * rows * nb * rows
    operands = [counts, pairw, weight, gathered, *state]
    scratch = [pltpu.VMEM(one.shape, one.dtype) for one in operands]
    scratch[1] = pltpu.SMEM(pairw.shape, pairw.dtype)
    return pl.pallas_call(
        functools.partial(finish_kernel, chunk, piece, held),
        in_specs=[pl.BlockSpec(memory_space=pltpu.HBM)] * len(operands),
        out_specs=pl.BlockSpec(memory_space=pltpu.VMEM),
        out_shape=jax.ShapeDtypeStruct((heads * HD, rows), jnp.bfloat16),
        scratch_shapes=[
            *scratch,
            pltpu.VMEM((8, rows), jnp.float32),
            pltpu.SemaphoreType.DMA((len(operands) - 1 + nb,)),
            pltpu.VMEM((heads * held, DEPTH), jnp.bfloat16),
            pltpu.VMEM((heads * held, 128), jnp.float32),
            pltpu.VMEM((HD + 16, heads * held), jnp.bfloat16),
            *[pltpu.VMEM((heads, DEPTH, rows), jnp.bfloat16)] * 3,
            pltpu.VMEM((heads, 8, rows), jnp.float32),
            pltpu.VMEM((chunk, rows), jnp.bfloat16),
            *[pltpu.VMEM((chunk, rows), jnp.float32)] * 3,
        ],
        compiler_params=pltpu.CompilerParams(vmem_limit_bytes=58 * 1024 * 1024),
        cost_estimate=pl.CostEstimate(
            flops=pairs * 2 * DEPTH * 4, bytes_accessed=1 << 20, transcendentals=4 * pairs
        ),
        name="finish",
    )(*operands)


def shards(hit_features, depth_kernel, point_weight, pair_weight, hit_order, valid_counts):
    rows = hit_features.shape[1]
    gathered, counts, *state = begin(
        hit_features, hit_order, depth_kernel, point_weight, pair_weight, valid_counts
    )
    gathered = gathered.reshape(gathered.shape[0], point_weight.shape[1], rows)
    return finish(counts, pair_weight, point_weight, gathered, state)


def solution(mesh):
    in_specs = (
        P("head", ("groups", "seq")),
        P(None, "head"),
        P("head", None),
        P("head", None),
        P(("groups", "seq")),
        P(("groups", "seq")),
    )
    out_specs = P("head", ("groups", "seq"))
    return jax.shard_map(shards, mesh=mesh, in_specs=in_specs, out_specs=out_specs, check_vma=False)
```

```python
import functools

import jax
import jax.numpy as jnp
from jax import lax
from jax.experimental import pallas as pl
from jax.experimental.pallas import tpu as pltpu
from jax.sharding import PartitionSpec as P

HD = 32
KSIZE = 7
PROJ = 100

floor_pt = 0.1
mass_offset = 0.1
masked_score = -1e30
LOG2E = 1.4426950408889634

DEPTH = 128
GROUPS = 2 * HD
ROW_TOP = 112
ROW_MASK = 123
PARTS = ((0, 0), (0, 1), (1, 0), (1, 1), (0, 2), (2, 0))
ONCE = (0, 2, 5)

GRAIN = 16
PROBE = 64
LIMIT = 2.0**100


def split3(x):
    high = x.astype(jnp.bfloat16).astype(jnp.float32)
    rest = x - high
    mid = rest.astype(jnp.bfloat16).astype(jnp.float32)
    low = (rest - mid).astype(jnp.bfloat16).astype(jnp.float32)
    return high, mid, low


def kinematics(a0, along_x, along_y, along_z):
    softplus = jnp.maximum(a0, 0.0) + jnp.log1p(jnp.exp(-jnp.abs(a0)))
    hit_mass = mass_offset + softplus
    mass_sq = hit_mass * hit_mass
    trans_sq = along_x * along_x + along_y * along_y
    energy = jnp.sqrt(mass_sq + trans_sq + along_z * along_z)
    trans_mass = jnp.sqrt(mass_sq + trans_sq)
    magnitude = jnp.log((jnp.abs(along_z) + energy) / trans_mass)
    rapidity = jnp.where(along_z < 0.0, -magnitude, magnitude)
    inverse_pt = 1.0 / jnp.maximum(jnp.sqrt(trans_sq), floor_pt)
    return energy, mass_sq, rapidity, along_x * inverse_pt, along_y * inverse_pt, trans_sq


def ones_row(width):
    at_row = lax.broadcasted_iota(jnp.int32, (16, width), 0)
    return jnp.where(at_row == 0, 1.0, 0.0).astype(jnp.bfloat16)


def ts_pick():
    at_row = lax.broadcasted_iota(jnp.int32, (DEPTH, 128), 0)
    pick = at_row == GROUPS + 6
    for number in ONCE[1:]:
        pick = pick | (at_row == GROUPS + 8 * number + 6)
    return jnp.where(pick, 1.0, 0.0).astype(jnp.bfloat16)


def vector_of(block):
    raw = block[3 * HD : 3 * HD + 4]
    return [raw[i : i + 1] for i in range(4)]


def quantities(block):
    vector = vector_of(block)
    energy, mass_sq, rapidity, unit_x, unit_y, trans_sq = kinematics(*vector)
    none = jnp.zeros_like(energy)
    stacked = [energy, rapidity, unit_x, unit_y, mass_sq, rapidity * rapidity, trans_sq, none]
    return split3(jnp.concatenate(stacked, axis=0)), vector[1:], trans_sq


def build_queries(block, q_s, q_m, q_d, q_ts):
    rows = block.shape[1]
    parts, momentum, trans_sq = quantities(block)
    q_ts[...] = jnp.broadcast_to(trans_sq, (8, rows))
    scaled = block[0:HD] * (LOG2E * HD**-0.5)
    high = scaled.astype(jnp.bfloat16).astype(jnp.float32)
    at_row = lax.broadcasted_iota(jnp.int32, (8, rows), 0)
    zero = jnp.zeros((8, rows), jnp.float32)
    for_m, for_d = [zero] * (GROUPS // 8), [zero] * (GROUPS // 8)
    for number, (_, b) in enumerate(PARTS):
        once = 1.0 if number in ONCE else 0.0
        for_m.append(jnp.where(at_row == 0, 2.0 * parts[b], jnp.where(at_row == 4, once, 0.0)))
        twice = jnp.where((at_row >= 1) & (at_row <= 3), -2.0 * parts[b], 0.0)
        for_d.append(jnp.where(at_row == 5, once, twice))
    none = jnp.zeros((1, rows), jnp.float32)
    for_m.append(jnp.concatenate([part[4:5] for part in parts] + [none] * 5, axis=0))
    squares = [part[5:6] for part in parts]
    for_d.append(jnp.concatenate([none] * 3 + squares + [none + 2.0, none], axis=0))
    for_m.append(jnp.concatenate([-2.0 * value for value in momentum] + [none] * 5, axis=0))
    for_d.append(zero)
    for_s = [high, scaled - high] + [zero] * 7 + [jnp.where(at_row == ROW_MASK % 8, 1.0, 0.0)]
    for ref, groups in ((q_s, for_s), (q_m, for_m), (q_d, for_d)):
        ref[...] = jnp.concatenate(groups, axis=0).astype(jnp.bfloat16)


def build_keys(block, mask):
    width = block.shape[1]
    parts, momentum, _ = quantities(block)
    key = block[HD : 2 * HD]
    one = jnp.ones((8, width), jnp.float32)
    none = jnp.zeros((4, width), jnp.float32)
    groups = [key, key] + [parts[a] for a, _ in PARTS]
    groups += [one, jnp.concatenate([*momentum, mask, none], axis=0)]
    return jnp.transpose(jnp.concatenate(groups, axis=0).astype(jnp.bfloat16))


def no_keys(count):
    lane = lax.broadcasted_iota(jnp.int32, (count, DEPTH), 1)
    empty = jnp.where(lane == ROW_MASK, masked_score, jnp.where(lane == GROUPS + 4, 1.0, 0.0))
    return empty.astype(jnp.bfloat16)


def products(keys, queries, at, count, cols):
    lhs = keys[pl.ds(at, count), :]
    return [
        jnp.dot(lhs, q[:, cols], preferred_element_type=jnp.float32)
        for q in (queries[2], queries[1], queries[0])
    ]


def combine(key_ts, queries, w, three, at, count, cols):
    separation, invariant, score = three
    ts_key = jnp.concatenate([key_ts[pl.ds(at, count), :]] * (score.shape[1] // 128), axis=1)
    ts_query = jnp.concatenate([queries[3][:, cols]] * (count // 8), axis=0)
    kt_sq = jnp.minimum(ts_key, ts_query) * separation
    score = score + w[0] * lax.log2(invariant)
    return score + w[1] * lax.log2(1.0 + kt_sq) + w[2] * lax.log2(1.0 + separation)


def probe(keys, key_ts, queries, w, best, start, count, piece):
    rows = best.shape[1]

    def one(index, carry):
        at = pl.multiple_of(start + index * PROBE, PROBE)
        for lo in range(0, rows, piece):
            cols = pl.ds(lo, piece)
            three = products(keys, queries, at, PROBE, cols)
            score = combine(key_ts, queries, w, three, at, PROBE, cols)
            top = jnp.max(score.reshape(PROBE // 8, 8, piece), axis=0)
            best[:, cols] = jnp.maximum(best[:, cols], top)
        return carry

    lax.fori_loop(0, count, one, 0)
    best[...] = jnp.broadcast_to(jnp.max(best[...], axis=0, keepdims=True), best.shape)


def set_reference(best, q_s):
    rows = best.shape[1]
    none = jnp.zeros((1, rows), jnp.float32)
    block = [*split3(-best[0:1, :]), *[none] * 5, *[none] * 3, none + 1.0, *[none] * 4]
    q_s[ROW_TOP:, :] = jnp.concatenate(block, axis=0).astype(jnp.bfloat16)


def fill(keys, queries, held, at, lo, chunk, piece):
    cols = pl.ds(lo, piece)
    for ref, value in zip(held, products(keys, queries, at, chunk, cols)):
        ref[:, cols] = value


def fill_all(keys, queries, held, at, chunk, piece):
    for lo in range(0, held[0].shape[1], piece):
        fill(keys, queries, held, at, lo, chunk, piece)


def visit(
    keys, key_ts, values, every_head, here, w, total, summed, wlow, held,
    start, chunks, next_start, next_here, chunk, piece, tail=None,
):
    rows = total.shape[1]
    queries = [ref.at[here] for ref in every_head]

    def collect(at, lo):
        cols = pl.ds(lo, piece)
        both = jnp.dot(values[:, pl.ds(at, chunk)], wlow[:, cols], preferred_element_type=jnp.float32)
        summed[:, cols] += both[:HD]
        total[:, cols] += both[HD : HD + 8]

    def one_chunk(index, carry):
        at = pl.multiple_of(start + index * chunk, chunk)
        waiting = (pl.multiple_of(start + jnp.maximum(index - 1, 0) * chunk, chunk), rows - piece)
        is_last = index == chunks - 1
        if tail is not None:
            is_last = is_last & jnp.logical_not(tail)
        following = pl.multiple_of(jnp.where(is_last, next_start, at + chunk), chunk)
        next_queries = [ref.at[jnp.where(is_last, next_here, here)] for ref in every_head]
        for lo in range(0, rows, piece):
            cols = pl.ds(lo, piece)
            score = combine(key_ts, queries, w, [ref[:, cols] for ref in held], at, chunk, cols)
            wlow[:, cols] = jnp.exp2(score).astype(jnp.bfloat16)
            fill(keys, next_queries, held, following, lo, chunk, piece)
            collect(*waiting)
            waiting = (at, lo)
        return carry

    wlow[:, rows - piece :] = jnp.zeros((chunk, piece), jnp.bfloat16)
    lax.fori_loop(0, chunks, one_chunk, 0)
    collect(pl.multiple_of(start + jnp.maximum(chunks - 1, 0) * chunk, chunk), rows - piece)
    if tail is None:
        return

    @pl.when(tail)
    def _():
        few = chunk // 2
        at = pl.multiple_of(start + chunks * chunk, chunk)
        next_queries = [ref.at[next_here] for ref in every_head]
        for lo in range(0, rows, piece):
            cols = pl.ds(lo, piece)
            some = [ref[0:few, cols] for ref in held]
            weights = jnp.exp2(combine(key_ts, queries, w, some, at, few, cols)).astype(jnp.bfloat16)
            fill(keys, next_queries, held, pl.multiple_of(next_start, chunk), lo, chunk, piece)
            both = jnp.dot(values[:, pl.ds(at, few)], weights, preferred_element_type=jnp.float32)
            summed[:, cols] += both[:HD]
            total[:, cols] += both[HD : HD + 8]


MESH = pl.DeviceIdType.MESH
DISTANCES = (-1, 1, -2)
EDGE = 128


def begin_kernel(
    nblocks, chips, chunk, piece,
    feats_at, order_at, taps_at, weight_at, pairw_at, count,
    kept, counts, best, total, summed,
    feats, order, taps, weight, pairw, in_sem, out_sem, tally, wide, halo, gathered, project,
    halo_send, halo_recv, z_send, z_recv, n_send, n_recv, x_send, x_recv, c_send, c_recv,
    keys, key_ts, values, q_s, q_m, q_d, q_ts, wlow, *held,
):
    group, block, head = [lax.axis_index(name) for name in ("groups", "seq", "head")]
    chip, core = head // 2, head % 2
    channels, rows = feats.shape
    loads = [
        pltpu.make_async_copy(order_at, order.at[0], in_sem.at[0]),
        pltpu.make_async_copy(feats_at, feats, in_sem.at[1]),
        pltpu.make_async_copy(taps_at, taps, in_sem.at[2]),
        pltpu.make_async_copy(weight_at, weight, in_sem.at[3]),
        pltpu.make_async_copy(pairw_at, pairw, in_sem.at[4]),
    ]
    for load in loads:
        load.start()
    partner = chip * 2 + 1 - core

    def at_block(distance):
        return (group, lax.rem(block + distance + nblocks, nblocks), head)

    def at_head(where):
        return (group, block, where)

    def other(offset):
        return lax.rem(chip + offset, chips) * 2 + core

    halo[0] = jnp.zeros((channels, EDGE), jnp.bfloat16)
    halo[1] = jnp.zeros((channels, EDGE), jnp.bfloat16)
    barrier = pltpu.get_barrier_semaphore()
    steps = sorted({d % nblocks for d in (1, -1, 2, -2)} - {0})
    peers = [(group, lax.rem(block + d, nblocks), head) for d in steps]
    peers += [at_head(other(e)) for e in range(1, chips)] + [at_head(partner)]
    for peer in peers:
        pl.semaphore_signal(barrier, inc=1, device_id=peer, device_id_type=MESH)

    tally[...] = jnp.full((8, 128), count[0].astype(jnp.float32), jnp.float32)
    for load in loads[:2]:
        load.wait()

    def reorder(lo, width):
        position = lax.broadcasted_iota(jnp.int32, (rows, width), 0)
        chosen = jnp.where(position == order[:, lo : lo + width], 1.0, 0.0).astype(jnp.bfloat16)
        some = jnp.dot(feats[...], chosen, preferred_element_type=jnp.float32)
        wide[:, EDGE + lo : EDGE + lo + width] = some.astype(jnp.bfloat16)

    for lo in range(0, rows, 256):
        reorder(lo, 256)
    def smooth(padded):
        half, width = KSIZE // 2, padded.shape[1]
        conv = jnp.zeros((channels, width - 2 * EDGE), jnp.float32)
        for offset in range(KSIZE):
            moved = pltpu.roll(padded, (half - offset) % width, 1)
            conv = conv + tap[:channels, offset : offset + 1] * moved[:, EDGE : width - EDGE]
        return conv.astype(jnp.bfloat16)

    pl.semaphore_wait(barrier, len(peers))

    def remote(source, target, send, recv, device):
        return pltpu.make_async_remote_copy(
            src_ref=source, dst_ref=target, send_sem=send, recv_sem=recv,
            device_id=device, device_id_type=MESH,
        )

    to_right = remote(wide.at[:, rows : rows + EDGE], halo.at[0], halo_send.at[0], halo_recv.at[0], at_block(1))
    to_left = remote(wide.at[:, EDGE : 2 * EDGE], halo.at[1], halo_send.at[1], halo_recv.at[1], at_block(-1))
    has_right, has_left = block < nblocks - 1, block > 0

    @pl.when(has_right)
    def _():
        to_right.start()

    @pl.when(has_left)
    def _():
        to_left.start()

    for load in loads[2:]:
        load.wait()
    middle = wide[:, EDGE : EDGE + rows].astype(jnp.float32)
    tap = jnp.concatenate([taps[...].astype(jnp.float32), jnp.zeros((1, channels), jnp.float32)], axis=0)
    tap = jnp.concatenate([tap, jnp.zeros((8, 128 - channels), jnp.float32)], axis=1)
    tap = jnp.transpose(tap)
    gathered[0, head, :, EDGE : rows - EDGE] = smooth(middle)

    along = [
        remote(gathered.at[0, head], gathered.at[1, head], z_send.at[0], z_recv.at[0], at_block(-1)),
        remote(gathered.at[0, head], gathered.at[2, head], z_send.at[1], z_recv.at[1], at_block(1)),
        remote(gathered.at[1, head], gathered.at[3, head], z_send.at[2], z_recv.at[2], at_block(-1)),
    ]
    small = [
        remote(tally, counts.at[k + 1], n_send.at[k], n_recv.at[k], at_block(d))
        for k, d in enumerate(DISTANCES)
    ]
    here = pltpu.make_async_copy(tally, counts.at[0], in_sem.at[0])
    out = [pltpu.make_async_copy(gathered.at[k], kept.at[k], out_sem.at[k]) for k in range(len(along) + 1)]

    slots = len(along) + 1
    pieces = [(0, EDGE, rows - EDGE)] + [(k, 0, rows) for k in range(1, slots)]
    pieces += [(0, 0, EDGE), (0, rows - EDGE, rows)]

    def over_chips(u, e):
        k, lo, hi = pieces[u]
        mine = gathered.at[k, head, :, lo:hi]
        return remote(mine, mine, x_send.at[u, e - 1], x_recv.at[u, e - 1], at_head(other(e)))

    def to_partner(u, e):
        k, lo, hi = pieces[u]
        there = gathered.at[k, other(chips - e) if e else head, :, lo:hi]
        return remote(there, there, c_send.at[u, e], c_recv.at[u, e], at_head(partner))

    def from_partner(u, e):
        k, lo, hi = pieces[u]
        there = gathered.at[k, lax.rem(chip - e + chips, chips) * 2 + 1 - core, :, lo:hi]
        return remote(there, there, c_send.at[u, e], c_recv.at[u, e], at_head(partner))

    def from_chips(u, e):
        k, lo, hi = pieces[u]
        there = gathered.at[k, other(chips - e), :, lo:hi]
        return remote(there, there, x_send.at[u, e - 1], x_recv.at[u, e - 1], at_head(other(e)))

    def spread(u):
        for e in range(1, chips):
            over_chips(u, e).start()
        to_partner(u, 0).start()

    def pass_on(u):
        for e in range(1, chips):
            from_chips(u, e).wait_recv()
            to_partner(u, e).start()

    def arrive(u):
        for e in range(chips):
            from_partner(u, e).wait_recv()

    def complete(k):
        arrive(k)
        out[k].start()

    def next_block(k):
        if k < len(along):
            along[k].wait_recv()
            spread(k + 1)
        if k + 1 < len(along):
            along[k].wait_send()
            along[k + 1].start()

    spread(0)
    @pl.when(has_left)
    def _():
        to_right.wait_recv()

    @pl.when(has_right)
    def _():
        to_left.wait_recv()

    low = jnp.where(has_left, halo[0].astype(jnp.float32), 0.0)
    high = jnp.where(has_right, halo[1].astype(jnp.float32), 0.0)
    gathered[0, head, :, 0:EDGE] = smooth(jnp.concatenate([low, middle[:, : 2 * EDGE]], axis=1))
    gathered[0, head, :, rows - EDGE :] = smooth(jnp.concatenate([middle[:, rows - 2 * EDGE :], high], axis=1))

    @pl.when(has_right)
    def _():
        to_right.wait_send()

    @pl.when(has_left)
    def _():
        to_left.wait_send()

    for u in (slots, slots + 1):
        spread(u)
    along[0].start()
    heads = weight.shape[0] // PROJ
    for h in range(heads):
        part = weight[...].astype(jnp.float32)[h * PROJ : (h + 1) * PROJ]
        project[h, 0:PROJ, :] = part
    values[HD:, :] = ones_row(values.shape[1])
    for u in (0, slots, slots + 1):
        pass_on(u)
    next_block(0)
    for u in (slots, slots + 1):
        arrive(u)
    complete(0)
    for copy in small + [here]:
        copy.start()

    first = rows // 2
    dot = functools.partial(jnp.dot, preferred_element_type=jnp.float32)
    every_head = (q_s, q_m, q_d, q_ts)
    steps = heads * (len(along) + 1)

    def weights_of(h):
        return [pairw[h, i] for i in range(3)]

    def prepare(number):
        k, h = number // heads, lax.rem(number, heads)
        low = pl.multiple_of(lax.rem(number, 2) * first, first)
        weight_here = project[h].astype(jnp.bfloat16)
        some = gathered[k, :, :, 0:first].reshape(-1, first)
        block = dot(weight_here, some).astype(jnp.bfloat16).astype(jnp.float32)
        turned = build_keys(block, jnp.zeros((1, first), jnp.float32))
        keys[pl.ds(low, first), :] = turned
        key_ts[pl.ds(low, first), :] = dot(turned, ts_pick())
        values[0:HD, pl.ds(low, first)] = block[2 * HD : 3 * HD].astype(jnp.bfloat16)

        @pl.when(number < heads)
        def _():
            everywhere = gathered[0].reshape(-1, rows)
            block = dot(weight_here, everywhere).astype(jnp.bfloat16).astype(jnp.float32)
            queries = [ref.at[h] for ref in every_head]
            build_queries(block, *queries)
            best[h] = jnp.full((8, rows), masked_score, jnp.float32)
            probe(keys, key_ts, queries, weights_of(h), best.at[h], low, 1, piece)
            set_reference(best.at[h], q_s.at[h])
            total[h] = jnp.zeros((8, rows), jnp.float32)
            summed[h] = jnp.zeros((HD, rows), jnp.float32)

    def one_step(number, carry):
        for k in range(1, len(along) + 1):
            @pl.when(number == k * heads - 1)
            def _():
                pass_on(k)
                next_block(k)
                complete(k)

        @pl.when(number + 1 < steps)
        def _():
            prepare(number + 1)

        h, low = lax.rem(number, heads), lax.rem(number, 2) * first
        visit(
            keys, key_ts, values, every_head, h, weights_of(h), total.at[h], summed.at[h], wlow, held,
            low, first // chunk, first - low, lax.rem(number + 1, heads), chunk, piece,
        )
        return carry

    prepare(jnp.int32(0))
    fill_all(keys, [ref.at[0] for ref in every_head], held, 0, chunk, piece)
    lax.fori_loop(0, steps, one_step, 0)
    for copy in small + [here]:
        copy.wait()
    for copy in out:
        copy.wait()
    along[-1].wait_send()
    for u in range(len(pieces)):
        for e in range(chips):
            if e:
                over_chips(u, e).wait_send()
            to_partner(u, e).wait_send()


def begin(feats, order, taps, weight, pairw, count, chunk=256, piece=256):
    channels, rows = feats.shape
    nblocks, places = lax.axis_size("seq"), lax.axis_size("head")
    heads = weight.shape[0] // PROJ
    chips = places // 2
    slots = len(DISTANCES) + 1
    held = rows // 2 * 2
    anywhere = pl.BlockSpec(memory_space=pltpu.HBM)
    vmem = pl.BlockSpec(memory_space=pltpu.VMEM)
    dma = pltpu.SemaphoreType.DMA
    return pl.pallas_call(
        functools.partial(begin_kernel, nblocks, chips, chunk, piece),
        in_specs=[anywhere] * 5 + [pl.BlockSpec(memory_space=pltpu.SMEM)],
        out_specs=[anywhere, anywhere, vmem, vmem, vmem],
        out_shape=[
            jax.ShapeDtypeStruct((slots, places, channels, rows), jnp.bfloat16),
            jax.ShapeDtypeStruct((slots, 8, 128), jnp.float32),
            *[jax.ShapeDtypeStruct((heads, size, rows), jnp.float32) for size in (8, 8, HD)],
        ],
        scratch_shapes=[
            pltpu.VMEM((channels, rows), jnp.bfloat16),
            pltpu.VMEM((1, rows), jnp.int32),
            pltpu.VMEM(taps.shape, taps.dtype),
            pltpu.VMEM(weight.shape, weight.dtype),
            pltpu.SMEM(pairw.shape, pairw.dtype),
            dma((5,)),
            dma((slots,)),
            pltpu.VMEM((8, 128), jnp.float32),
            pltpu.VMEM((channels, rows + 2 * EDGE), jnp.bfloat16),
            pltpu.VMEM((2, channels, EDGE), jnp.bfloat16),
            pltpu.VMEM((slots, places, channels, rows), jnp.bfloat16),
            pltpu.VMEM((heads, PROJ + 4, weight.shape[1]), jnp.float32),
            dma((2,)), dma((2,)),
            dma((slots - 1,)), dma((slots - 1,)),
            dma((slots - 1,)), dma((slots - 1,)),
            dma((slots + 2, max(chips - 1, 1))), dma((slots + 2, max(chips - 1, 1))),
            dma((slots + 2, chips)), dma((slots + 2, chips)),
            pltpu.VMEM((held, DEPTH), jnp.bfloat16),
            pltpu.VMEM((held, 128), jnp.float32),
            pltpu.VMEM((HD + 16, held), jnp.bfloat16),
            *[pltpu.VMEM((heads, DEPTH, rows), jnp.bfloat16)] * 3,
            pltpu.VMEM((heads, 8, rows), jnp.float32),
            pltpu.VMEM((chunk, rows), jnp.bfloat16),
            *[pltpu.VMEM((chunk, rows), jnp.float32)] * 3,
        ],
        compiler_params=pltpu.CompilerParams(
            collective_id=0, has_side_effects=True, vmem_limit_bytes=58 * 1024 * 1024
        ),
        name="begin",
    )(feats, order, taps, weight, pairw, count)


def finish_kernel(
    chunk, piece, held_rows,
    counts_at, pairw_at, weight_at, gathered_at, best_at, total_at, summed_at,
    out_ref,
    counts_ref, pairw, weight, gathered, best, total, summed, old, in_sem,
    keys, key_ts, values, q_s, q_m, q_d, q_ts, wlow, *held,
):
    nb, _, rows = gathered.shape
    heads = weight.shape[0] // PROJ
    dot = functools.partial(jnp.dot, preferred_element_type=jnp.float32)
    loads = [
        pltpu.make_async_copy(source, target, in_sem.at[k])
        for k, (source, target) in enumerate([
            (counts_at, counts_ref), (pairw_at, pairw), (weight_at, weight), (best_at, best),
            (gathered_at.at[0], gathered.at[0]),
            *[(gathered_at.at[i, :, rows // 2 :], gathered.at[i, :, rows // 2 :]) for i in range(1, nb)],
            (total_at, total), (summed_at, summed),
        ])
    ]
    for load in loads:
        load.start()
    values[HD:, :] = ones_row(values.shape[1])
    for load in loads:
        load.wait()
    counts = [jnp.max(counts_ref[i]).astype(jnp.int32) for i in range(nb)]
    every_head = (q_s, q_m, q_d, q_ts)

    def project(h):
        part = weight[0:PROJ, :]
        for other in range(1, heads):
            part = jnp.where(h == other, weight[other * PROJ : (other + 1) * PROJ, :], part)
        return part

    def weights_of(h):
        return [pairw[h, i] for i in range(3)]

    def place(v, at):
        width = v.shape[1]
        shift = at % 128
        base = pl.multiple_of(at - shift, 128)
        v = pltpu.roll(jnp.concatenate([v, jnp.zeros((HD, 128), jnp.float32)], axis=1), shift, 1)
        before = values[0:HD, pl.ds(base, 128)].astype(jnp.float32)
        lane = lax.broadcasted_iota(jnp.int32, (HD, 128), 1)
        joined = jnp.where(lane < shift, before, v[:, :128])
        values[0:HD, pl.ds(base, 128)] = joined.astype(jnp.bfloat16)
        values[0:HD, pl.ds(base + 128, width)] = v[:, 128:].astype(jnp.bfloat16)

    def lay_out(h, low):
        width = rows - low
        start = h * held_rows
        part = project(h)
        lanes = lax.broadcasted_iota(jnp.int32, (1, width), 1) + low
        for i in range(nb):
            block = dot(part, gathered[i, :, low:]).astype(jnp.bfloat16).astype(jnp.float32)
            turned = build_keys(block, jnp.where(lanes < counts[i], 0.0, masked_score))
            at = pl.multiple_of(start, GRAIN)
            keys[pl.ds(at, width), :] = turned
            key_ts[pl.ds(at, width), :] = dot(turned, ts_pick())
            place(block[2 * HD : 3 * HD], at)
            start = start + (counts[i] - low + GRAIN - 1) // GRAIN * GRAIN
        at = pl.multiple_of(start, GRAIN)
        keys[pl.ds(at, chunk), :] = no_keys(chunk)
        key_ts[pl.ds(at, chunk), :] = jnp.zeros((chunk, 128), jnp.float32)
        place(jnp.zeros((HD, chunk), jnp.float32), at)

    def attempt(number, go):
        reached = jnp.int32(0)
        for i in range(nb):
            left = counts[i] - jnp.where(number == 0, rows // 2, 0)
            reached = reached + (left + GRAIN - 1) // GRAIN * GRAIN
        chunks = (reached + chunk // 2 - 1) // chunk
        tail = reached > chunks * chunk

        def prepare(h, carry):
            queries = [ref.at[h] for ref in every_head]

            @pl.when(number == 0)
            def _():
                block = dot(project(h), gathered[0]).astype(jnp.bfloat16).astype(jnp.float32)
                build_queries(block, *queries)
                lay_out(h, rows // 2)

            @pl.when(number == 1)
            def _():
                lay_out(h, 0)
                none = jnp.zeros((8, rows), jnp.float32)
                best[h] = none + masked_score
                set_reference(old, q_s.at[h])
                probes = (reached + PROBE - 1) // PROBE
                probe(keys, key_ts, queries, weights_of(h), best.at[h], h * held_rows, probes, piece)
                total[h] = none
                summed[h] = jnp.zeros((HD, rows), jnp.float32)

            set_reference(best.at[h], q_s.at[h])
            return carry

        def one_head(h, carry):
            after = lax.rem(h + 1, heads)
            visit(
                keys, key_ts, values, every_head, h, weights_of(h), total.at[h], summed.at[h], wlow, held,
                h * held_rows, chunks, after * held_rows, after, chunk, piece, tail,
            )
            return carry

        @pl.when((go == 1) & (number == 1))
        def _():
            for i in range(1, nb):
                half = gathered.at[i, :, 0 : rows // 2]
                load = pltpu.make_async_copy(gathered_at.at[i, :, 0 : rows // 2], half, in_sem.at[i])
                load.start()
                load.wait()

        @pl.when(go == 1)
        def _():
            lax.fori_loop(0, heads, prepare, 0)
            fill_all(keys, [ref.at[0] for ref in every_head], held, 0, chunk, piece)
            lax.fori_loop(0, heads, one_head, 0)

        return jnp.logical_not(jnp.max(total[...]) < LIMIT).astype(jnp.int32)

    old[...] = jnp.zeros((8, rows), jnp.float32)
    lax.fori_loop(0, 2, attempt, jnp.int32(1))
    for h in range(heads):
        out_ref[h * HD : (h + 1) * HD, :] = (summed[h] / total[h, 0:1, :]).astype(jnp.bfloat16)


def finish(counts, pairw, weight, gathered, state, chunk=256, piece=256):
    heads = weight.shape[0] // PROJ
    nb, _, rows = gathered.shape
    held = nb * rows + 2 * chunk
    pairs = heads * rows * nb * rows
    operands = [counts, pairw, weight, gathered, *state]
    scratch = [pltpu.VMEM(one.shape, one.dtype) for one in operands]
    scratch[1] = pltpu.SMEM(pairw.shape, pairw.dtype)
    return pl.pallas_call(
        functools.partial(finish_kernel, chunk, piece, held),
        in_specs=[pl.BlockSpec(memory_space=pltpu.HBM)] * len(operands),
        out_specs=pl.BlockSpec(memory_space=pltpu.VMEM),
        out_shape=jax.ShapeDtypeStruct((heads * HD, rows), jnp.bfloat16),
        scratch_shapes=[
            *scratch,
            pltpu.VMEM((8, rows), jnp.float32),
            pltpu.SemaphoreType.DMA((len(operands) - 1 + nb,)),
            pltpu.VMEM((heads * held, DEPTH), jnp.bfloat16),
            pltpu.VMEM((heads * held, 128), jnp.float32),
            pltpu.VMEM((HD + 16, heads * held), jnp.bfloat16),
            *[pltpu.VMEM((heads, DEPTH, rows), jnp.bfloat16)] * 3,
            pltpu.VMEM((heads, 8, rows), jnp.float32),
            pltpu.VMEM((chunk, rows), jnp.bfloat16),
            *[pltpu.VMEM((chunk, rows), jnp.float32)] * 3,
        ],
        compiler_params=pltpu.CompilerParams(vmem_limit_bytes=58 * 1024 * 1024),
        cost_estimate=pl.CostEstimate(
            flops=pairs * 2 * DEPTH * 4, bytes_accessed=1 << 20, transcendentals=4 * pairs
        ),
        name="finish",
    )(*operands)


def shards(hit_features, depth_kernel, point_weight, pair_weight, hit_order, valid_counts):
    rows = hit_features.shape[1]
    gathered, counts, *state = begin(
        hit_features, hit_order, depth_kernel, point_weight, pair_weight, valid_counts
    )
    gathered = gathered.reshape(gathered.shape[0], point_weight.shape[1], rows)
    return finish(counts, pair_weight, point_weight, gathered, state)


def solution(mesh):
    in_specs = (
        P("head", ("groups", "seq")),
        P(None, "head"),
        P("head", None),
        P("head", None),
        P(("groups", "seq")),
        P(("groups", "seq")),
    )
    out_specs = P("head", ("groups", "seq"))
    return jax.shard_map(shards, mesh=mesh, in_specs=in_specs, out_specs=out_specs, check_vma=False)
```
